32 devices in a mesh: dp: 8 (over z, x), mp: 4 (over y, core).
Axes of the slice: x: 2, y: 2, z: 4, core: 2. Of those that a mesh axis runs over, the one named last changes fastest.
Arguments:
- inputs: bfloat16 [16384, 768], P('dp'), may hold values from -6 to 6
- segments: int32 [256, 64], P('dp'), may hold values from 0 to 5, never falling along the last dimension, each value on 1 to 24 neighbouring positions
- cotangent: bfloat16 [16384, 768], P('dp'), may hold values from -12 to 12
- triple_weight: float32 [3, 768, 768], P(None, 'dp', 'mp'), may hold values from -0.21875 to 0.21875
- triple_first: float32 [3, 768, 768], P(None, 'dp', 'mp')
- triple_second: float32 [3, 768, 768], P(None, 'dp', 'mp'), as said below
- outward_weight: float32 [768, 768], P('mp', 'dp'), may hold values from -0.625 to 0.625
- outward_first: float32 [768, 768], P('mp', 'dp')
- outward_second: float32 [768, 768], P('mp', 'dp'), as said below
- expand_weight: float32 [768, 3072], P('dp', 'mp'), may hold values from -2 to 2
- expand_first: float32 [768, 3072], P('dp', 'mp')
- expand_second: float32 [768, 3072], P('dp', 'mp'), as said below
- reduce_weight: float32 [3072, 768], P('mp', 'dp'), may hold values from -0.109375 to 0.109375
- reduce_first: float32 [3072, 768], P('mp', 'dp')
- reduce_second: float32 [3072, 768], P('mp', 'dp'), as said below
- norm_params: float32 [6, 768], replicated, may hold values from -3 to 4
- norm_first: float32 [6, 768], replicated
- norm_second: float32 [6, 768], replicated, as said below
- paired_bias: float32 [2, 768], P(None, 'mp'), may hold values from -1.8 to 1.8
- paired_first: float32 [2, 768], P(None, 'mp')
- paired_second: float32 [2, 768], P(None, 'mp'), as said below
- hidden_bias: float32 [3072], P('mp'), may hold values from -1.8 to 1.8
- hidden_first: float32 [3072], P('mp')
- hidden_second: float32 [3072], P('mp'), as said below
Outputs:
- outputs: bfloat16 [16384, 768], P('dp')
- input_gradient: bfloat16 [16384, 768], P('dp')
- gradient_norm: float32 [], replicated
- triple_moment: float32 [3, 768, 768], P(None, 'dp', 'mp')
- triple_square: float32 [3, 768, 768], P(None, 'dp', 'mp')
- triple_updated: float32 [3, 768, 768], P(None, 'dp', 'mp')
- outward_moment: float32 [768, 768], P('mp', 'dp')
- outward_square: float32 [768, 768], P('mp', 'dp')
- outward_updated: float32 [768, 768], P('mp', 'dp')
- expand_moment: float32 [768, 3072], P('dp', 'mp')
- expand_square: float32 [768, 3072], P('dp', 'mp')
- expand_updated: float32 [768, 3072], P('dp', 'mp')
- reduce_moment: float32 [3072, 768], P('mp', 'dp')
- reduce_square: float32 [3072, 768], P('mp', 'dp')
- reduce_updated: float32 [3072, 768], P('mp', 'dp')
- norm_moment: float32 [6, 768], replicated
- norm_square: float32 [6, 768], replicated
- norm_updated: float32 [6, 768], replicated
- paired_moment: float32 [2, 768], P(None, 'mp')
- paired_square: float32 [2, 768], P(None, 'mp')
- paired_updated: float32 [2, 768], P(None, 'mp')
- hidden_moment: float32 [3072], P('mp')
- hidden_square: float32 [3072], P('mp')
- hidden_updated: float32 [3072], P('mp')
The draws below stay inside these ranges and needn't reach their ends.
Inputs may be any that keep to these rules, and one draw needn't show every extreme that they name: `segments`: within each row of 64 tokens the numbers never fall; each of the 6 captions holds 1 to 24 tokens, one exactly 24. `triple_second`: positive. `outward_second`: positive. `expand_second`: positive. `reduce_second`: positive. `norm_second`: positive. `paired_second`: positive. `hidden_second`: positive.
All inputs are finite; a program needn't handle non-finite values.
Results may differ from the reference program's by a relative error of at most 0.02.
Values may be sent and summed in bfloat16 or wider, within the bound.
No kernel may reach another device: no remote copies, remote signals or barrier semaphores. Data moves between devices by JAX's collectives and lax.ppermute only.
A program may use at most 128 MiB of HBM per device.

```python
import math
import jax
import jax.numpy as jnp
import numpy as np
from jax import lax

D = 768
HEADS = 12
HD = 64
FF = 3072
SEQ = 64
SEGS = 6
MOST = 24
STEP = 5
ROWS = 256
TOKENS = 16384
HH = 768
N_MP = 4


def rising(count, start_value, end_value):
    place = jnp.arange(count, dtype=jnp.float32) / max(count - 1, 1)
    return start_value * (end_value / start_value) ** place


def overall_level():
    return (D * (3.13 * HEADS * HD + 0.51 * FF)) ** 0.5


def first_moment(key, shape, factor):
    level = factor / overall_level()
    return level * jax.random.truncated_normal(key, -6.0, 6.0, shape, jnp.float32)


def second_moment(key, shape, factor):
    level = factor / overall_level()
    spread = jnp.exp(jax.random.uniform(key, shape, jnp.float32, 0.0, math.log(4.0)))
    return level * level * spread


def draw_cotangent(key, part):
    first_key = jax.random.fold_in(key, 0)
    base = jax.random.truncated_normal(first_key, -6.0, 6.0, (TOKENS, D), jnp.float32)
    return (base * rising(D, 0.6, 1.8)).astype(jnp.bfloat16)


def draw_norm_params(key, part):
    first_key, second_key = jax.random.split(key)
    gains = rising(D, 0.6, 1.8) * jax.random.uniform(first_key, (6, D), jnp.float32, 0.7, 1.4)
    shifts = 0.3 * jax.random.truncated_normal(second_key, -6.0, 6.0, (6, D), jnp.float32)
    which = jnp.array([1.0, 0.0, 1.0, 0.0, 0.0, 0.0], jnp.float32)[:, None]
    return which * gains + (1.0 - which) * shifts


def draw_expand_weight(key, part):
    base = jax.random.truncated_normal(key, -6.0, 6.0, (D, FF), jnp.float32)
    return base * D ** (-0.5) * rising(FF, 0.6, 1.8)


def draw_triple_first(key, part):
    return first_moment(key, (3, D, HEADS * HD), 1.0)


def draw_triple_second(key, part):
    return second_moment(key, (3, D, HEADS * HD), 1.0)


def draw_outward_first(key, part):
    return first_moment(key, (HEADS * HD, D), 0.36)


def draw_outward_second(key, part):
    return second_moment(key, (HEADS * HD, D), 0.36)


def draw_expand_first(key, part):
    return first_moment(key, (D, FF), 0.3)


def draw_expand_second(key, part):
    return second_moment(key, (D, FF), 0.3)


def draw_reduce_first(key, part):
    return first_moment(key, (FF, D), 0.65)


def draw_reduce_second(key, part):
    return second_moment(key, (FF, D), 0.65)


def draw_norm_first(key, part):
    return first_moment(key, (6, D), 1.2)


def draw_norm_second(key, part):
    return second_moment(key, (6, D), 1.2)


def draw_paired_first(key, part):
    return first_moment(key, (2, HEADS * HD), 1.0)


def draw_paired_second(key, part):
    return second_moment(key, (2, HEADS * HD), 1.0)


def draw_hidden_first(key, part):
    return first_moment(key, (FF,), 0.3)


def draw_hidden_second(key, part):
    return second_moment(key, (FF,), 0.3)


def level_of(own_key, extent, cuts, least, largest):
    level = 1.0
    for axis_at, shards_of in cuts:
        draws = jax.random.uniform(jax.random.fold_in(jax.random.fold_in(own_key, 6), axis_at), (shards_of,), jnp.float32, least / len(cuts), largest / len(cuts))
        level = level * jnp.repeat(jnp.exp(draws), extent[axis_at] // shards_of).reshape((-1,) + (1,) * (len(extent) - 1 - axis_at))
    return level


def profile(number_of, total, most, lean):
    weights = [(1 << 20) // math.isqrt(rank ** lean) + 1 for rank in range(2, number_of + 1)]
    spare, holding = total - most - (number_of - 1), [1] * (number_of - 1)
    while spare > 0:
        candidates = [i for i in range(number_of - 1) if holding[i] < most]
        whole, left = sum([weights[i] for i in candidates]), spare
        for i in candidates:
            more = min(most - holding[i], max(1, left * weights[i] // whole), spare)
            holding[i] = holding[i] + more
            spare = spare - more
    return np.array([most] + holding)


def uneven(stream_key, count, total, limit, lean):
    if count == 2:
        one = jax.random.randint(stream_key, (), max(1, total - limit), min(limit, total - 1) + 1)
        return jnp.stack([one, total - one])
    lengths = jnp.asarray(profile(count, total, limit, lean), jnp.int32)
    twos = (count - 1) // 2
    giver, taker = lengths[1:1 + 2 * twos:2], lengths[2:2 + 2 * twos:2]
    margin = jnp.minimum(giver - 1, limit - taker)
    passed = jax.random.randint(jax.random.fold_in(stream_key, 1), (twos,), 0, 1 << 20) % (margin + 1)
    lengths = lengths.at[1:1 + 2 * twos:2].set(giver - passed).at[2:2 + 2 * twos:2].set(taker + passed)
    return lengths[jax.random.permutation(jax.random.fold_in(stream_key, 2), count)]


def bell_draw(key, extent, width, most, cuts=(), kind=jnp.bfloat16):
    values = jax.random.normal(key, extent, jnp.float32) * width
    if len(cuts) > 0:
        values = level_of(key, extent, cuts, -0.22, 0.18) * values
    return jnp.clip(values, min=-most, max=most).astype(kind)


def setup_inputs(seed: int = 0) -> dict:
    keys = jax.random.split(jax.random.key(seed), 25)
    return {
        "inputs": bell_draw(keys[0], (TOKENS, D), 1.0, 6.0, ((0, 8),)),
        "segments": jax.vmap(lambda own: jnp.searchsorted(jnp.cumsum(uneven(own, SEGS, SEQ, MOST, 0)), jnp.arange(SEQ), side="right"))(jax.random.split(keys[1], ROWS)).reshape((ROWS, SEQ)).astype(jnp.int32),
        "cotangent": draw_cotangent(jax.random.fold_in(keys[24], 71), 0),
        "triple_weight": bell_draw(keys[3], (3, D, HH), D ** -0.5, 0.21875, ((1, 8), (2, 4)), jnp.float32),
        "triple_first": draw_triple_first(jax.random.fold_in(keys[24], 71), 0),
        "triple_second": draw_triple_second(jax.random.fold_in(keys[24], 71), 0),
        "outward_weight": bell_draw(keys[6], (HH, D), (HH // 8) ** -0.5, 0.625, ((0, 4), (1, 8)), jnp.float32),
        "outward_first": draw_outward_first(jax.random.fold_in(keys[24], 71), 0),
        "outward_second": draw_outward_second(jax.random.fold_in(keys[24], 71), 0),
        "expand_weight": draw_expand_weight(jax.random.fold_in(keys[24], 71), 0),
        "expand_first": draw_expand_first(jax.random.fold_in(keys[24], 71), 0),
        "expand_second": draw_expand_second(jax.random.fold_in(keys[24], 71), 0),
        "reduce_weight": bell_draw(keys[12], (FF, D), FF ** -0.5, 0.109375, ((0, 4), (1, 8)), jnp.float32),
        "reduce_first": draw_reduce_first(jax.random.fold_in(keys[24], 71), 0),
        "reduce_second": draw_reduce_second(jax.random.fold_in(keys[24], 71), 0),
        "norm_params": draw_norm_params(jax.random.fold_in(keys[24], 71), 0),
        "norm_first": draw_norm_first(jax.random.fold_in(keys[24], 71), 0),
        "norm_second": draw_norm_second(jax.random.fold_in(keys[24], 71), 0),
        "paired_bias": bell_draw(keys[18], (2, HH), 0.3, 1.8, ((1, 4),), jnp.float32),
        "paired_first": draw_paired_first(jax.random.fold_in(keys[24], 71), 0),
        "paired_second": draw_paired_second(jax.random.fold_in(keys[24], 71), 0),
        "hidden_bias": bell_draw(keys[21], (FF,), 0.3, 1.8, ((0, 4),), jnp.float32),
        "hidden_first": draw_hidden_first(jax.random.fold_in(keys[24], 71), 0),
        "hidden_second": draw_hidden_second(jax.random.fold_in(keys[24], 71), 0),
    }


@jax.custom_vjp
def low(v):
    return lax.optimization_barrier(v.astype(jnp.bfloat16)).astype(jnp.float32)

@jax.custom_vjp
def low_back(v):
    return v

def low_keep(v):
    return (low(v), None)

def low_pass(kept, grad):
    return (grad,)

def back_keep(v):
    return (v, None)

def back_low(kept, grad):
    return (low(grad),)
low.defvjp(low_keep, low_pass)
low_back.defvjp(back_keep, back_low)
EPS_NORM = 1e-06
BETA = 0.5
LR_MATRIX = 0.03
LR_VECTOR = 0.2
DECAY = 0.1
ADAM_EPS = 1e-08
CLIP = 1.0
NEG = -1e+30
HIGHEST = lax.Precision.HIGHEST

def layer_norm(rows_in, gain_row, shift_row):
    row_mean = lax.optimization_barrier(jnp.mean(rows_in, axis=-1, keepdims=True))
    centred = rows_in - row_mean
    variance = lax.optimization_barrier(jnp.mean(centred * centred, axis=-1, keepdims=True))
    return centred * lax.rsqrt(variance + EPS_NORM) * gain_row + shift_row

def matmul(left, right):
    return jnp.dot(left, right, precision=HIGHEST, preferred_element_type=jnp.float32)

def block_forward(params, flat_rows, seg_block):
    triple, outward, expand, reduce_mat, norm_rows, pair_bias, unit_bias = params
    block_rows = seg_block.shape[0]
    token_count = flat_rows.shape[0]
    heads_dev = HEADS // N_MP
    head_width = heads_dev * HD
    hidden_width = FF // N_MP
    scale_factor = HD ** (-0.5)
    same_caption = (seg_block[:, :, None] == seg_block[:, None, :])[:, None, :, :]
    first_low = low(layer_norm(flat_rows, norm_rows[0], norm_rows[1]))
    attended = jnp.zeros((token_count, D), jnp.float32)
    for group in range(N_MP):
        start = group * head_width
        stop = start + head_width
        shared = low_back(first_low)
        queries = low_back(low(matmul(shared, triple[0][:, start:stop]) + pair_bias[0][start:stop]))
        key_rows = low_back(low(matmul(shared, triple[1][:, start:stop])))
        value_rows = low_back(low(matmul(shared, triple[2][:, start:stop]) + pair_bias[1][start:stop]))
        queries = queries.reshape(block_rows, SEQ, heads_dev, HD)
        key_rows = key_rows.reshape(block_rows, SEQ, heads_dev, HD)
        value_rows = value_rows.reshape(block_rows, SEQ, heads_dev, HD)
        raw_scores = low_back(jnp.einsum('rqhd,rkhd->rhqk', queries, key_rows, precision=HIGHEST))
        scores = jnp.where(same_caption, raw_scores * scale_factor, NEG)
        probs = low(jax.nn.softmax(scores, axis=-1))
        context = jnp.einsum('rhqk,rkhd->rqhd', probs, value_rows, precision=HIGHEST)
        context = low_back(low(context)).reshape(token_count, head_width)
        attended = attended + low(matmul(context, outward[start:stop]))
    middle = flat_rows + low_back(attended) + norm_rows[4]
    second_low = low(layer_norm(middle, norm_rows[2], norm_rows[3]))
    fed = jnp.zeros((token_count, D), jnp.float32)
    for group in range(N_MP):
        start = group * hidden_width
        stop = start + hidden_width
        shared = low_back(second_low)
        hidden_pre = low_back(matmul(shared, expand[:, start:stop]) + unit_bias[start:stop])
        activated = low(jax.nn.gelu(hidden_pre, approximate=True))
        fed = fed + low(matmul(activated, reduce_mat[start:stop]))
    return middle + low_back(fed) + norm_rows[5]

def forward(params, input_rows, segments):
    triple, outward, expand, reduce_mat, norm_rows, pair_bias, unit_bias = params
    lowered = (low(triple), low(outward), low(expand), low(reduce_mat), norm_rows, pair_bias, unit_bias)
    block_rows = math.gcd(ROWS, max(1, 4096 // SEQ))
    blocks = input_rows.reshape(ROWS // block_rows, block_rows * SEQ, D)
    seg_blocks = segments.reshape(ROWS // block_rows, block_rows, SEQ)
    runner = jax.checkpoint(block_forward)

    def advance(carry, item):
        return (carry, runner(lowered, item[0], item[1]))
    unused, results = lax.scan(advance, jnp.zeros((), jnp.float32), (blocks, seg_blocks))
    return results.reshape(TOKENS, D)

def adam_step(weight, first, second, grad, factor, rate, decay):
    clipped = grad * factor
    first_new = BETA * first + (1.0 - BETA) * clipped
    second_new = BETA * second + (1.0 - BETA) * clipped * clipped
    correction = 1.0 - BETA ** STEP
    direction = first_new / correction / (jnp.sqrt(second_new / correction) + ADAM_EPS)
    return (first_new, second_new, weight - rate * (direction + decay * weight))

def reference(inputs, segments, cotangent, triple_weight, triple_first, triple_second, outward_weight, outward_first, outward_second, expand_weight, expand_first, expand_second, reduce_weight, reduce_first, reduce_second, norm_params, norm_first, norm_second, paired_bias, paired_first, paired_second, hidden_bias, hidden_first, hidden_second):
    params = (triple_weight, outward_weight, expand_weight, reduce_weight, norm_params, paired_bias, hidden_bias)
    firsts = (triple_first, outward_first, expand_first, reduce_first, norm_first, paired_first, hidden_first)
    seconds = (triple_second, outward_second, expand_second, reduce_second, norm_second, paired_second, hidden_second)

    def whole_layer(param_set, input_rows):
        return forward(param_set, input_rows, segments)
    result, pullback = jax.vjp(whole_layer, params, inputs.astype(jnp.float32))
    grads, input_grad = pullback(cotangent.astype(jnp.float32))
    total_square = jnp.zeros((), jnp.float32)
    for grad_item in grads:
        total_square = total_square + jnp.sum(grad_item * grad_item)
    gradient_norm = jnp.sqrt(total_square)
    factor = jnp.minimum(1.0, CLIP / gradient_norm)
    rates = (LR_MATRIX, LR_MATRIX, LR_MATRIX, LR_MATRIX, LR_VECTOR, LR_VECTOR, LR_VECTOR)
    decays = (DECAY, DECAY, DECAY, DECAY, 0.0, 0.0, 0.0)
    updated = []
    for index in range(7):
        updated.extend(adam_step(params[index], firsts[index], seconds[index], grads[index], factor, rates[index], decays[index]))
    return (result.astype(jnp.bfloat16), input_grad.astype(jnp.bfloat16), gradient_norm, updated[0], updated[1], updated[2], updated[3], updated[4], updated[5], updated[6], updated[7], updated[8], updated[9], updated[10], updated[11], updated[12], updated[13], updated[14], updated[15], updated[16], updated[17], updated[18], updated[19], updated[20])
```

```python
import functools

import jax
import jax.numpy as jnp
from jax import lax
from jax.experimental import pallas as pl
from jax.experimental.pallas import tpu as pltpu
from jax.sharding import PartitionSpec as P

HD = 64
STEP = 5
EPS_NORM = 1e-06
BETA = 0.5
LR_MATRIX = 0.03
LR_VECTOR = 0.2
DECAY = 0.1
ADAM_EPS = 1e-08
CLIP = 1.0
NEG = -1e30
GELU_C = 0.7978845608028654
GELU_K = 0.044715

f32 = jnp.float32
bf16 = jnp.bfloat16
AXES = ("dp", "mp")
LANES = 128
CHUNK = 256
MIB = 1 << 20


def mm(left, right):
    return lax.dot_general(left, right, (((1,), (0,)), ((), ())), preferred_element_type=f32)


def mm_nt(left, right):
    return lax.dot_general(left, right, (((1,), (1,)), ((), ())), preferred_element_type=f32)


def mm_tn(left, right):
    return lax.dot_general(left, right, (((0,), (0,)), ((), ())), preferred_element_type=f32)


def norm_stats(rows_in):
    centred = rows_in - jnp.mean(rows_in, axis=-1, keepdims=True)
    scaled = lax.rsqrt(jnp.mean(centred * centred, axis=-1, keepdims=True) + EPS_NORM)
    return centred * scaled, scaled


def norm_backward(upstream, normal_rows, scaled, gain_row):
    gained = upstream * gain_row
    mean_one = jnp.mean(gained, axis=-1, keepdims=True)
    mean_two = jnp.mean(gained * normal_rows, axis=-1, keepdims=True)
    return scaled * (gained - mean_one - normal_rows * mean_two)


def lane_low(shape):
    return lax.broadcasted_iota(jnp.int32, shape, 1) % LANES < HD


def split_heads(block):
    low = lane_low(block.shape)
    zero = jnp.zeros_like(block)
    return jnp.concatenate([jnp.where(low, block, zero), jnp.where(low, zero, block)], axis=0)


def join_heads(stacked):
    half = stacked.shape[0] // 2
    low = lane_low((half, stacked.shape[1]))
    return jnp.where(low, stacked[:half], stacked[half:])


class Plan:
    def __init__(self, ndp, nmp, width, hidden):
        assert ndp % 2 == 0 and nmp == 4
        self.ndev = ndp * nmp
        self.nz = ndp // 2
        self.rows = width // ndp
        self.half = self.rows // 2
        self.width = width
        self.cols = width // 2
        self.part = hidden // nmp
        self.direct = self.half % 16 == 0

    def perm(self, move):
        pairs = []
        for z in range(self.nz):
            for x in range(2):
                for y in range(2):
                    for c in range(2):
                        there = move(z, x, y, c)
                        pairs.append((self.index(z, x, y, c), self.index(*there)))
        return pairs

    def index(self, z, x, y, c):
        return (2 * z + x) * 4 + 2 * y + c

    def core(self, value):
        return lax.ppermute(value, AXES, self.perm(lambda z, x, y, c: (z, x, y, 1 - c)))

    def along_x(self, value):
        return lax.ppermute(value, AXES, self.perm(lambda z, x, y, c: (z, 1 - x, y, c)))

    def along_y(self, value):
        return lax.ppermute(value, AXES, self.perm(lambda z, x, y, c: (z, x, 1 - y, c)))

    def along_z(self, value, step):
        return lax.ppermute(
            value, AXES, self.perm(lambda z, x, y, c: ((z + step) % self.nz, x, y, c))
        )

    def first(self, value):
        return lax.ppermute(
            value,
            AXES,
            self.perm(lambda z, x, y, c: (z, x, 1 - y, c) if c else (z, 1 - x, y, c)),
        )

    def second(self, value):
        return lax.ppermute(
            value,
            AXES,
            self.perm(lambda z, x, y, c: (z, 1 - x, y, c) if c else (z, x, 1 - y, c)),
        )


def piece_spot(plan, meta, r, fy, fx, k, sign):
    z, x, y, c = meta[1], meta[2], meta[3], meta[4]
    cc = jnp.bitwise_xor(c, r)
    zz = lax.rem(z + sign * k + plan.nz, plan.nz)
    xx = jnp.bitwise_xor(x, fx)
    yy = jnp.bitwise_xor(y, fy)
    return cc, zz, xx, yy


def attn_weight_copies(plan, meta, own, other, w, sem, lanes):
    if not plan.direct:
        src = own.at[:, :, lanes]
        return [pltpu.make_async_copy(src, w, sem.at[0])]
    copies = []
    for r, src in enumerate((own, other)):
        for s2 in range(2):
            for s1 in range(2):
                for k in range(plan.nz):
                    cc = jnp.bitwise_xor(meta[4], r)
                    fx = jnp.where(cc == 0, s1, s2)
                    fy = jnp.where(cc == 0, s2, s1)
                    _, zz, xx, yy = piece_spot(plan, meta, r, fy, fx, k, -1)
                    row = pl.multiple_of((zz * 2 + xx) * plan.rows + cc * plan.half, 16)
                    copies.append(
                        pltpu.make_async_copy(
                            src.at[s2, s1, k, :, lanes],
                            w.at[yy, pl.ds(row, plan.half), :],
                            sem.at[len(copies)],
                        )
                    )
    return copies


def attn_fwd_kernel(
    plan,
    meta,
    x_ref,
    segc_ref,
    segr_ref,
    np_ref,
    pb_ref,
    own,
    other,
    sl_ref,
    mid_ref,
    fl_ref,
    qkv_ref,
    p_ref,
    ctx_ref,
    w,
    sem,
):
    cols = plan.cols
    first = pl.program_id(0) == 0

    @pl.when(first)
    def _():
        for copy in attn_weight_copies(plan, meta, own, other, w, sem, slice(None)):
            copy.start()

    x = x_ref[...].astype(f32)
    normal, _ = norm_stats(x)
    fl = (normal * np_ref[0:1, :] + np_ref[1:2, :]).astype(bf16)
    fl_ref[...] = fl

    @pl.when(first)
    def _():
        for copy in attn_weight_copies(plan, meta, own, other, w, sem, slice(None)):
            copy.wait()

    for y in range(2):
        for part in range(3):
            got = mm(fl, w[y, :, part * cols : (part + 1) * cols])
            if part != 1:
                got = got + pb_ref[part // 2 : part // 2 + 1, y * cols : (y + 1) * cols]
            qkv_ref[y, :, part * cols : (part + 1) * cols] = got.astype(bf16)
    tiles = x.shape[0] // LANES
    pairs = cols // LANES
    for t in range(tiles):
        tok = slice(t * LANES, (t + 1) * LANES)
        same = segc_ref[tok, :] == segr_ref[0, t : t + 1, :]
        same = jnp.concatenate([same, same], axis=0)
        for y in range(2):
            for p in range(pairs):
                at = [slice(b * cols + p * LANES, b * cols + (p + 1) * LANES) for b in range(3)]
                qs = split_heads(qkv_ref[y, tok, at[0]])
                s = mm_nt(qs, qkv_ref[y, tok, at[1]]) * HD**-0.5
                s = jnp.where(same, s, NEG)
                e = jnp.exp(s - jnp.max(s, axis=-1, keepdims=True))
                probs = (e / jnp.sum(e, axis=-1, keepdims=True)).astype(bf16)
                p_ref[(t * 2 + y) * pairs + p] = probs
                ctx = join_heads(mm(probs, qkv_ref[y, tok, at[2]]))
                ctx_ref[tok, y * cols + p * LANES : y * cols + (p + 1) * LANES] = ctx.astype(bf16)
    attended = mm_nt(ctx_ref[:, 0:cols], w[0, :, 3 * cols :])
    attended = attended + mm_nt(ctx_ref[:, cols:], w[1, :, 3 * cols :])
    middle = x + attended + np_ref[4:5, :]
    mid_ref[...] = middle
    normal, _ = norm_stats(middle)
    sl_ref[...] = (normal * np_ref[2:3, :] + np_ref[3:4, :]).astype(bf16)


def ff_weight_copies(plan, meta, own, other, w, sem, r, e):
    if not plan.direct:
        return [pltpu.make_async_copy((own, other)[r].at[e], w.at[e, r], sem.at[r, e, 0])]
    copies = []
    src = (own, other)[r]
    for fx in range(2):
        for k in range(plan.nz):
            _, zz, xx, _ = piece_spot(plan, meta, r, 0, fx, k, -1)
            row = pl.multiple_of((zz * 2 + xx) * plan.rows, 16)
            copies.append(
                pltpu.make_async_copy(
                    src.at[fx, k, e],
                    w.at[e, r, pl.ds(row, plan.rows), :],
                    sem.at[r, e, len(copies)],
                )
            )
    return copies


def ff_kernel(
    plan, meta, sl_ref, cot_ref, hb_ref, own, other, sg_ref, fed_ref, act_ref, hg_ref, gh_ref, w, sem
):
    step = pl.program_id(0)
    first = step == 0

    def when_first(action, r, e):
        @pl.when(first)
        def _():
            for copy in ff_weight_copies(plan, meta, own, other, w, sem, r, e):
                getattr(copy, action)()

    for r in range(2):
        for e in range(2):
            when_first("start", r, e)

    @pl.when(first)
    def _():
        gh_ref[...] = jnp.zeros_like(gh_ref)

    sl = sl_ref[...]
    cot = cot_ref[...]
    sg = None
    fed = None
    for r in range(2):
        when_first("wait", r, 0)
        h = mm(sl, w[0, r]) + hb_ref[r : r + 1, :]
        square = h * h
        t = jnp.tanh(GELU_C * (h + GELU_K * h * square))
        act = (0.5 * h * (1.0 + t)).astype(bf16)
        slope = 0.5 * (1.0 + t) + (0.5 * GELU_C) * h * (1.0 - t * t) * (
            1.0 + (3.0 * GELU_K) * square
        )
        act_ref[r] = act
        when_first("wait", r, 1)
        hg = (mm(cot, w[1, r]) * slope).astype(bf16)
        hg_ref[r] = hg
        gh_ref[r : r + 1, :] += jnp.sum(hg.astype(f32), axis=0, keepdims=True)
        part = mm_nt(hg, w[0, r])
        sg = part if sg is None else sg + part
        part = mm_nt(act, w[1, r])
        fed = part if fed is None else fed + part
    sg_ref[...] = sg.astype(sg_ref.dtype)
    fed_ref[...] = fed.astype(fed_ref.dtype)


def ff_grad_copies(plan, meta, buf, outs, sem, r):
    if not plan.direct:
        return [pltpu.make_async_copy(buf.at[r], outs[r], sem.at[r, 0])]
    copies = []
    for e in range(2):
        for fx in range(2):
            for k in range(plan.nz):
                _, zz, xx, _ = piece_spot(plan, meta, r, 0, fx, k, 1)
                row = pl.multiple_of((zz * 2 + xx) * plan.rows, 16)
                copies.append(
                    pltpu.make_async_copy(
                        buf.at[r, e, pl.ds(row, plan.rows), :],
                        outs[r].at[fx, k, e],
                        sem.at[r, len(copies)],
                    )
                )
    return copies


def ff_grad_kernel(
    plan,
    meta,
    sl_a,
    sl_b,
    cot_a,
    cot_b,
    act_a,
    act_b,
    hg_a,
    hg_b,
    mine,
    theirs,
    left,
    buf,
    sem,
):
    step = pl.program_id(0)
    count = sl_a.shape[0]

    @pl.when(step == 0)
    def _():
        left[0, :, :count] = sl_a[...].T
        left[0, :, count:] = sl_b[...].T
        left[1, :, :count] = cot_a[...].T
        left[1, :, count:] = cot_b[...].T

    wide = plan.part // 2
    for r in range(2):

        @pl.when(step == r)
        def _():
            for e, (one, two) in enumerate(((hg_a, hg_b), (act_a, act_b))):
                for n in range(2):
                    at = slice(n * wide, (n + 1) * wide)
                    got = mm(left[e, :, :count], one[0, :, at])
                    got = got + mm(left[e, :, count:], two[0, :, at])
                    buf[r, e, :, at] = got.astype(bf16)
            for copy in ff_grad_copies(plan, meta, buf, (mine, theirs), sem, r):
                copy.start()

    @pl.when(step == 1)
    def _():
        for r in range(2):
            for copy in ff_grad_copies(plan, meta, buf, (mine, theirs), sem, r):
                copy.wait()


def attn_bwd_kernel(
    plan,
    meta,
    sga_ref,
    sgb_ref,
    mid_ref,
    cot_ref,
    np_ref,
    qkv_ref,
    p_ref,
    own,
    other,
    dqkv_ref,
    ml_ref,
    mg_ref,
    vec_ref,
    pair_ref,
    w,
    sem,
):
    cols = plan.cols
    first = pl.program_id(0) == 0
    lanes = slice(3 * cols, 4 * cols)

    @pl.when(first)
    def _():
        for copy in attn_weight_copies(plan, meta, own, other, w, sem, lanes):
            copy.start()
        vec_ref[...] = jnp.zeros_like(vec_ref)
        pair_ref[...] = jnp.zeros_like(pair_ref)

    sg = sga_ref[...].astype(f32) + sgb_ref[...].astype(f32)
    cot = cot_ref[...].astype(f32)
    normal, scaled = norm_stats(mid_ref[...])
    mg = cot + norm_backward(sg, normal, scaled, np_ref[2:3, :])
    mg_ref[...] = mg
    ml = mg.astype(bf16)
    ml_ref[...] = ml
    vec_ref[0:1, :] += jnp.sum(sg * normal, axis=0, keepdims=True)
    vec_ref[1:2, :] += jnp.sum(sg, axis=0, keepdims=True)
    vec_ref[2:3, :] += jnp.sum(mg, axis=0, keepdims=True)
    vec_ref[3:4, :] += jnp.sum(cot, axis=0, keepdims=True)

    @pl.when(first)
    def _():
        for copy in attn_weight_copies(plan, meta, own, other, w, sem, lanes):
            copy.wait()

    tiles = ml.shape[0] // LANES
    pairs = cols // LANES
    for y in range(2):
        dctx = mm(ml, w[y]).astype(bf16)
        for t in range(tiles):
            tok = slice(t * LANES, (t + 1) * LANES)
            for p in range(pairs):
                at = [slice(b * cols + p * LANES, b * cols + (p + 1) * LANES) for b in range(3)]
                dcs = split_heads(dctx[tok, p * LANES : (p + 1) * LANES])
                qs = split_heads(qkv_ref[y, tok, at[0]])
                low = p_ref[(t * 2 + y) * pairs + p]
                probs = low.astype(f32)
                dp = mm_nt(dcs, qkv_ref[y, tok, at[2]])
                inner = jnp.sum(dp * probs, axis=-1, keepdims=True)
                ds = (probs * (dp - inner) * HD**-0.5).astype(bf16)
                dq = join_heads(mm(ds, qkv_ref[y, tok, at[1]])).astype(bf16)
                dk = mm_tn(ds, qs).astype(bf16)
                dv = mm_tn(low, dcs).astype(bf16)
                dqkv_ref[y, tok, at[0]] = dq
                dqkv_ref[y, tok, at[1]] = dk
                dqkv_ref[y, tok, at[2]] = dv
        for b in (0, 2):
            at = slice(b * cols, (b + 1) * cols)
            pair_ref[b // 2 : b // 2 + 1, y * cols : (y + 1) * cols] += jnp.sum(
                dqkv_ref[y, :, at].astype(f32), axis=0, keepdims=True
            )


def attn_grad_copies(plan, meta, buf, outs, sem, fy):
    if not plan.direct:
        yy = jnp.bitwise_xor(meta[3], fy)
        return [pltpu.make_async_copy(buf.at[fy], outs[0].at[yy], sem.at[fy, 0])]
    copies = []
    for r in range(2):
        for fx in range(2):
            for k in range(plan.nz):
                cc, zz, xx, _ = piece_spot(plan, meta, r, fy, fx, k, 1)
                s1 = jnp.where(cc == 0, fx, fy)
                s2 = jnp.where(cc == 0, fy, fx)
                row = pl.multiple_of((zz * 2 + xx) * plan.rows + cc * plan.half, 16)
                copies.append(
                    pltpu.make_async_copy(
                        buf.at[fy, pl.ds(row, plan.half), :],
                        outs[r].at[s2, s1, k],
                        sem.at[fy, len(copies)],
                    )
                )
    return copies


def attn_grad_kernel(plan, meta, fl_ref, ml_ref, dqkv_ref, ctx_ref, *rest):
    *outs, left, buf, sem = rest
    step = pl.program_id(0)
    cols = plan.cols

    @pl.when(step == 0)
    def _():
        left[0] = fl_ref[...].T
        left[1] = ml_ref[...].T

    for fy in range(2):

        @pl.when(step == fy)
        def _():
            for b in range(3):
                at = slice(b * cols, (b + 1) * cols)
                buf[fy, :, at] = mm(left[0], dqkv_ref[0, :, at]).astype(bf16)
            buf[fy, :, 3 * cols :] = mm(left[1], ctx_ref[...]).astype(bf16)
            for copy in attn_grad_copies(plan, meta, buf, outs, sem, fy):
                copy.start()

    @pl.when(step == 1)
    def _():
        for fy in range(2):
            for copy in attn_grad_copies(plan, meta, buf, outs, sem, fy):
                copy.wait()


def input_grad_kernel(
    plan, meta, x_ref, mg_ref, np_ref, dqkv_ref, own, other, ig_ref, vec_ref, w, sem
):
    cols = plan.cols
    first = pl.program_id(0) == 0
    lanes = slice(0, 3 * cols)

    @pl.when(first)
    def _():
        for copy in attn_weight_copies(plan, meta, own, other, w, sem, lanes):
            copy.start()
        vec_ref[...] = jnp.zeros_like(vec_ref)

    normal, scaled = norm_stats(x_ref[...].astype(f32))

    @pl.when(first)
    def _():
        for copy in attn_weight_copies(plan, meta, own, other, w, sem, lanes):
            copy.wait()

    fg = mm_nt(dqkv_ref[0], w[0]) + mm_nt(dqkv_ref[1], w[1])
    vec_ref[0:1, :] += jnp.sum(fg * normal, axis=0, keepdims=True)
    vec_ref[1:2, :] += jnp.sum(fg, axis=0, keepdims=True)
    ig = mg_ref[...] + norm_backward(fg, normal, scaled, np_ref[0:1, :])
    ig_ref[...] = ig.astype(bf16)


def place_kernel(meta, own, by_y, by_c, by_yc, out, sem):
    count = own.shape[0]
    copies = []
    for fy, fc, src in ((0, 0, own), (1, 0, by_y), (0, 1, by_c), (1, 1, by_yc)):
        at = jnp.bitwise_xor(meta[3], fy) * 2 + jnp.bitwise_xor(meta[4], fc)
        dst = out.at[pl.ds(pl.multiple_of(at * count, 16), count), :]
        copies.append(pltpu.make_async_copy(src, dst, sem.at[len(copies)]))
    for copy in copies:
        copy.start()
    for copy in copies:
        copy.wait()


def adam_kernel(rates, factor_ref, *refs):
    count = len(rates)
    factor = factor_ref[0, 0]
    correction = 1.0 - BETA**STEP
    for i, (rate, decay) in enumerate(rates):
        w_ref, m_ref, s_ref, g_ref = refs[4 * i : 4 * i + 4]
        m_out, s_out, w_out = refs[4 * count + 3 * i : 4 * count + 3 * i + 3]
        clipped = g_ref[...] * factor
        first = BETA * m_ref[...] + (1.0 - BETA) * clipped
        second = BETA * s_ref[...] + (1.0 - BETA) * clipped * clipped
        weight = w_ref[...]
        direction = first / correction / (jnp.sqrt(second / correction) + ADAM_EPS)
        m_out[...] = first
        s_out[...] = second
        w_out[...] = weight - rate * (direction + decay * weight)


def any_spec():
    return pl.BlockSpec(memory_space=pl.ANY)


def call(kernel, name, grid, ins, outs, scratch, flops, moved, vmem=56):
    def spec(item):
        if item[1] is None:
            return any_spec()
        return pl.BlockSpec(item[1], item[2])

    return pl.pallas_call(
        kernel,
        name=name,
        out_shape=[o[0] for o in outs],
        grid_spec=pltpu.PrefetchScalarGridSpec(
            num_scalar_prefetch=1,
            grid=grid,
            in_specs=[spec(i) for i in ins],
            out_specs=[spec(o) for o in outs],
            scratch_shapes=scratch,
        ),
        compiler_params=pltpu.CompilerParams(vmem_limit_bytes=vmem * MIB),
        cost_estimate=pl.CostEstimate(flops=flops, bytes_accessed=moved, transcendentals=0),
    )


def per_device(
    inputs,
    segments,
    cotangent,
    triple_weight,
    triple_first,
    triple_second,
    outward_weight,
    outward_first,
    outward_second,
    expand_weight,
    expand_first,
    expand_second,
    reduce_weight,
    reduce_first,
    reduce_second,
    norm_params,
    norm_first,
    norm_second,
    paired_bias,
    paired_first,
    paired_second,
    hidden_bias,
    hidden_first,
    hidden_second,
):
    ndp, nmp = lax.axis_size("dp"), lax.axis_size("mp")
    width = inputs.shape[1]
    hidden = hidden_bias.shape[0] * nmp
    plan = Plan(ndp, nmp, width, hidden)
    nz, rows, half, cols, part = plan.nz, plan.rows, plan.half, plan.cols, plan.part
    count = inputs.shape[0] // nmp
    row_count, row_length = segments.shape
    own_rows = row_count // nmp
    steps = count // CHUNK
    tiles = CHUNK // LANES
    units = tiles * 2 * (cols // LANES)
    quarter = cols // 2

    dp, mp = lax.axis_index("dp"), lax.axis_index("mp")
    z, x, y, c = dp // 2, dp % 2, mp // 2, mp % 2
    meta = jnp.stack([mp, z, x, y, c, jnp.bitwise_xor(mp, 2)]).astype(jnp.int32)
    core_zero = c == 0
    SDS = jax.ShapeDtypeStruct

    shard = jnp.concatenate(
        [triple_weight.astype(bf16), outward_weight.T.astype(bf16)[None]], axis=0
    ).transpose(1, 0, 2)
    keep = lax.dynamic_slice_in_dim(shard, c * half, half, 0)
    send = lax.dynamic_slice_in_dim(shard, (1 - c) * half, half, 0)
    got = plan.core(send)
    low = jnp.where(core_zero, keep, got)
    high = jnp.where(core_zero, got, keep)
    unit = jnp.concatenate([low, high], axis=2).reshape(half, 4 * cols)
    spread = jnp.stack([unit] + [plan.along_z(unit, k) for k in range(1, nz)])
    spread = jnp.stack([spread, plan.first(spread)])
    attn_own = jnp.stack([spread, plan.second(spread)])
    attn_other = plan.core(attn_own)

    unit = jnp.stack([expand_weight.astype(bf16), reduce_weight.T.astype(bf16)])
    spread = jnp.stack([unit] + [plan.along_z(unit, k) for k in range(1, nz)])
    ff_own = jnp.stack([spread, plan.along_x(spread)])
    ff_other = plan.core(ff_own)

    if not plan.direct:
        attn_own = absolute_attn(plan, attn_own, attn_other, z, x, y, c)
        attn_other = meta
        ff_own = absolute_ff(plan, ff_own, z, x)
        ff_other = absolute_ff(plan, ff_other, z, x)

    by_core = plan.core(jnp.concatenate([paired_bias.reshape(-1), hidden_bias]))
    other_pair = by_core[: 2 * quarter].reshape(2, quarter)
    near = jnp.where(
        core_zero,
        jnp.concatenate([paired_bias, other_pair], axis=1),
        jnp.concatenate([other_pair, paired_bias], axis=1),
    )
    far = plan.along_y(near)
    pair_full = jnp.where(
        y == 0, jnp.concatenate([near, far], axis=1), jnp.concatenate([far, near], axis=1)
    )
    hidden_rows = jnp.stack([hidden_bias, by_core[2 * quarter :]])

    marks = lax.dynamic_slice_in_dim(segments, mp * own_rows, own_rows, 0)
    marks = marks + row_length * lax.broadcasted_iota(jnp.int32, marks.shape, 0)
    mark_col = marks.reshape(count, 1)
    mark_row = marks.reshape(steps, tiles, LANES)

    whole = lambda shape: (shape, lambda i, m: (0,) * len(shape))
    chunk = lambda n: ((CHUNK, n), lambda i, m: (i, 0))
    mine_rows = ((CHUNK, width), lambda i, m: (m[0] * steps + i, 0))
    pair_rows = ((CHUNK, width), lambda i, m: (m[5] * steps + i, 0))
    pieces = 2 * 2 * 2 * nz if plan.direct else 1
    dma = pltpu.SemaphoreType.DMA
    qkv_block = ((2, CHUNK, 3 * cols), lambda i, m: (0, i, 0))
    p_block = ((units, 2 * LANES, LANES), lambda i, m: (i, 0, 0))

    sl, middle, fl, qkv, probs, ctx = call(
        functools.partial(attn_fwd_kernel, plan),
        "attn_fwd",
        (steps,),
        [
            (inputs, *mine_rows),
            (mark_col, *chunk(1)),
            (mark_row, (1, tiles, LANES), lambda i, m: (i, 0, 0)),
            (norm_params, *whole(norm_params.shape)),
            (pair_full, *whole(pair_full.shape)),
            (attn_own, None, None),
            (attn_other, None, None),
        ],
        [
            (SDS((count, width), bf16), *chunk(width)),
            (SDS((count, width), f32), *chunk(width)),
            (SDS((count, width), bf16), *chunk(width)),
            (SDS((2, count, 3 * cols), bf16), *qkv_block),
            (SDS((steps * units, 2 * LANES, LANES), bf16), *p_block),
            (SDS((count, width), bf16), *chunk(width)),
        ],
        [pltpu.VMEM((2, width, 4 * cols), bf16), dma((pieces,))],
        flops=8 * count * width * width,
        moved=16 * MIB,
    )(meta, inputs, mark_col, mark_row, norm_params, pair_full, attn_own, attn_other)

    sl_far = plan.along_y(sl)

    def feed_forward(sl_in, cot_rows, out_type):
        return call(
            functools.partial(ff_kernel, plan),
            "feed_forward",
            (steps,),
            [
                (sl_in, *chunk(width)),
                (cotangent, *cot_rows),
                (hidden_rows, *whole(hidden_rows.shape)),
                (ff_own, None, None),
                (ff_other, None, None),
            ],
            [
                (SDS((count, width), out_type), *chunk(width)),
                (SDS((count, width), out_type), *chunk(width)),
                (SDS((2, count, part), bf16), (2, CHUNK, part), lambda i, m: (0, i, 0)),
                (SDS((2, count, part), bf16), (2, CHUNK, part), lambda i, m: (0, i, 0)),
                (SDS((2, part), f32), *whole((2, part))),
            ],
            [
                pltpu.VMEM((2, 2, width, part), bf16),
                dma((2, 2, 2 * nz if plan.direct else 1)),
            ],
            flops=16 * count * width * part,
            moved=14 * MIB,
        )(meta, sl_in, cotangent, hidden_rows, ff_own, ff_other)

    sg_near, fed_near, act_near, hg_near, gh_near = feed_forward(sl, mine_rows, f32)
    sg_send, fed_send, act_far, hg_far, gh_far = feed_forward(sl_far, pair_rows, bf16)
    sg_far = plan.along_y(sg_send)
    fed_far = plan.along_y(fed_send)

    half_block = ((1, count, part), lambda i, m: (i, 0, 0))
    all_mine = ((count, width), lambda i, m: (m[0], 0))
    all_pair = ((count, width), lambda i, m: (m[5], 0))
    if plan.direct:
        grad_shape = SDS((2, nz, 2, rows, part), bf16)
    else:
        grad_shape = SDS((2, width, part), bf16)
    ff_mine, ff_theirs = call(
        functools.partial(ff_grad_kernel, plan),
        "ff_grad",
        (2,),
        [
            (sl, *whole((count, width))),
            (sl_far, *whole((count, width))),
            (cotangent, *all_mine),
            (cotangent, *all_pair),
            (act_near, *half_block),
            (act_far, *half_block),
            (hg_near, *half_block),
            (hg_far, *half_block),
        ],
        [(grad_shape, None, None), (grad_shape, None, None)],
        [
            pltpu.VMEM((2, width, 2 * count), bf16),
            pltpu.VMEM((2, 2, width, part), bf16),
            dma((2, 4 * nz if plan.direct else 1)),
        ],
        flops=16 * count * width * part,
        moved=16 * MIB,
    )(meta, sl, sl_far, cotangent, cotangent, act_near, act_far, hg_near, hg_far)

    dqkv, ml, mg, vec_two, pair_sum = call(
        functools.partial(attn_bwd_kernel, plan),
        "attn_bwd",
        (steps,),
        [
            (sg_near, *chunk(width)),
            (sg_far, *chunk(width)),
            (middle, *chunk(width)),
            (cotangent, *mine_rows),
            (norm_params, *whole(norm_params.shape)),
            (qkv, *qkv_block),
            (probs, *p_block),
            (attn_own, None, None),
            (attn_other, None, None),
        ],
        [
            (SDS((2, count, 3 * cols), bf16), *qkv_block),
            (SDS((count, width), bf16), *chunk(width)),
            (SDS((count, width), f32), *chunk(width)),
            (SDS((8, width), f32), *whole((8, width))),
            (SDS((2, width), f32), *whole((2, width))),
        ],
        [pltpu.VMEM((2, width, cols), bf16), dma((pieces,))],
        flops=6 * count * width * width,
        moved=12 * MIB,
    )(meta, sg_near, sg_far, middle, cotangent, norm_params, qkv, probs, attn_own, attn_other)

    if plan.direct:
        grad_shapes = [SDS((2, 2, nz, half, 4 * cols), bf16)] * 2
    else:
        grad_shapes = [SDS((2, width, 4 * cols), bf16)]
    attn_grads = call(
        functools.partial(attn_grad_kernel, plan),
        "attn_grad",
        (2,),
        [
            (fl, *whole((count, width))),
            (ml, *whole((count, width))),
            (dqkv, (1, count, 3 * cols), lambda i, m: (jnp.bitwise_xor(m[3], i), 0, 0)),
            (ctx, (count, cols), lambda i, m: (0, jnp.bitwise_xor(m[3], i))),
        ],
        [(s, None, None) for s in grad_shapes],
        [
            pltpu.VMEM((2, width, count), bf16),
            pltpu.VMEM((2, width, 4 * cols), bf16),
            dma((2, 4 * nz if plan.direct else 1)),
        ],
        flops=8 * count * width * width,
        moved=10 * MIB,
    )(meta, fl, ml, dqkv, ctx)
    if plan.direct:
        attn_mine, attn_theirs = attn_grads
    else:
        attn_mine, attn_theirs = relative_attn(plan, attn_grads[0], z, x, y, c)
        ff_mine = relative_ff(plan, ff_mine, z, x)
        ff_theirs = relative_ff(plan, ff_theirs, z, x)

    ig, vec_one = call(
        functools.partial(input_grad_kernel, plan),
        "input_grad",
        (steps,),
        [
            (inputs, *mine_rows),
            (mg, *chunk(width)),
            (norm_params, *whole(norm_params.shape)),
            (dqkv, *qkv_block),
            (attn_own, None, None),
            (attn_other, None, None),
        ],
        [
            (SDS((count, width), bf16), *chunk(width)),
            (SDS((8, width), f32), *whole((8, width))),
        ],
        [pltpu.VMEM((2, width, 3 * cols), bf16), dma((pieces,))],
        flops=6 * count * width * width,
        moved=10 * MIB,
    )(meta, inputs, mg, norm_params, dqkv, attn_own, attn_other)

    out = (middle + fed_near + fed_far.astype(f32) + norm_params[5]).astype(bf16)

    def everywhere(block):
        by_y = plan.along_y(block)
        by_c = plan.core(block)
        by_yc = plan.core(by_y)
        return call(
            place_kernel,
            "place",
            (1,),
            [(b, None, None) for b in (block, by_y, by_c, by_yc)],
            [(SDS((count * nmp, width), bf16), None, None)],
            [dma((4,))],
            flops=0,
            moved=6 * MIB,
            vmem=8,
        )(meta, block, by_y, by_c, by_yc)[0]

    outputs = everywhere(out)
    input_gradient = everywhere(ig)

    def plus(one, two):
        return (one.astype(f32) + two.astype(f32)).astype(bf16)

    def sum_z(parts):
        total = parts[0].astype(f32)
        for k in range(1, nz):
            total = total + plan.along_z(parts[k], k).astype(f32)
        return total

    got = plan.core(ff_theirs)
    keep, send = plus(ff_mine[0], got[0]), plus(ff_mine[1], got[1])
    ff_grads = sum_z(plus(keep, plan.along_x(send)))
    grad_expand = ff_grads[0]
    grad_reduce = ff_grads[1].T

    got = plan.core(attn_theirs)
    keep, send = plus(attn_mine[0], got[0]), plus(attn_mine[1], got[1])
    got = plan.second(send)
    keep, send = plus(keep[0], got[0]), plus(keep[1], got[1])
    unit = sum_z(plus(keep, plan.first(send))).reshape(half, 4, 2, quarter)
    keep = jnp.where(core_zero, unit[:, :, 0], unit[:, :, 1])
    got = plan.core(jnp.where(core_zero, unit[:, :, 1], unit[:, :, 0]))
    shard = jnp.concatenate(
        [jnp.where(core_zero, keep, got), jnp.where(core_zero, got, keep)], axis=0
    )
    grad_triple = shard[:, :3].transpose(1, 0, 2)
    grad_outward = shard[:, 3].T

    gh = gh_near + gh_far
    gh = jnp.where(core_zero, gh, gh[::-1]).reshape(-1)
    zero = jnp.zeros_like(gh)
    gh = jnp.where(y == 0, jnp.concatenate([gh, zero]), jnp.concatenate([zero, gh]))
    vectors = jnp.concatenate(
        [vec_one[:2].reshape(-1), vec_two[:4].reshape(-1), pair_sum.reshape(-1), gh]
    )
    size = vectors.shape[0] // plan.ndev
    got = lax.all_to_all(vectors.reshape(plan.ndev, size), AXES, 0, 0, tiled=True)
    local = jnp.sum(got, axis=0)
    square = jnp.sum(ff_grads * ff_grads) + jnp.sum(unit * unit)
    square = square + jnp.sum(local * local)
    payload = jnp.concatenate([local, square[None]])
    payload = jnp.broadcast_to(payload[None], (plan.ndev, size + 1))
    got = lax.all_to_all(payload, AXES, 0, 0, tiled=True)
    gradient_norm = jnp.sqrt(jnp.sum(got[:, size]))
    factor = jnp.minimum(1.0, CLIP / gradient_norm)
    vectors = got[:, :size].reshape(-1)
    grad_norms = vectors[: 6 * width].reshape(6, width)
    grad_paired = vectors[6 * width : 8 * width].reshape(2, width)
    grad_paired = lax.dynamic_slice_in_dim(grad_paired, mp * quarter, quarter, 1)
    grad_hidden = lax.dynamic_slice_in_dim(vectors[8 * width :], mp * part, part, 0)

    matrix, vector = (LR_MATRIX, DECAY), (LR_VECTOR, 0.0)
    groups = [
        (triple_weight, triple_first, triple_second, grad_triple),
        (outward_weight, outward_first, outward_second, grad_outward),
        (expand_weight, expand_first, expand_second, grad_expand),
        (reduce_weight, reduce_first, reduce_second, grad_reduce),
        (norm_params, norm_first, norm_second, grad_norms),
        (paired_bias, paired_first, paired_second, grad_paired),
        tuple(
            v.reshape(1, -1) for v in (hidden_bias, hidden_first, hidden_second, grad_hidden)
        ),
    ]
    flat = [v for group in groups for v in group]
    vmem = pl.BlockSpec(memory_space=pltpu.VMEM)
    new = pl.pallas_call(
        functools.partial(adam_kernel, (matrix,) * 4 + (vector,) * 3),
        name="adam",
        out_shape=[SDS(group[0].shape, f32) for group in groups for _ in range(3)],
        in_specs=[pl.BlockSpec(memory_space=pltpu.SMEM)] + [vmem] * len(flat),
        out_specs=[vmem] * (3 * len(groups)),
        compiler_params=pltpu.CompilerParams(vmem_limit_bytes=32 * MIB),
    )(factor.reshape(1, 1), *flat)
    new = list(new)
    new[18:] = [v.reshape(-1) for v in new[18:]]
    return (outputs, input_gradient, gradient_norm, *new)


def turn(plan, value, z, axis):
    value = jnp.flip(value, axis)
    return jnp.roll(value, z + 1, axis)


def unturn(plan, value, z, axis):
    return jnp.roll(value, -z, axis)


def swap(value, flag, axis):
    return jnp.where(flag == 1, jnp.flip(value, axis), value)


def absolute_ff(plan, value, z, x):
    value = swap(turn(plan, value, z, 1), x, 0)
    value = value.transpose(2, 1, 0, 3, 4)
    return value.reshape(2, plan.width, plan.part)


def relative_ff(plan, value, z, x):
    value = value.reshape(2, plan.nz, 2, plan.rows, plan.part).transpose(2, 1, 0, 3, 4)
    return unturn(plan, swap(value, x, 0), z, 1)


def absolute_attn(plan, own, other, z, x, y, c):
    zero = jnp.where(c == 0, own, other)
    one = jnp.where(c == 0, other, own).transpose(1, 0, 2, 3, 4)
    value = jnp.stack([zero, one])
    value = turn(plan, swap(swap(value, y, 1), x, 2), z, 3)
    value = value.transpose(1, 3, 2, 0, 4, 5)
    return value.reshape(2, plan.width, 4 * plan.cols)


def relative_attn(plan, value, z, x, y, c):
    value = value.reshape(2, plan.nz, 2, 2, plan.half, 4 * plan.cols)
    value = value.transpose(3, 0, 2, 1, 4, 5)
    value = unturn(plan, swap(swap(value, y, 1), x, 2), z, 3)
    zero, one = value[0], value[1].transpose(1, 0, 2, 3, 4)
    return jnp.where(c == 0, zero, one), jnp.where(c == 0, one, zero)


def solution(mesh):
    tokens = P("dp", None)
    triple = P(None, "dp", "mp")
    tall = P("mp", "dp")
    wide = P("dp", "mp")
    pair = P(None, "mp")
    states = ((triple,) * 3, (tall,) * 3, (wide,) * 3, (tall,) * 3, (P(),) * 3, (pair,) * 3)
    states = sum(states, ()) + (P("mp"),) * 3
    return jax.shard_map(
        per_device,
        mesh=mesh,
        in_specs=(tokens,) * 3 + states,
        out_specs=(tokens, tokens, P()) + states,
        check_vma=False,
    )
```

```python
import functools

import jax
import jax.numpy as jnp
from jax import lax
from jax.experimental import pallas as pl
from jax.experimental.pallas import tpu as pltpu
from jax.sharding import PartitionSpec as P

HD = 64
STEP = 5
EPS_NORM = 1e-06
BETA = 0.5
LR_MATRIX = 0.03
LR_VECTOR = 0.2
DECAY = 0.1
ADAM_EPS = 1e-08
CLIP = 1.0
NEG = -1e30
GELU_C = 0.7978845608028654
GELU_K = 0.044715

f32 = jnp.float32
bf16 = jnp.bfloat16
AXES = ("dp", "mp")
LANES = 128
CHUNK = 256
MIB = 1 << 20


def mm(left, right):
    return lax.dot_general(left, right, (((1,), (0,)), ((), ())), preferred_element_type=f32)


def mm_nt(left, right):
    return lax.dot_general(left, right, (((1,), (1,)), ((), ())), preferred_element_type=f32)


def mm_tn(left, right):
    return lax.dot_general(left, right, (((0,), (0,)), ((), ())), preferred_element_type=f32)


def norm_stats(rows_in):
    centred = rows_in - jnp.mean(rows_in, axis=-1, keepdims=True)
    scaled = lax.rsqrt(jnp.mean(centred * centred, axis=-1, keepdims=True) + EPS_NORM)
    return centred * scaled, scaled


def norm_backward(upstream, normal_rows, scaled, gain_row):
    gained = upstream * gain_row
    mean_one = jnp.mean(gained, axis=-1, keepdims=True)
    mean_two = jnp.mean(gained * normal_rows, axis=-1, keepdims=True)
    return scaled * (gained - mean_one - normal_rows * mean_two)


def lane_low(shape):
    return lax.broadcasted_iota(jnp.int32, shape, 1) % LANES < HD


def split_heads(block):
    low = lane_low(block.shape)
    zero = jnp.zeros_like(block)
    return jnp.concatenate([jnp.where(low, block, zero), jnp.where(low, zero, block)], axis=0)


def join_heads(stacked):
    half = stacked.shape[0] // 2
    low = lane_low((half, stacked.shape[1]))
    return jnp.where(low, stacked[:half], stacked[half:])


class Plan:
    def __init__(self, ndp, nmp, width, hidden):
        assert ndp % 2 == 0 and nmp == 4
        self.ndev = ndp * nmp
        self.nz = ndp // 2
        self.rows = width // ndp
        self.half = self.rows // 2
        self.width = width
        self.cols = width // 2
        self.part = hidden // nmp
        self.direct = self.half % 16 == 0

    def perm(self, move):
        pairs = []
        for z in range(self.nz):
            for x in range(2):
                for y in range(2):
                    for c in range(2):
                        there = move(z, x, y, c)
                        pairs.append((self.index(z, x, y, c), self.index(*there)))
        return pairs

    def index(self, z, x, y, c):
        return (2 * z + x) * 4 + 2 * y + c

    def core(self, value):
        return lax.ppermute(value, AXES, self.perm(lambda z, x, y, c: (z, x, y, 1 - c)))

    def along_x(self, value):
        return lax.ppermute(value, AXES, self.perm(lambda z, x, y, c: (z, 1 - x, y, c)))

    def along_y(self, value):
        return lax.ppermute(value, AXES, self.perm(lambda z, x, y, c: (z, x, 1 - y, c)))

    def along_z(self, value, step):
        return lax.ppermute(
            value, AXES, self.perm(lambda z, x, y, c: ((z + step) % self.nz, x, y, c))
        )

    def first(self, value):
        return lax.ppermute(
            value,
            AXES,
            self.perm(lambda z, x, y, c: (z, x, 1 - y, c) if c else (z, 1 - x, y, c)),
        )

    def second(self, value):
        return lax.ppermute(
            value,
            AXES,
            self.perm(lambda z, x, y, c: (z, 1 - x, y, c) if c else (z, x, 1 - y, c)),
        )


def piece_spot(plan, meta, r, fy, fx, k, sign):
    z, x, y, c = meta[1], meta[2], meta[3], meta[4]
    cc = jnp.bitwise_xor(c, r)
    zz = lax.rem(z + sign * k + plan.nz, plan.nz)
    xx = jnp.bitwise_xor(x, fx)
    yy = jnp.bitwise_xor(y, fy)
    return cc, zz, xx, yy


def attn_weight_copies(plan, meta, srcs, w, sem, lanes):
    if not plan.direct:
        return [pltpu.make_async_copy(srcs[0].at[:, :, lanes], w, sem.at[0])]
    copies = []
    for s2 in range(2):
        for r in range(2):
            for s1 in range(2):
                for k in range(plan.nz):
                    cc = jnp.bitwise_xor(meta[4], r)
                    fx = jnp.where(cc == 0, s1, s2)
                    fy = jnp.where(cc == 0, s2, s1)
                    _, zz, xx, yy = piece_spot(plan, meta, r, fy, fx, k, -1)
                    row = pl.multiple_of((zz * 2 + xx) * plan.rows + cc * plan.half, 16)
                    copies.append(
                        pltpu.make_async_copy(
                            srcs[2 * r + s2].at[s1, k, :, lanes],
                            w.at[yy, pl.ds(row, plan.half), :],
                            sem.at[len(copies)],
                        )
                    )
    return copies


def attn_fwd_kernel(
    plan,
    meta,
    x_ref,
    segc_ref,
    segr_ref,
    np_ref,
    pb_ref,
    w_a,
    w_b,
    w_c,
    w_d,
    sl_ref,
    mid_ref,
    fl_ref,
    qkv_ref,
    p_ref,
    ctx_ref,
    w,
    sem,
):
    cols = plan.cols
    first = pl.program_id(0) == 0
    srcs = (w_a, w_b, w_c, w_d)

    @pl.when(first)
    def _():
        for copy in attn_weight_copies(plan, meta, srcs, w, sem, slice(None)):
            copy.start()

    x = x_ref[...].astype(f32)
    normal, _ = norm_stats(x)
    fl = (normal * np_ref[0:1, :] + np_ref[1:2, :]).astype(bf16)
    fl_ref[...] = fl

    @pl.when(first)
    def _():
        for copy in attn_weight_copies(plan, meta, srcs, w, sem, slice(None)):
            copy.wait()

    for y in range(2):
        for part in range(3):
            got = mm(fl, w[y, :, part * cols : (part + 1) * cols])
            if part != 1:
                got = got + pb_ref[part // 2 : part // 2 + 1, y * cols : (y + 1) * cols]
            qkv_ref[y, :, part * cols : (part + 1) * cols] = got.astype(bf16)
    tiles = x.shape[0] // LANES
    pairs = cols // LANES
    for t in range(tiles):
        tok = slice(t * LANES, (t + 1) * LANES)
        same = segc_ref[tok, :] == segr_ref[0, t : t + 1, :]
        same = jnp.concatenate([same, same], axis=0)
        for y in range(2):
            for p in range(pairs):
                at = [slice(b * cols + p * LANES, b * cols + (p + 1) * LANES) for b in range(3)]
                qs = split_heads(qkv_ref[y, tok, at[0]])
                s = mm_nt(qs, qkv_ref[y, tok, at[1]]) * HD**-0.5
                s = jnp.where(same, s, NEG)
                e = jnp.exp(s - jnp.max(s, axis=-1, keepdims=True))
                probs = (e / jnp.sum(e, axis=-1, keepdims=True)).astype(bf16)
                p_ref[(t * 2 + y) * pairs + p] = probs
                ctx = join_heads(mm(probs, qkv_ref[y, tok, at[2]]))
                ctx_ref[tok, y * cols + p * LANES : y * cols + (p + 1) * LANES] = ctx.astype(bf16)
    attended = mm_nt(ctx_ref[:, 0:cols], w[0, :, 3 * cols :])
    attended = attended + mm_nt(ctx_ref[:, cols:], w[1, :, 3 * cols :])
    middle = x + attended + np_ref[4:5, :]
    mid_ref[...] = middle
    normal, _ = norm_stats(middle)
    sl_ref[...] = (normal * np_ref[2:3, :] + np_ref[3:4, :]).astype(bf16)


def ff_weight_copies(plan, meta, srcs, w, sem, r, e):
    src = srcs[4 * e + 2 * r : 4 * e + 2 * r + 2]
    if not plan.direct:
        return [pltpu.make_async_copy(src[0], w.at[e, r], sem.at[r, e, 0])]
    copies = []
    for fx in range(2):
        for k in range(plan.nz):
            _, zz, xx, _ = piece_spot(plan, meta, r, 0, fx, k, -1)
            row = pl.multiple_of((zz * 2 + xx) * plan.rows, 16)
            copies.append(
                pltpu.make_async_copy(
                    src[fx].at[k],
                    w.at[e, r, pl.ds(row, plan.rows), :],
                    sem.at[r, e, len(copies)],
                )
            )
    return copies


def ff_kernel(plan, own, meta, sl_ref, cot_ref, hb_ref, *refs):
    srcs, refs = refs[:8], refs[8:]
    if own:
        mid_ref, *refs = refs
    sg_ref, fed_ref, act_ref, hg_ref, gh_ref, w, sem = refs
    step = pl.program_id(0)
    first = step == 0

    def when_first(action, r, e):
        @pl.when(first)
        def _():
            for copy in ff_weight_copies(plan, meta, srcs, w, sem, r, e):
                getattr(copy, action)()

    for r in range(2):
        for e in range(2):
            when_first("start", r, e)

    @pl.when(first)
    def _():
        gh_ref[...] = jnp.zeros_like(gh_ref)

    sl = sl_ref[...]
    cot = cot_ref[...]
    sg = None
    fed = None
    for r in range(2):
        when_first("wait", r, 0)
        h = mm(sl, w[0, r]) + hb_ref[r : r + 1, :]
        square = h * h
        t = jnp.tanh(GELU_C * (h + GELU_K * h * square))
        act = (0.5 * h * (1.0 + t)).astype(bf16)
        slope = 0.5 * (1.0 + t) + (0.5 * GELU_C) * h * (1.0 - t * t) * (
            1.0 + (3.0 * GELU_K) * square
        )
        act_ref[r] = act
        when_first("wait", r, 1)
        hg = (mm(cot, w[1, r]) * slope).astype(bf16)
        hg_ref[r] = hg
        gh_ref[r : r + 1, :] += jnp.sum(hg.astype(f32), axis=0, keepdims=True)
        part = mm_nt(hg, w[0, r])
        sg = part if sg is None else sg + part
        part = mm_nt(act, w[1, r])
        fed = part if fed is None else fed + part
    sg_ref[...] = sg.astype(sg_ref.dtype)
    if own:
        fed = fed + mid_ref[...]
    fed_ref[...] = fed.astype(fed_ref.dtype)


def ff_grad_copies(plan, meta, buf, outs, sem, r):
    if not plan.direct:
        return [
            pltpu.make_async_copy(buf.at[r, e], outs[2 * r + e], sem.at[r, e]) for e in range(2)
        ]
    copies = []
    for e in range(2):
        for fx in range(2):
            for k in range(plan.nz):
                _, zz, xx, _ = piece_spot(plan, meta, r, 0, fx, k, 1)
                row = pl.multiple_of((zz * 2 + xx) * plan.rows, 16)
                copies.append(
                    pltpu.make_async_copy(
                        buf.at[r, e, pl.ds(row, plan.rows), :],
                        outs[4 * r + 2 * e + fx].at[k],
                        sem.at[r, len(copies)],
                    )
                )
    return copies


def ff_grad_kernel(
    plan,
    meta,
    sl_a,
    sl_b,
    cot_a,
    cot_b,
    act_a,
    act_b,
    hg_a,
    hg_b,
    *rest,
):
    *outs, left, buf, sem = rest
    step = pl.program_id(0)
    count = sl_a.shape[0]

    @pl.when(step == 0)
    def _():
        left[0, :, :count] = sl_a[...].T
        left[0, :, count:] = sl_b[...].T
        left[1, :, :count] = cot_a[...].T
        left[1, :, count:] = cot_b[...].T

    wide = plan.part // 2
    for r in range(2):

        @pl.when(step == r)
        def _():
            for e, (one, two) in enumerate(((hg_a, hg_b), (act_a, act_b))):
                for n in range(2):
                    at = slice(n * wide, (n + 1) * wide)
                    got = mm(left[e, :, :count], one[0, :, at])
                    got = got + mm(left[e, :, count:], two[0, :, at])
                    buf[r, e, :, at] = got.astype(bf16)
            for copy in ff_grad_copies(plan, meta, buf, outs, sem, r):
                copy.start()

    @pl.when(step == 1)
    def _():
        for r in range(2):
            for copy in ff_grad_copies(plan, meta, buf, outs, sem, r):
                copy.wait()


def attn_bwd_kernel(
    plan,
    meta,
    sga_ref,
    sgb_ref,
    mid_ref,
    cot_ref,
    np_ref,
    qkv_ref,
    p_ref,
    w_a,
    w_b,
    w_c,
    w_d,
    dqkv_ref,
    ml_ref,
    mg_ref,
    vec_ref,
    pair_ref,
    w,
    sem,
):
    cols = plan.cols
    first = pl.program_id(0) == 0
    lanes = slice(3 * cols, 4 * cols)
    srcs = (w_a, w_b, w_c, w_d)

    @pl.when(first)
    def _():
        for copy in attn_weight_copies(plan, meta, srcs, w, sem, lanes):
            copy.start()
        vec_ref[...] = jnp.zeros_like(vec_ref)
        pair_ref[...] = jnp.zeros_like(pair_ref)

    sg = sga_ref[...].astype(f32) + sgb_ref[...].astype(f32)
    cot = cot_ref[...].astype(f32)
    normal, scaled = norm_stats(mid_ref[...])
    mg = cot + norm_backward(sg, normal, scaled, np_ref[2:3, :])
    mg_ref[...] = mg
    ml = mg.astype(bf16)
    ml_ref[...] = ml
    vec_ref[0:1, :] += jnp.sum(sg * normal, axis=0, keepdims=True)
    vec_ref[1:2, :] += jnp.sum(sg, axis=0, keepdims=True)
    vec_ref[2:3, :] += jnp.sum(mg, axis=0, keepdims=True)
    vec_ref[3:4, :] += jnp.sum(cot, axis=0, keepdims=True)

    @pl.when(first)
    def _():
        for copy in attn_weight_copies(plan, meta, srcs, w, sem, lanes):
            copy.wait()

    tiles = ml.shape[0] // LANES
    pairs = cols // LANES
    for y in range(2):
        dctx = mm(ml, w[y]).astype(bf16)
        for t in range(tiles):
            tok = slice(t * LANES, (t + 1) * LANES)
            for p in range(pairs):
                at = [slice(b * cols + p * LANES, b * cols + (p + 1) * LANES) for b in range(3)]
                dcs = split_heads(dctx[tok, p * LANES : (p + 1) * LANES])
                qs = split_heads(qkv_ref[y, tok, at[0]])
                low = p_ref[(t * 2 + y) * pairs + p]
                probs = low.astype(f32)
                dp = mm_nt(dcs, qkv_ref[y, tok, at[2]])
                inner = jnp.sum(dp * probs, axis=-1, keepdims=True)
                ds = (probs * (dp - inner) * HD**-0.5).astype(bf16)
                dq = join_heads(mm(ds, qkv_ref[y, tok, at[1]])).astype(bf16)
                dk = mm_tn(ds, qs).astype(bf16)
                dv = mm_tn(low, dcs).astype(bf16)
                dqkv_ref[y, tok, at[0]] = dq
                dqkv_ref[y, tok, at[1]] = dk
                dqkv_ref[y, tok, at[2]] = dv
        for b in (0, 2):
            at = slice(b * cols, (b + 1) * cols)
            pair_ref[b // 2 : b // 2 + 1, y * cols : (y + 1) * cols] += jnp.sum(
                dqkv_ref[y, :, at].astype(f32), axis=0, keepdims=True
            )


def attn_grad_copies(plan, meta, buf, outs, sem, fy):
    if not plan.direct:
        yy = jnp.bitwise_xor(meta[3], fy)
        return [pltpu.make_async_copy(buf.at[fy], outs[0].at[yy], sem.at[fy, 0])]
    copies = []
    for r in range(2):
        for fx in range(2):
            for k in range(plan.nz):
                cc, zz, xx, _ = piece_spot(plan, meta, r, fy, fx, k, 1)
                s1 = jnp.where(cc == 0, fx, fy)
                s2 = jnp.where(cc == 0, fy, fx)
                row = pl.multiple_of((zz * 2 + xx) * plan.rows + cc * plan.half, 16)
                copies.append(
                    pltpu.make_async_copy(
                        buf.at[fy, pl.ds(row, plan.half), :],
                        outs[r * plan.nz + k].at[s2, s1],
                        sem.at[fy, len(copies)],
                    )
                )
    return copies


def attn_grad_kernel(plan, meta, fl_ref, ml_ref, dqkv_ref, ctx_ref, *rest):
    *outs, left, buf, sem = rest
    step = pl.program_id(0)
    cols = plan.cols

    @pl.when(step == 0)
    def _():
        left[0] = fl_ref[...].T
        left[1] = ml_ref[...].T

    for fy in range(2):

        @pl.when(step == fy)
        def _():
            for b in range(3):
                at = slice(b * cols, (b + 1) * cols)
                buf[fy, :, at] = mm(left[0], dqkv_ref[0, :, at]).astype(bf16)
            buf[fy, :, 3 * cols :] = mm(left[1], ctx_ref[...]).astype(bf16)
            for copy in attn_grad_copies(plan, meta, buf, outs, sem, fy):
                copy.start()

    @pl.when(step == 1)
    def _():
        for fy in range(2):
            for copy in attn_grad_copies(plan, meta, buf, outs, sem, fy):
                copy.wait()


def input_grad_kernel(
    plan, meta, x_ref, mg_ref, np_ref, dqkv_ref, w_a, w_b, w_c, w_d, ig_ref, vec_ref, w, sem
):
    cols = plan.cols
    first = pl.program_id(0) == 0
    lanes = slice(0, 3 * cols)
    srcs = (w_a, w_b, w_c, w_d)

    @pl.when(first)
    def _():
        for copy in attn_weight_copies(plan, meta, srcs, w, sem, lanes):
            copy.start()
        vec_ref[...] = jnp.zeros_like(vec_ref)

    normal, scaled = norm_stats(x_ref[...].astype(f32))

    @pl.when(first)
    def _():
        for copy in attn_weight_copies(plan, meta, srcs, w, sem, lanes):
            copy.wait()

    fg = mm_nt(dqkv_ref[0], w[0]) + mm_nt(dqkv_ref[1], w[1])
    vec_ref[0:1, :] += jnp.sum(fg * normal, axis=0, keepdims=True)
    vec_ref[1:2, :] += jnp.sum(fg, axis=0, keepdims=True)
    ig = mg_ref[...] + norm_backward(fg, normal, scaled, np_ref[0:1, :])
    ig_ref[...] = ig.astype(bf16)


def add_kernel(meta, left, right, *outs):
    for i, out in enumerate(outs):
        out[...] = (left[i].astype(f32) + right[i].astype(f32)).astype(out.dtype)


def add_parts(meta, left, right):
    n, size = left.shape[0], left.shape[-1]
    shape = left.shape[1:]
    left, right = left.reshape(n, -1, size), right.reshape(n, -1, size)
    length = left.shape[1]
    blocks = 4 if length % 64 == 0 and length >= 384 else 1
    step = length // blocks
    outs = call(
        add_kernel,
        "add_parts",
        (blocks,),
        [(v, (n, step, size), lambda i, m: (0, i, 0)) for v in (left, right)],
        [(jax.ShapeDtypeStruct((length, size), bf16), (step, size), lambda i, m: (i, 0))] * n,
        [],
        vmem=24,
    )(meta, left, right)
    return [v.reshape(shape) for v in outs]


def sums_kernel(meta, *refs):
    n = len(refs) // 3
    for left, right, out in zip(refs[:n], refs[n : 2 * n], refs[2 * n :]):
        out[...] = (left[...].astype(f32) + right[...].astype(f32)).astype(out.dtype)


def add_lists(meta, left, right):
    n, shape = len(left), left[0].shape
    flat = [v.reshape(-1, shape[-1]) for v in (*left, *right)]
    length, size = flat[0].shape
    blocks = 2 if length % 32 == 0 and length >= 384 else 1
    block = ((length // blocks, size), lambda i, m: (i, 0))
    outs = call(
        sums_kernel,
        "add_lists",
        (blocks,),
        [(v, *block) for v in flat],
        [(jax.ShapeDtypeStruct((length, size), bf16), *block)] * n,
        [],
    )(meta, *flat)
    return [v.reshape(shape) for v in outs]


def first_kernel(meta, *refs):
    n = (len(refs) - 2) // 2
    for k in range(n):
        for s in range(2):
            total = refs[k][s].astype(f32) + refs[n + k][s].astype(f32)
            refs[2 * n + s][:, k] = total.astype(bf16)


def add_first(meta, left, right):
    shape = left[0].shape[1:]
    row = 16 if shape[1] % 16 == 0 else shape[1]
    grid = (shape[0], shape[1] // row)
    block = (2, 1, row, shape[2])
    out = (shape[0], len(left), *shape[1:])
    out_block = (1, len(left), row, shape[2])
    return call(
        first_kernel,
        "add_first",
        grid,
        [(v, block, lambda i, j, m: (0, i, j, 0)) for v in (*left, *right)],
        [(jax.ShapeDtypeStruct(out, bf16), out_block, lambda i, j, m: (i, 0, j, 0))] * 2,
        [],
    )(meta, *left, *right)


def by_z_kernel(meta, a, b, c, d, *outs):
    for k, out in enumerate(outs):
        out[0] = (a[k].astype(f32) + b[k].astype(f32)).astype(out.dtype)
        out[1] = (c[k].astype(f32) + d[k].astype(f32)).astype(out.dtype)


def add_by_z(meta, a, b, c, d):
    shape = (2, *a.shape[1:])
    full = (a.shape, lambda i, m: (0, 0, 0))
    return call(
        by_z_kernel,
        "add_by_z",
        (1,),
        [(v, *full) for v in (a, b, c, d)],
        [(jax.ShapeDtypeStruct(shape, bf16), shape, lambda i, m: (0, 0, 0))] * a.shape[0],
        [],
    )(meta, a, b, c, d)


def total_kernel(meta, *refs):
    *parts, ff_square, local, keep, send, payload = refs
    total = parts[0][...].astype(f32)
    for part in parts[1:]:
        total = total + part[...].astype(f32)
    quarter = total.shape[1] // 8
    for core in range(2):
        for out, c in ((keep, core), (send, 1 - core)):

            @pl.when(meta[4] == core)
            def _():
                for b in range(4):
                    at = (2 * b + c) * quarter
                    out[:, b * quarter : (b + 1) * quarter] = total[:, at : at + quarter]

    square = jnp.sum(total * total) + jnp.sum(ff_square[...]) + jnp.sum(local[...] * local[...])
    size = local.shape[1]
    count = payload.shape[0]
    payload[:, :, :size] = jnp.broadcast_to(local[...][None], (count, 1, size))
    payload[:, :, size:] = jnp.full((count, 1, LANES), square, f32)


def out_kernel(meta, pre_a, fed_a, pre_b, fed_b, np_ref, out_a, out_b):
    for pre, fed, out in ((pre_a, fed_a, out_a), (pre_b, fed_b, out_b)):
        total = pre[...].astype(f32) + fed[...].astype(f32) + np_ref[5:6, :]
        out[...] = total.astype(bf16)


def place_kernel(meta, own, by_y, by_c, by_yc, out, sem):
    count = own.shape[0]
    copies = []
    for fy, fc, src in ((0, 0, own), (1, 0, by_y), (0, 1, by_c), (1, 1, by_yc)):
        at = jnp.bitwise_xor(meta[3], fy) * 2 + jnp.bitwise_xor(meta[4], fc)
        dst = out.at[pl.ds(pl.multiple_of(at * count, 16), count), :]
        copies.append(pltpu.make_async_copy(src, dst, sem.at[len(copies)]))
    for copy in copies:
        copy.start()
    for copy in copies:
        copy.wait()


def adam_kernel(plan, rates, meta, got, *refs):
    per = got.shape[2] // LANES - 1
    total = jnp.sum(got[:, 0, per * LANES :], axis=0, keepdims=True)[:, 0:1]
    norm = jnp.sqrt(total)
    refs[-1][...] = norm
    factor = jnp.minimum(1.0, CLIP / norm)
    correction = 1.0 - BETA**STEP
    width, quarter, part = plan.width, plan.width // 4, plan.part

    def line(start, length):
        spots = range(start // LANES, (start + length) // LANES)
        return jnp.concatenate(
            [got[b // per, :, b % per * LANES : (b % per + 1) * LANES] for b in spots],
            axis=1,
        )

    def owned(pick):
        value = pick(0)
        for m in range(1, 4):
            value = jnp.where(meta[0] == m, pick(m), value)
        return value

    pairs = [line((6 + i) * width, width) for i in range(2)]
    small = (
        jnp.concatenate([line(i * width, width) for i in range(6)], axis=0),
        jnp.concatenate(
            [owned(lambda m: v[:, m * quarter : (m + 1) * quarter]) for v in pairs], axis=0
        ),
        owned(lambda m: line(8 * width + m * part, part)),
    )
    ins, outs = refs[: 4 * 4 + 3 * 3], refs[4 * 4 + 3 * 3 : -1]
    for i, (rate, decay) in enumerate(rates):
        if i < 4:
            w_ref, m_ref, s_ref, g_ref = ins[4 * i : 4 * i + 4]
        else:
            w_ref, m_ref, s_ref = ins[3 * i + 4 : 3 * i + 7]
            g_ref = {Ellipsis: small[i - 4]}
        m_out, s_out, w_out = outs[3 * i : 3 * i + 3]
        planes = range(w_ref.shape[0]) if len(w_ref.shape) == 3 else (Ellipsis,)
        for p in planes:
            clipped = g_ref[p] * factor
            shape = w_ref[p].shape
            weight, first, second = (
                v[p].reshape(clipped.shape) for v in (w_ref, m_ref, s_ref)
            )
            first = BETA * first + (1.0 - BETA) * clipped
            second = BETA * second + (1.0 - BETA) * clipped * clipped
            direction = first / correction / (jnp.sqrt(second / correction) + ADAM_EPS)
            m_out[p] = first.reshape(shape)
            s_out[p] = second.reshape(shape)
            w_out[p] = (weight - rate * (direction + decay * weight)).reshape(shape)


def after(value, *others):
    return lax.optimization_barrier((value, *others))[0]


def any_spec():
    return pl.BlockSpec(memory_space=pl.ANY)


def call(kernel, name, grid, ins, outs, scratch, vmem=60):
    def spec(item):
        if item[1] is None:
            return any_spec()
        return pl.BlockSpec(item[1], item[2])

    return pl.pallas_call(
        kernel,
        name=name,
        out_shape=[o[0] for o in outs],
        grid_spec=pltpu.PrefetchScalarGridSpec(
            num_scalar_prefetch=1,
            grid=grid,
            in_specs=[spec(i) for i in ins],
            out_specs=[spec(o) for o in outs],
            scratch_shapes=scratch,
        ),
        compiler_params=pltpu.CompilerParams(vmem_limit_bytes=vmem * MIB),
        cost_estimate=pl.CostEstimate(flops=1, bytes_accessed=1, transcendentals=0),
    )


def per_device(
    inputs,
    segments,
    cotangent,
    triple_weight,
    triple_first,
    triple_second,
    outward_weight,
    outward_first,
    outward_second,
    expand_weight,
    expand_first,
    expand_second,
    reduce_weight,
    reduce_first,
    reduce_second,
    norm_params,
    norm_first,
    norm_second,
    paired_bias,
    paired_first,
    paired_second,
    hidden_bias,
    hidden_first,
    hidden_second,
):
    ndp, nmp = lax.axis_size("dp"), lax.axis_size("mp")
    width = inputs.shape[1]
    hidden = hidden_bias.shape[0] * nmp
    plan = Plan(ndp, nmp, width, hidden)
    nz, rows, half, cols, part = plan.nz, plan.rows, plan.half, plan.cols, plan.part
    count = inputs.shape[0] // nmp
    row_count, row_length = segments.shape
    own_rows = row_count // nmp
    steps = count // CHUNK
    tiles = CHUNK // LANES
    units = tiles * 2 * (cols // LANES)
    quarter = cols // 2

    dp, mp = lax.axis_index("dp"), lax.axis_index("mp")
    z, x, y, c = dp // 2, dp % 2, mp // 2, mp % 2
    meta = jnp.stack([mp, z, x, y, c, jnp.bitwise_xor(mp, 2)]).astype(jnp.int32)
    core_zero = c == 0
    SDS = jax.ShapeDtypeStruct

    shard = jnp.concatenate(
        [triple_weight.astype(bf16), outward_weight.T.astype(bf16)[None]], axis=0
    ).transpose(1, 0, 2)
    keep = lax.dynamic_slice_in_dim(shard, c * half, half, 0)
    send = lax.dynamic_slice_in_dim(shard, (1 - c) * half, half, 0)
    got = plan.core(send)
    low = jnp.where(core_zero, keep, got)
    high = jnp.where(core_zero, got, keep)
    unit = jnp.concatenate([low, high], axis=2).reshape(half, 4 * cols)
    attn_z = [plan.along_z(unit, k) for k in range(1, nz)]

    e_unit = after(expand_weight.astype(bf16), unit)
    e_z = [plan.along_z(e_unit, k) for k in range(1, nz)]
    r_unit = after(reduce_weight.T.astype(bf16), e_z[0])
    r_z = [plan.along_z(r_unit, k) for k in range(1, nz)]

    biases = jnp.concatenate([paired_bias.reshape(-1), hidden_bias])
    by_core = plan.core(after(biases, attn_z[0]))
    other_pair = by_core[: 2 * quarter].reshape(2, quarter)
    near = jnp.where(
        core_zero,
        jnp.concatenate([paired_bias, other_pair], axis=1),
        jnp.concatenate([other_pair, paired_bias], axis=1),
    )
    far = plan.along_y(near)
    pair_full = jnp.where(
        y == 0, jnp.concatenate([near, far], axis=1), jnp.concatenate([far, near], axis=1)
    )
    hidden_rows = jnp.stack([hidden_bias, by_core[2 * quarter :]])

    marks = lax.dynamic_slice_in_dim(segments, mp * own_rows, own_rows, 0)
    marks = marks + row_length * lax.broadcasted_iota(jnp.int32, marks.shape, 0)
    mark_col = marks.reshape(count, 1)
    mark_row = marks.reshape(steps, tiles, LANES)

    spread = after(jnp.stack([unit] + attn_z), e_z[0])
    spread = jnp.stack([spread, plan.first(spread)])
    spread, *_, meta, mark_col, mark_row, pair_full, hidden_rows = lax.optimization_barrier(
        (spread, *e_z[1:], meta, mark_col, mark_row, pair_full, hidden_rows)
    )
    e_spread = jnp.stack([e_unit] + e_z)
    e_x = plan.along_x(e_spread)
    attn_w = [spread, after(plan.second(spread), *r_z, e_x)]
    r_spread = jnp.stack([r_unit] + r_z)
    r_x = plan.along_x(r_spread)
    attn_w = attn_w + [plan.core(v) for v in attn_w]
    attn_w[1] = after(attn_w[1], e_spread, r_spread)

    if not plan.direct:
        attn_w = [absolute_attn(plan, jnp.stack(attn_w[:2]), jnp.stack(attn_w[2:]), z, x, y, c)]
        attn_w = attn_w + [meta] * 3

    whole = lambda shape: (shape, lambda i, m: (0,) * len(shape))
    chunk = lambda n: ((CHUNK, n), lambda i, m: (i, 0))
    mine_rows = ((CHUNK, width), lambda i, m: (m[0] * steps + i, 0))
    pair_rows = ((CHUNK, width), lambda i, m: (m[5] * steps + i, 0))
    pieces = 2 * 2 * 2 * nz if plan.direct else 1
    dma = pltpu.SemaphoreType.DMA
    qkv_block = ((2, CHUNK, 3 * cols), lambda i, m: (0, i, 0))
    p_block = ((units, 2 * LANES, LANES), lambda i, m: (i, 0, 0))

    sl, middle, fl, qkv, probs, ctx = call(
        functools.partial(attn_fwd_kernel, plan),
        "attn_fwd",
        (steps,),
        [
            (inputs, *mine_rows),
            (mark_col, *chunk(1)),
            (mark_row, (1, tiles, LANES), lambda i, m: (i, 0, 0)),
            (norm_params, *whole(norm_params.shape)),
            (pair_full, *whole(pair_full.shape)),
            *[(v, None, None) for v in attn_w],
        ],
        [
            (SDS((count, width), bf16), *chunk(width)),
            (SDS((count, width), f32), *chunk(width)),
            (SDS((count, width), bf16), *chunk(width)),
            (SDS((2, count, 3 * cols), bf16), *qkv_block),
            (SDS((steps * units, 2 * LANES, LANES), bf16), *p_block),
            (SDS((count, width), bf16), *chunk(width)),
        ],
        [pltpu.VMEM((2, width, 4 * cols), bf16), dma((pieces,))],
    )(meta, inputs, mark_col, mark_row, norm_params, pair_full, *attn_w)

    sl_far = plan.along_y(sl)
    e_x, r_x = after(e_x, sl), after(r_x, sl)
    ff_w = []
    for near, far in ((e_spread, e_x), (r_spread, r_x)):
        pieces_of = [near, far, plan.core(near), plan.core(far)]
        if not plan.direct:
            pairs = (pieces_of[:2], pieces_of[2:])
            pieces_of = [v for p in pairs for v in (absolute_ff(plan, jnp.stack(p), z, x), meta)]
        ff_w = ff_w + pieces_of

    def feed_forward(sl_in, cot_rows, sg_type, base):
        return call(
            functools.partial(ff_kernel, plan, len(base) > 0),
            "feed_forward",
            (steps,),
            [
                (sl_in, *chunk(width)),
                (cotangent, *cot_rows),
                (hidden_rows, *whole(hidden_rows.shape)),
                *[(v, None, None) for v in ff_w],
                *[(v, *chunk(width)) for v in base],
            ],
            [
                (SDS((count, width), sg_type), *chunk(width)),
                (SDS((count, width), bf16), *chunk(width)),
                (SDS((2, count, part), bf16), (2, CHUNK, part), lambda i, m: (0, i, 0)),
                (SDS((2, count, part), bf16), (2, CHUNK, part), lambda i, m: (0, i, 0)),
                (SDS((2, part), f32), *whole((2, part))),
            ],
            [
                pltpu.VMEM((2, 2, width, part), bf16),
                dma((2, 2, 2 * nz if plan.direct else 1)),
            ],
        )(meta, sl_in, cotangent, hidden_rows, *ff_w, *base)

    sg_near, pre_near, act_near, hg_near, gh_near = feed_forward(sl, mine_rows, f32, [middle])
    sl_far = after(sl_far, sg_near)
    sg_send, fed_send, act_far, hg_far, gh_far = feed_forward(sl_far, pair_rows, bf16, [])
    pre_far = plan.along_y(pre_near)
    sg_far = plan.along_y(after(sg_send, pre_far))

    half_block = ((1, count, part), lambda i, m: (i, 0, 0))
    all_mine = ((count, width), lambda i, m: (m[0], 0))
    all_pair = ((count, width), lambda i, m: (m[5], 0))
    if plan.direct:
        grad_shapes = [SDS((nz, rows, part), bf16)] * 8
    else:
        grad_shapes = [SDS((width, part), bf16)] * 4
    ff_grads = call(
        functools.partial(ff_grad_kernel, plan),
        "ff_grad",
        (2,),
        [
            (sl, *whole((count, width))),
            (sl_far, *whole((count, width))),
            (cotangent, *all_mine),
            (cotangent, *all_pair),
            (act_near, *half_block),
            (act_far, *half_block),
            (hg_near, *half_block),
            (hg_far, *half_block),
        ],
        [(v, None, None) for v in grad_shapes],
        [
            pltpu.VMEM((2, width, 2 * count), bf16),
            pltpu.VMEM((2, 2, width, part), bf16),
            dma((2, 4 * nz if plan.direct else 2)),
        ],
    )(meta, sl, sl_far, cotangent, cotangent, act_near, act_far, hg_near, hg_far)
    if not plan.direct:
        ff_grads = [v for g in ff_grads for v in relative_ff(plan, g, z, x)]

    e_keep, e_send, r_keep, r_send = add_lists(
        meta, ff_grads[:4], [plan.core(v) for v in ff_grads[4:]]
    )
    sg_far = after(sg_far, e_send, r_send)
    e_send, r_send, fed_send = lax.optimization_barrier((e_send, r_send, fed_send, sg_far))[:3]
    e_got, r_got = plan.along_x(e_send), plan.along_x(r_send)
    fed_far = plan.along_y(fed_send)

    dqkv, ml, mg, vec_two, pair_sum = call(
        functools.partial(attn_bwd_kernel, plan),
        "attn_bwd",
        (steps,),
        [
            (sg_near, *chunk(width)),
            (sg_far, *chunk(width)),
            (middle, *chunk(width)),
            (cotangent, *mine_rows),
            (norm_params, *whole(norm_params.shape)),
            (qkv, *qkv_block),
            (probs, *p_block),
            *[(v, None, None) for v in attn_w],
        ],
        [
            (SDS((2, count, 3 * cols), bf16), *qkv_block),
            (SDS((count, width), bf16), *chunk(width)),
            (SDS((count, width), f32), *chunk(width)),
            (SDS((8, width), f32), *whole((8, width))),
            (SDS((2, width), f32), *whole((2, width))),
        ],
        [pltpu.VMEM((2, width, cols), bf16), dma((pieces,))],
    )(meta, sg_near, sg_far, middle, cotangent, norm_params, qkv, probs, *attn_w)

    if plan.direct:
        grad_shapes = [SDS((2, 2, half, 4 * cols), bf16)] * (2 * nz)
    else:
        grad_shapes = [SDS((2, width, 4 * cols), bf16)]
    ml = after(ml, e_got)
    attn_grads = call(
        functools.partial(attn_grad_kernel, plan),
        "attn_grad",
        (2,),
        [
            (fl, *whole((count, width))),
            (ml, *whole((count, width))),
            (dqkv, (1, count, 3 * cols), lambda i, m: (jnp.bitwise_xor(m[3], i), 0, 0)),
            (ctx, (count, cols), lambda i, m: (0, jnp.bitwise_xor(m[3], i))),
        ],
        [(s, None, None) for s in grad_shapes],
        [
            pltpu.VMEM((2, width, count), bf16),
            pltpu.VMEM((2, width, 4 * cols), bf16),
            dma((2, 4 * nz if plan.direct else 1)),
        ],
    )(meta, fl, ml, dqkv, ctx)
    if not plan.direct:
        both = relative_attn(plan, attn_grads[0], z, x, y, c)
        attn_grads = [v[:, :, k] for v in both for k in range(nz)]
    attn_mine, attn_theirs = list(attn_grads[:nz]), list(attn_grads[nz:])
    attn_theirs[0] = after(attn_theirs[0], r_got, fed_far)
    attn_got = [plan.core(v) for v in attn_theirs]

    ff_parts = add_by_z(meta, e_keep, e_got, r_keep, after(r_got, attn_theirs[0]))

    attn_got[0] = after(attn_got[0], *ff_parts)
    attn_keep, attn_send = add_first(meta, attn_mine, attn_got)
    attn_got = plan.second(attn_send)
    ff_parts = [after(v, attn_send) for v in ff_parts]
    ff_z = [plan.along_z(ff_parts[k], k) for k in range(1, nz)]
    dqkv_late = after(dqkv, attn_send)
    ig, vec_one = call(
        functools.partial(input_grad_kernel, plan),
        "input_grad",
        (steps,),
        [
            (inputs, *mine_rows),
            (mg, *chunk(width)),
            (norm_params, *whole(norm_params.shape)),
            (dqkv, *qkv_block),
            *[(v, None, None) for v in attn_w],
        ],
        [
            (SDS((count, width), bf16), *chunk(width)),
            (SDS((8, width), f32), *whole((8, width))),
        ],
        [pltpu.VMEM((2, width, 3 * cols), bf16), dma((pieces,))],
    )(meta, inputs, mg, norm_params, dqkv_late, *attn_w)
    attn_got = after(attn_got, ig, *(ff_z[:1] + ff_z[2:]))
    attn_keep, attn_send = add_parts(meta, attn_keep, attn_got)
    attn_got = plan.first(attn_send)

    gh = gh_near + gh_far
    gh = jnp.where(core_zero, gh, gh[::-1]).reshape(-1)
    zero = jnp.zeros_like(gh)
    gh = jnp.where(y == 0, jnp.concatenate([gh, zero]), jnp.concatenate([zero, gh]))
    vectors = jnp.concatenate(
        [vec_one[:2].reshape(-1), vec_two[:4].reshape(-1), pair_sum.reshape(-1), gh]
    )
    size = -(-vectors.shape[0] // (LANES * plan.ndev)) * LANES
    vectors = jnp.pad(vectors, (0, size * plan.ndev - vectors.shape[0]))
    got = lax.all_to_all(vectors.reshape(plan.ndev, size), AXES, 0, 0, tiled=True)
    local = jnp.sum(got, axis=0, keepdims=True)

    ff_grads = ff_parts[0].astype(f32)
    for part_z in ff_z:
        ff_grads = ff_grads + part_z.astype(f32)
    ff_square = jnp.sum(ff_grads * ff_grads).reshape(1, 1)

    attn_parts = add_parts(meta, attn_keep, after(attn_got, local, ff_square))

    pre_in = after(pre_near, attn_parts[0])
    out, out_pair = call(
        out_kernel,
        "out_sum",
        (steps,),
        [
            (pre_in, *chunk(width)),
            (fed_far, *chunk(width)),
            (pre_far, *chunk(width)),
            (fed_send, *chunk(width)),
            (norm_params, *whole(norm_params.shape)),
        ],
        [(SDS((count, width), bf16), *chunk(width))] * 2,
        [],
    )(meta, pre_in, fed_far, pre_far, fed_send, norm_params)
    ig = after(ig, attn_parts[0])
    ig_pair = plan.along_y(ig)
    attn_z = [attn_parts[0]] + [plan.along_z(attn_parts[k], k) for k in range(1, nz)]
    total_in = attn_z + [ff_square, local]
    def everywhere(block, by_y):
        blocks = [block, by_y, plan.core(block), plan.core(by_y)]
        return call(
            place_kernel,
            "place",
            (1,),
            [(b, *whole((count, width))) for b in blocks],
            [(SDS((count * nmp, width), bf16), None, None)],
            [dma((4,))],
        )(meta, *blocks)[0]

    outputs = everywhere(out, out_pair)
    total_in[-1] = after(total_in[-1], outputs)
    keep, send, payload = call(
        total_kernel,
        "total",
        (1,),
        [(v, *whole(v.shape)) for v in total_in],
        [
            (SDS((half, 2 * cols), f32), *whole((half, 2 * cols))),
            (SDS((half, 2 * cols), f32), *whole((half, 2 * cols))),
            (
                SDS((plan.ndev, 1, size + LANES), f32),
                *whole((plan.ndev, 1, size + LANES)),
            ),
        ],
        [],
    )(meta, *total_in)
    by_core = plan.core(send)
    ig_pair = after(ig_pair, keep)
    input_gradient = everywhere(ig, ig_pair)
    got = after(lax.all_to_all(payload, AXES, 0, 0, tiled=True), input_gradient)

    low, high = jnp.where(core_zero, keep, by_core), jnp.where(core_zero, by_core, keep)
    shard = jnp.concatenate([low, high], axis=0).reshape(rows, 4, quarter)
    grad_triple = shard[:, :3].transpose(1, 0, 2)
    grad_outward = shard[:, 3].T

    matrix, vector = (LR_MATRIX, DECAY), (LR_VECTOR, 0.0)
    groups = [
        [triple_weight, triple_first, triple_second, grad_triple],
        [outward_weight, outward_first, outward_second, grad_outward],
        [expand_weight, expand_first, expand_second, ff_grads[0]],
        [reduce_weight.T, reduce_first.T, reduce_second.T, ff_grads[1]],
        [norm_params, norm_first, norm_second],
        [paired_bias, paired_first, paired_second],
        [hidden_bias, hidden_first, hidden_second],
    ]
    flat = [got] + [v for group in groups for v in group]
    new_shapes = [SDS(group[0].shape, f32) for group in groups for _ in range(3)]
    new_shapes.append(SDS((1, 1), f32))
    new = call(
        functools.partial(adam_kernel, plan, (matrix,) * 4 + (vector,) * 3),
        "adam",
        (1,),
        [(v, *whole(v.shape)) for v in flat],
        [(s, *whole(s.shape)) for s in new_shapes],
        [],
    )(meta, *flat)
    new = list(new)
    gradient_norm = new.pop().reshape(())
    new[9:12] = [v.T for v in new[9:12]]
    return (outputs, input_gradient, gradient_norm, *new)


def turn(plan, value, z, axis):
    value = jnp.flip(value, axis)
    return jnp.roll(value, z + 1, axis)


def unturn(plan, value, z, axis):
    return jnp.roll(value, -z, axis)


def swap(value, flag, axis):
    return jnp.where(flag == 1, jnp.flip(value, axis), value)


def absolute_ff(plan, value, z, x):
    value = swap(turn(plan, value, z, 1), x, 0)
    return value.transpose(1, 0, 2, 3).reshape(plan.width, plan.part)


def relative_ff(plan, value, z, x):
    value = value.reshape(plan.nz, 2, plan.rows, plan.part).transpose(1, 0, 2, 3)
    value = unturn(plan, swap(value, x, 0), z, 1)
    return value[0], value[1]


def absolute_attn(plan, own, other, z, x, y, c):
    zero = jnp.where(c == 0, own, other)
    one = jnp.where(c == 0, other, own).transpose(1, 0, 2, 3, 4)
    value = jnp.stack([zero, one])
    value = turn(plan, swap(swap(value, y, 1), x, 2), z, 3)
    value = value.transpose(1, 3, 2, 0, 4, 5)
    return value.reshape(2, plan.width, 4 * plan.cols)


def relative_attn(plan, value, z, x, y, c):
    value = value.reshape(2, plan.nz, 2, 2, plan.half, 4 * plan.cols)
    value = value.transpose(3, 0, 2, 1, 4, 5)
    value = unturn(plan, swap(swap(value, y, 1), x, 2), z, 3)
    zero, one = value[0], value[1].transpose(1, 0, 2, 3, 4)
    return jnp.where(c == 0, zero, one), jnp.where(c == 0, one, zero)


def solution(mesh):
    tokens = P("dp", None)
    triple = P(None, "dp", "mp")
    tall = P("mp", "dp")
    wide = P("dp", "mp")
    pair = P(None, "mp")
    states = ((triple,) * 3, (tall,) * 3, (wide,) * 3, (tall,) * 3, (P(),) * 3, (pair,) * 3)
    states = sum(states, ()) + (P("mp"),) * 3
    return jax.shard_map(
        per_device,
        mesh=mesh,
        in_specs=(tokens,) * 3 + states,
        out_specs=(tokens, tokens, P()) + states,
        check_vma=False,
    )
```

```python
import functools

import jax
import jax.numpy as jnp
from jax import lax
from jax.experimental import pallas as pl
from jax.experimental.pallas import tpu as pltpu
from jax.sharding import PartitionSpec as P

HD = 64
STEP = 5
EPS_NORM = 1e-06
BETA = 0.5
LR_MATRIX = 0.03
LR_VECTOR = 0.2
DECAY = 0.1
ADAM_EPS = 1e-08
CLIP = 1.0
NEG = -1e30
GELU_C = 0.7978845608028654
GELU_K = 0.044715

f32 = jnp.float32
bf16 = jnp.bfloat16
AXES = ("dp", "mp")
LANES = 128
CHUNK = 256
MIB = 1 << 20


def mm(left, right):
    return lax.dot_general(left, right, (((1,), (0,)), ((), ())), preferred_element_type=f32)


def mm_nt(left, right):
    return lax.dot_general(left, right, (((1,), (1,)), ((), ())), preferred_element_type=f32)


def mm_tn(left, right):
    return lax.dot_general(left, right, (((0,), (0,)), ((), ())), preferred_element_type=f32)


def norm_stats(rows_in):
    centred = rows_in - jnp.mean(rows_in, axis=-1, keepdims=True)
    scaled = lax.rsqrt(jnp.mean(centred * centred, axis=-1, keepdims=True) + EPS_NORM)
    return centred * scaled, scaled


def norm_backward(upstream, normal_rows, scaled, gain_row):
    gained = upstream * gain_row
    mean_one = jnp.mean(gained, axis=-1, keepdims=True)
    mean_two = jnp.mean(gained * normal_rows, axis=-1, keepdims=True)
    return scaled * (gained - mean_one - normal_rows * mean_two)


def lane_low(shape):
    return lax.broadcasted_iota(jnp.int32, shape, 1) % LANES < HD


def split_heads(block):
    low = lane_low(block.shape)
    zero = jnp.zeros_like(block)
    return jnp.concatenate([jnp.where(low, block, zero), jnp.where(low, zero, block)], axis=0)


def join_heads(stacked):
    half = stacked.shape[0] // 2
    low = lane_low((half, stacked.shape[1]))
    return jnp.where(low, stacked[:half], stacked[half:])


class Plan:
    def __init__(self, ndp, nmp, width, hidden):
        assert ndp % 2 == 0 and nmp == 4
        self.ndev = ndp * nmp
        self.nz = ndp // 2
        self.rows = width // ndp
        self.half = self.rows // 2
        self.width = width
        self.cols = width // 2
        self.part = hidden // nmp
        self.direct = self.half % 16 == 0

    def perm(self, move):
        pairs = []
        for z in range(self.nz):
            for x in range(2):
                for y in range(2):
                    for c in range(2):
                        there = move(z, x, y, c)
                        pairs.append((self.index(z, x, y, c), self.index(*there)))
        return pairs

    def index(self, z, x, y, c):
        return (2 * z + x) * 4 + 2 * y + c

    def core(self, value):
        return lax.ppermute(value, AXES, self.perm(lambda z, x, y, c: (z, x, y, 1 - c)))

    def along_x(self, value):
        return lax.ppermute(value, AXES, self.perm(lambda z, x, y, c: (z, 1 - x, y, c)))

    def along_y(self, value):
        return lax.ppermute(value, AXES, self.perm(lambda z, x, y, c: (z, x, 1 - y, c)))

    def along_z(self, value, step):
        return lax.ppermute(
            value, AXES, self.perm(lambda z, x, y, c: ((z + step) % self.nz, x, y, c))
        )

    def first(self, value):
        return lax.ppermute(
            value,
            AXES,
            self.perm(lambda z, x, y, c: (z, x, 1 - y, c) if c else (z, 1 - x, y, c)),
        )

    def second(self, value):
        return lax.ppermute(
            value,
            AXES,
            self.perm(lambda z, x, y, c: (z, 1 - x, y, c) if c else (z, x, 1 - y, c)),
        )


def piece_spot(plan, meta, r, fy, fx, k, sign):
    z, x, y, c = meta[1], meta[2], meta[3], meta[4]
    cc = jnp.bitwise_xor(c, r)
    zz = lax.rem(z + sign * k + plan.nz, plan.nz)
    xx = jnp.bitwise_xor(x, fx)
    yy = jnp.bitwise_xor(y, fy)
    return cc, zz, xx, yy


def attn_weight_copies(plan, meta, srcs, w, sem, lanes):
    if not plan.direct:
        return [pltpu.make_async_copy(srcs[0].at[:, :, lanes], w, sem.at[0])]
    copies = []
    for s2 in range(2):
        for r in range(2):
            for s1 in range(2):
                for k in range(plan.nz):
                    cc = jnp.bitwise_xor(meta[4], r)
                    fx = jnp.where(cc == 0, s1, s2)
                    fy = jnp.where(cc == 0, s2, s1)
                    _, zz, xx, yy = piece_spot(plan, meta, r, fy, fx, k, -1)
                    row = pl.multiple_of((zz * 2 + xx) * plan.rows + cc * plan.half, 16)
                    copies.append(
                        pltpu.make_async_copy(
                            srcs[2 * r + s2].at[s1, k, :, lanes],
                            w.at[yy, pl.ds(row, plan.half), :],
                            sem.at[len(copies)],
                        )
                    )
    return copies


def token_copy(src, block, dst, sem):
    count = dst.shape[0]
    return pltpu.make_async_copy(
        src.at[pl.ds(pl.multiple_of(block * count, 16), count), :], dst, sem
    )


def chunks(count, body):
    def step(i, carry):
        body(i, pl.ds(pl.multiple_of(i * CHUNK, CHUNK), CHUNK))
        return carry

    lax.fori_loop(0, count // CHUNK, step, 0)


def lanes_of(base, b, cols, p):
    return slice(base + b * cols + p * LANES, base + b * cols + (p + 1) * LANES)


def attn_fwd_kernel(plan, meta, x_all, segc_ref, segr_ref, np_ref, pb_ref, *refs):
    srcs, refs = refs[:4], refs[4:]
    sl_ref, mid_ref, fl_ref, qkv_ref, p_ref, ctx_ref, w, sl_buf, x_ref, sem, sem_x = refs
    cols = plan.cols
    count = x_ref.shape[0]
    copies = attn_weight_copies(plan, meta, srcs, w, sem, slice(None))
    load = token_copy(x_all, meta[0], x_ref, sem_x.at[0])
    load.start()
    for copy in copies:
        copy.start()
    load.wait()

    def first(i, at):
        normal, _ = norm_stats(x_ref[at, :].astype(f32))
        fl_ref[at, :] = (normal * np_ref[0:1, :] + np_ref[1:2, :]).astype(bf16)

    chunks(count, first)
    for copy in copies:
        copy.wait()
    tiles = CHUNK // LANES
    pairs = cols // LANES

    def second(i, at):
        for y in range(2):
            for part in range(3):
                lanes = slice(part * cols, (part + 1) * cols)
                got = mm(fl_ref[at, :], w[y, :, lanes])
                if part != 1:
                    got = got + pb_ref[part // 2 : part // 2 + 1, y * cols : (y + 1) * cols]
                qkv_ref[y, at, lanes] = got.astype(bf16)
        for t in range(tiles):
            tile = i * tiles + t
            tok = pl.ds(pl.multiple_of(tile * LANES, LANES), LANES)
            same = segc_ref[tok, :] == segr_ref[pl.ds(tile, 1), :]
            same = jnp.concatenate([same] * (2 * pairs), axis=0)
            for y in range(2):
                s = jnp.concatenate(
                    [
                        mm_nt(
                            split_heads(qkv_ref[y, tok, lanes_of(0, 0, cols, p)]),
                            qkv_ref[y, tok, lanes_of(0, 1, cols, p)],
                        )
                        for p in range(pairs)
                    ],
                    axis=0,
                )
                s = jnp.where(same, s * HD**-0.5, NEG)
                e = jnp.exp(s - jnp.max(s, axis=-1, keepdims=True))
                probs = (e * (1.0 / jnp.sum(e, axis=-1, keepdims=True))).astype(bf16)
                p_ref[tile * 2 + y] = probs
                for p in range(pairs):
                    own = probs[p * 2 * LANES : (p + 1) * 2 * LANES]
                    ctx = join_heads(mm(own, qkv_ref[y, tok, lanes_of(0, 2, cols, p)]))
                    ctx_ref[tok, lanes_of(y * cols, 0, cols, p)] = ctx.astype(bf16)
        attended = mm_nt(ctx_ref[at, 0:cols], w[0, :, 3 * cols :])
        attended = attended + mm_nt(ctx_ref[at, cols:], w[1, :, 3 * cols :])
        middle = x_ref[at, :].astype(f32) + attended + np_ref[4:5, :]
        mid_ref[at, :] = middle
        normal, _ = norm_stats(middle)
        sl = (normal * np_ref[2:3, :] + np_ref[3:4, :]).astype(bf16)
        sl_buf[at, :] = sl
        pltpu.make_async_copy(sl_buf.at[at, :], sl_ref.at[at, :], sem_x.at[i]).start()

    chunks(count, second)
    for i in range(count // CHUNK):
        at = pl.ds(i * CHUNK, CHUNK)
        pltpu.make_async_copy(sl_buf.at[at, :], sl_ref.at[at, :], sem_x.at[i]).wait()


def ff_weight_copies(plan, meta, srcs, w, sem, r, e):
    src = srcs[4 * e + 2 * r : 4 * e + 2 * r + 2]
    if not plan.direct:
        return [pltpu.make_async_copy(src[0], w.at[e, r], sem.at[r, e, 0])]
    copies = []
    for fx in range(2):
        for k in range(plan.nz):
            _, zz, xx, _ = piece_spot(plan, meta, r, 0, fx, k, -1)
            row = pl.multiple_of((zz * 2 + xx) * plan.rows, 16)
            copies.append(
                pltpu.make_async_copy(
                    src[fx].at[k],
                    w.at[e, r, pl.ds(row, plan.rows), :],
                    sem.at[r, e, len(copies)],
                )
            )
    return copies


def ff_kernel(plan, own, meta, sl_ref, cot_all, hb_ref, *refs):
    copies = []
    if own:
        w, mid_ref, sg_ref, fed_ref, act_ref, hg_ref, gh_ref, cot_ref, buf, sem_x = refs
    else:
        *srcs, sg_ref, fed_ref, act_ref, hg_ref, gh_ref, cot_ref, w, sg_buf, buf, sem, sem_x = refs
        for r in range(2):
            for e in range(2):
                copies = copies + ff_weight_copies(plan, meta, srcs, w, sem, r, e)
    for copy in copies:
        copy.start()
    count = cot_ref.shape[0]
    load = token_copy(cot_all, meta[0 if own else 5], cot_ref, sem_x.at[0])
    load.start()
    gh_ref[...] = jnp.zeros_like(gh_ref)
    load.wait()
    for copy in copies:
        copy.wait()

    def body(i, at):
        sl = sl_ref[at, :]
        cot = cot_ref[at, :]
        total = [None, None]
        for r in range(2):
            h = mm(sl, w[0, r]) + hb_ref[r : r + 1, :]
            grown = mm(cot, w[1, r])
            square = h * h
            half = 0.5 * jnp.tanh(h * (GELU_C + (GELU_C * GELU_K) * square)) + 0.5
            act = h * half
            slope = half + (act - act * half) * (2.0 * GELU_C + (6.0 * GELU_C * GELU_K) * square)
            grown = grown * slope
            gh_ref[r : r + 1, :] += jnp.sum(grown, axis=0, keepdims=True)
            act = act.astype(bf16)
            grown = grown.astype(bf16)
            act_ref[r, at, :] = act
            hg_ref[r, at, :] = grown
            for e, left in enumerate((grown, act)):
                got = mm_nt(left, w[e, r])
                total[e] = got if total[e] is None else total[e] + got
        fed = total[1] + mid_ref[at, :] if own else total[1]
        buf[at, :] = fed.astype(bf16)
        pltpu.make_async_copy(buf.at[at, :], fed_ref.at[at, :], sem_x.at[i]).start()
        if own:
            sg_ref[at, :] = total[0].astype(bf16)
        else:
            sg_buf[at, :] = total[0].astype(bf16)
            pltpu.make_async_copy(
                sg_buf.at[at, :], sg_ref.at[at, :], sem_x.at[count // CHUNK + i]
            ).start()

    chunks(count, body)
    for i in range(count // CHUNK):
        at = pl.ds(i * CHUNK, CHUNK)
        pltpu.make_async_copy(buf.at[at, :], fed_ref.at[at, :], sem_x.at[i]).wait()
        if not own:
            pltpu.make_async_copy(
                sg_buf.at[at, :], sg_ref.at[at, :], sem_x.at[count // CHUNK + i]
            ).wait()


def ff_grad_copies(plan, meta, buf, outs, sem, r):
    if not plan.direct:
        return [
            pltpu.make_async_copy(buf.at[r, e], outs[2 * r + e], sem.at[r, e]) for e in range(2)
        ]
    copies = []
    for e in range(2):
        for fx in range(2):
            for k in range(plan.nz):
                _, zz, xx, _ = piece_spot(plan, meta, r, 0, fx, k, 1)
                row = pl.multiple_of((zz * 2 + xx) * plan.rows, 16)
                copies.append(
                    pltpu.make_async_copy(
                        buf.at[r, e, pl.ds(row, plan.rows), :],
                        outs[4 * r + 2 * e + fx].at[k],
                        sem.at[r, len(copies)],
                    )
                )
    return copies


def ff_grad_kernel(plan, meta, sl_a, sl_b, cot_a, cot_b, act_a, act_b, hg_a, hg_b, *rest):
    *outs, buf, sem = rest
    for r in (1, 0):
        for e, (a, b, one, two) in enumerate(
            ((sl_a, sl_b, hg_a, hg_b), (cot_a, cot_b, act_a, act_b))
        ):
            buf[r, e] = (mm_tn(a[...], one[r]) + mm_tn(b[...], two[r])).astype(bf16)
        for copy in ff_grad_copies(plan, meta, buf, outs, sem, r):
            copy.start()
    for r in range(2):
        for copy in ff_grad_copies(plan, meta, buf, outs, sem, r):
            copy.wait()


def attn_bwd_kernel(
    plan,
    meta,
    sga_ref,
    sgb_ref,
    mid_ref,
    cot_ref,
    np_ref,
    qkv_ref,
    p_ref,
    w,
    dqkv_ref,
    ml_ref,
    mg_ref,
    vec_ref,
    pair_ref,
):
    cols = plan.cols
    tiles = CHUNK // LANES
    pairs = cols // LANES
    vec_ref[...] = jnp.zeros_like(vec_ref)
    pair_ref[...] = jnp.zeros_like(pair_ref)

    def body(i, at):
        sg = sga_ref[at, :].astype(f32) + sgb_ref[at, :].astype(f32)
        cot = cot_ref[at, :].astype(f32)
        normal, scaled = norm_stats(mid_ref[at, :])
        mg = cot + norm_backward(sg, normal, scaled, np_ref[2:3, :])
        mg_ref[at, :] = mg
        ml = mg.astype(bf16)
        ml_ref[at, :] = ml
        vec_ref[0:1, :] += jnp.sum(sg * normal, axis=0, keepdims=True)
        vec_ref[1:2, :] += jnp.sum(sg, axis=0, keepdims=True)
        vec_ref[2:3, :] += jnp.sum(mg, axis=0, keepdims=True)
        vec_ref[3:4, :] += jnp.sum(cot, axis=0, keepdims=True)
        for y in range(2):
            dctx = mm(ml, w[y, :, 3 * cols :]).astype(bf16)
            for t in range(tiles):
                tile = i * tiles + t
                tok = pl.ds(pl.multiple_of(tile * LANES, LANES), LANES)
                dcs = [
                    split_heads(dctx[t * LANES : (t + 1) * LANES, lanes_of(0, 0, cols, p)])
                    for p in range(pairs)
                ]
                low = p_ref[tile * 2 + y]
                probs = low.astype(f32)
                dp = jnp.concatenate(
                    [
                        mm_nt(dcs[p], qkv_ref[y, tok, lanes_of(0, 2, cols, p)])
                        for p in range(pairs)
                    ],
                    axis=0,
                )
                inner = jnp.sum(dp * probs, axis=-1, keepdims=True)
                ds = (probs * (dp - inner) * HD**-0.5).astype(bf16)
                for p in range(pairs):
                    at_q, at_k, at_v = (lanes_of(0, b, cols, p) for b in range(3))
                    rows = slice(p * 2 * LANES, (p + 1) * 2 * LANES)
                    qs = split_heads(qkv_ref[y, tok, at_q])
                    dq = join_heads(mm(ds[rows], qkv_ref[y, tok, at_k])).astype(bf16)
                    dqkv_ref[y, tok, at_q] = dq
                    dqkv_ref[y, tok, at_k] = mm_tn(ds[rows], qs).astype(bf16)
                    dqkv_ref[y, tok, at_v] = mm_tn(low[rows], dcs[p]).astype(bf16)
            for b in (0, 2):
                lanes = slice(b * cols, (b + 1) * cols)
                pair_ref[b // 2 : b // 2 + 1, y * cols : (y + 1) * cols] += jnp.sum(
                    dqkv_ref[y, at, lanes].astype(f32), axis=0, keepdims=True
                )

    chunks(sga_ref.shape[0], body)


def attn_grad_pieces(plan, meta, buf, outs, sem, fy):
    if not plan.direct:
        yy = jnp.bitwise_xor(meta[3], fy)
        return [pltpu.make_async_copy(buf.at[fy], outs[0].at[yy], sem.at[fy, 0])]
    copies = []
    for r in range(2):
        for fx in range(2):
            for k in range(plan.nz):
                cc, zz, xx, _ = piece_spot(plan, meta, r, fy, fx, k, 1)
                s1 = jnp.where(cc == 0, fx, fy)
                s2 = jnp.where(cc == 0, fy, fx)
                row = pl.multiple_of((zz * 2 + xx) * plan.rows + cc * plan.half, 16)
                out = outs[r * plan.nz + k]
                if r == 0:
                    out[s2, s1] = buf[fy, pl.ds(row, plan.half), :]
                else:
                    copies.append(
                        pltpu.make_async_copy(
                            buf.at[fy, pl.ds(row, plan.half), :],
                            out.at[s2, s1],
                            sem.at[fy, len(copies)],
                        )
                    )
    return copies


def attn_grad_kernel(plan, meta, fl_ref, ml_ref, dqkv_ref, ctx_ref, *rest):
    *outs, buf, sem = rest
    cols = plan.cols
    copies = []
    for fy in range(2):
        y = jnp.bitwise_xor(meta[3], fy)
        lanes = pl.ds(pl.multiple_of(y * cols, LANES), cols)
        buf[fy, :, : 3 * cols] = mm_tn(fl_ref[...], dqkv_ref[y]).astype(bf16)
        buf[fy, :, 3 * cols :] = mm_tn(ml_ref[...], ctx_ref[:, lanes]).astype(bf16)
        some = attn_grad_pieces(plan, meta, buf, outs, sem, fy)
        for copy in some:
            copy.start()
        copies = copies + some
    for copy in copies:
        copy.wait()


def input_grad_kernel(
    plan, meta, x_all, mg_ref, np_ref, dqkv_ref, w, ig_ref, vec_ref, x_ref, buf, sem
):
    cols = plan.cols
    count = x_ref.shape[0]
    load = token_copy(x_all, meta[0], x_ref, sem.at[0])
    load.start()
    vec_ref[...] = jnp.zeros_like(vec_ref)
    load.wait()

    def body(i, at):
        normal, scaled = norm_stats(x_ref[at, :].astype(f32))
        fg = mm_nt(dqkv_ref[0, at, :], w[0, :, : 3 * cols])
        fg = fg + mm_nt(dqkv_ref[1, at, :], w[1, :, : 3 * cols])
        vec_ref[0:1, :] += jnp.sum(fg * normal, axis=0, keepdims=True)
        vec_ref[1:2, :] += jnp.sum(fg, axis=0, keepdims=True)
        ig = mg_ref[at, :] + norm_backward(fg, normal, scaled, np_ref[0:1, :])
        buf[at, :] = ig.astype(bf16)
        pltpu.make_async_copy(buf.at[at, :], ig_ref.at[at, :], sem.at[i]).start()

    chunks(count, body)
    for i in range(count // CHUNK):
        at = pl.ds(i * CHUNK, CHUNK)
        pltpu.make_async_copy(buf.at[at, :], ig_ref.at[at, :], sem.at[i]).wait()


def add_kernel(meta, left, right, *outs):
    for i, out in enumerate(outs):
        out[...] = (left[i].astype(f32) + right[i].astype(f32)).astype(out.dtype)


def add_parts(meta, left, right):
    n, size = left.shape[0], left.shape[-1]
    shape = left.shape[1:]
    left, right = left.reshape(n, -1, size), right.reshape(n, -1, size)
    length = left.shape[1]
    blocks = 4 if length % 64 == 0 and length >= 384 else 1
    step = length // blocks
    outs = call(
        add_kernel,
        "add_parts",
        (blocks,),
        [(v, (n, step, size), lambda i, m: (0, i, 0)) for v in (left, right)],
        [(jax.ShapeDtypeStruct((length, size), bf16), (step, size), lambda i, m: (i, 0))] * n,
        [],
    )(meta, left, right)
    return [v.reshape(shape) for v in outs]


def sums_kernel(meta, *refs):
    n = len(refs) // 3
    for left, right, out in zip(refs[:n], refs[n : 2 * n], refs[2 * n :]):
        out[...] = (left[...].astype(f32) + right[...].astype(f32)).astype(out.dtype)


def add_lists(meta, left, right):
    n, shape = len(left), left[0].shape
    flat = [v.reshape(-1, shape[-1]) for v in (*left, *right)]
    length, size = flat[0].shape
    blocks = 2 if length % 32 == 0 and length >= 384 else 1
    block = ((length // blocks, size), lambda i, m: (i, 0))
    outs = call(
        sums_kernel,
        "add_lists",
        (blocks,),
        [(v, *block) for v in flat],
        [(jax.ShapeDtypeStruct((length, size), bf16), *block)] * n,
        [],
    )(meta, *flat)
    return [v.reshape(shape) for v in outs]


def first_kernel(n, meta, *refs):
    left, right, (keep, send, got, buf, sem) = refs[:n], refs[n : 2 * n], refs[2 * n :]
    loads = [pltpu.make_async_copy(right[k], got.at[k], sem.at[k]) for k in range(n)]
    for load in loads:
        load.start()
    for k in range(n):
        loads[k].wait()
        for s, out in enumerate((keep, buf)):
            for i in range(out.shape[0]):
                out[i, k] = (left[k][s, i].astype(f32) + got[k, s, i].astype(f32)).astype(bf16)
    store = pltpu.make_async_copy(buf, send, sem.at[n])
    store.start()
    store.wait()


def add_first(meta, left, right):
    n, shape = len(left), left[0].shape[1:]
    out = jax.ShapeDtypeStruct((shape[0], n, *shape[1:]), bf16)
    return local_call(
        meta,
        functools.partial(first_kernel, n),
        "add_first",
        [(v, True) for v in left] + [(v, False) for v in right],
        [(out, True), (out, False)],
        [
            pltpu.VMEM((n, 2, *shape), bf16),
            pltpu.VMEM(out.shape, bf16),
            pltpu.SemaphoreType.DMA((n + 1,)),
        ],
    )


def vectors_kernel(plan, meta, one, two, pair, near, far, out, buf, sem):
    buf[...] = jnp.zeros_like(buf)
    per = buf.shape[2] // LANES
    lines = plan.width // LANES

    def put(start, row):
        for q in range(row.shape[1] // LANES):
            b = start + q
            at = slice(b % per * LANES, (b % per + 1) * LANES)
            buf[b // per, :, at] = row[:, q * LANES : (q + 1) * LANES]

    for i in range(2):
        put(i * lines, one[i : i + 1, :])
        put((6 + i) * lines, pair[i : i + 1, :])
    for i in range(4):
        put((2 + i) * lines, two[i : i + 1, :])
    total = near[...] + far[...]
    for y in range(2):
        for c in range(2):

            @pl.when((meta[3] == y) & (meta[4] == c))
            def _():
                for r in range(2):
                    m = 2 * y + (c + r) % 2
                    put(8 * lines + m * plan.part // LANES, total[r : r + 1, :])

    copy = pltpu.make_async_copy(buf, out, sem.at[0])
    copy.start()
    copy.wait()


def ff_total_kernel(meta, *refs):
    *parts, expand, reduce, square = refs
    half = len(parts) // 2
    sums = None
    for out, some in ((expand, parts[:half]), (reduce, parts[half:])):
        total = some[0][...].astype(f32)
        for part in some[1:]:
            total = total + part[...].astype(f32)
        out[...] = total
        line = jnp.sum(total * total, axis=0, keepdims=True)
        sums = line if sums is None else sums + line
    square[...] = jnp.sum(sums, axis=1, keepdims=True)


def total_kernel(meta, *refs):
    *parts, ff_square, local, keep, send, payload = refs
    total = parts[0][...].astype(f32)
    for part in parts[1:]:
        total = total + part[...].astype(f32)
    quarter = total.shape[1] // 8
    for core in range(2):
        for out, c in ((keep, core), (send, 1 - core)):

            @pl.when(meta[4] == core)
            def _():
                for b in range(4):
                    at = (2 * b + c) * quarter
                    out[:, b * quarter : (b + 1) * quarter] = total[:, at : at + quarter]

    square = jnp.sum(total * total) + jnp.sum(ff_square[...]) + jnp.sum(local[...] * local[...])
    size = local.shape[1]
    count = payload.shape[0]
    payload[:, :, :size] = jnp.broadcast_to(local[...][None], (count, 1, size))
    payload[:, :, size:] = jnp.full((count, 1, LANES), square, f32)


def out_kernel(meta, pre_a, fed_a, pre_b, fed_b, np_ref, out_a, out_b):
    for pre, fed, out in ((pre_a, fed_a, out_a), (pre_b, fed_b, out_b)):
        total = pre[...].astype(f32) + fed[...].astype(f32) + np_ref[5:6, :]
        out[...] = total.astype(bf16)


def place_kernel(meta, own, by_y, by_c, by_yc, out, sem):
    count = own.shape[0]
    copies = []
    for fy, fc, src in ((0, 0, own), (1, 0, by_y), (0, 1, by_c), (1, 1, by_yc)):
        at = jnp.bitwise_xor(meta[3], fy) * 2 + jnp.bitwise_xor(meta[4], fc)
        dst = out.at[pl.ds(pl.multiple_of(at * count, 16), count), :]
        copies.append(pltpu.make_async_copy(src, dst, sem.at[len(copies)]))
    for copy in copies:
        copy.start()
    for copy in copies:
        copy.wait()


def adam_kernel(plan, rates, meta, got, *refs):
    per = got.shape[2] // LANES - 1
    total = jnp.sum(got[:, 0, per * LANES :], axis=0, keepdims=True)[:, 0:1]
    norm = jnp.sqrt(total)
    refs[-1][...] = norm
    factor = jnp.minimum(1.0, CLIP / norm)
    correction = 1.0 - BETA**STEP
    width, quarter, part = plan.width, plan.width // 4, plan.part

    def line(start, length):
        spots = range(start // LANES, (start + length) // LANES)
        return jnp.concatenate(
            [got[b // per, :, b % per * LANES : (b % per + 1) * LANES] for b in spots],
            axis=1,
        )

    def owned(pick):
        value = pick(0)
        for m in range(1, 4):
            value = jnp.where(meta[0] == m, pick(m), value)
        return value

    pairs = [line((6 + i) * width, width) for i in range(2)]
    small = (
        jnp.concatenate([line(i * width, width) for i in range(6)], axis=0),
        jnp.concatenate(
            [owned(lambda m: v[:, m * quarter : (m + 1) * quarter]) for v in pairs], axis=0
        ),
        owned(lambda m: line(8 * width + m * part, part)),
    )
    ins, outs = refs[: 4 * 4 + 3 * 3], refs[4 * 4 + 3 * 3 : -1]
    for i, (rate, decay) in enumerate(rates):
        if i < 4:
            w_ref, m_ref, s_ref, g_ref = ins[4 * i : 4 * i + 4]
        else:
            w_ref, m_ref, s_ref = ins[3 * i + 4 : 3 * i + 7]
            g_ref = {Ellipsis: small[i - 4]}
        m_out, s_out, w_out = outs[3 * i : 3 * i + 3]
        planes = range(w_ref.shape[0]) if len(w_ref.shape) == 3 else (Ellipsis,)
        for p in planes:
            clipped = g_ref[p] * factor
            shape = w_ref[p].shape
            weight, first, second = (
                v[p].reshape(clipped.shape) for v in (w_ref, m_ref, s_ref)
            )
            first = BETA * first + (1.0 - BETA) * clipped
            second = BETA * second + (1.0 - BETA) * clipped * clipped
            direction = first / correction / (jnp.sqrt(second / correction) + ADAM_EPS)
            m_out[p] = first.reshape(shape)
            s_out[p] = second.reshape(shape)
            w_out[p] = (weight - rate * (direction + decay * weight)).reshape(shape)


def after(value, *others):
    return lax.optimization_barrier((value, *others))[0]


def any_spec():
    return pl.BlockSpec(memory_space=pl.ANY)


def local_call(meta, kernel, name, ins, outs, scratch, vmem=16):
    def space(item):
        return pltpu.VMEM if item[1] else pltpu.HBM

    def place(item):
        return item[0] if item[1] else pltpu.with_memory_space_constraint(item[0], pltpu.HBM)

    kernel_call = pl.pallas_call(
        kernel,
        name=name,
        out_shape=[space(o)(o[0].shape, o[0].dtype) for o in outs],
        in_specs=[pl.BlockSpec(memory_space=s) for s in (pltpu.SMEM, *map(space, ins))],
        out_specs=[pl.BlockSpec(memory_space=space(o)) for o in outs],
        scratch_shapes=scratch,
        compiler_params=pltpu.CompilerParams(vmem_limit_bytes=vmem * MIB),
        cost_estimate=pl.CostEstimate(flops=1, bytes_accessed=1, transcendentals=0),
    )
    return kernel_call(meta, *map(place, ins))


def call(kernel, name, grid, ins, outs, scratch, vmem=16):
    def spec(item):
        if item[1] is None:
            return any_spec()
        return pl.BlockSpec(item[1], item[2])

    return pl.pallas_call(
        kernel,
        name=name,
        out_shape=[o[0] for o in outs],
        grid_spec=pltpu.PrefetchScalarGridSpec(
            num_scalar_prefetch=1,
            grid=grid,
            in_specs=[spec(i) for i in ins],
            out_specs=[spec(o) for o in outs],
            scratch_shapes=scratch,
        ),
        compiler_params=pltpu.CompilerParams(vmem_limit_bytes=vmem * MIB),
        cost_estimate=pl.CostEstimate(flops=1, bytes_accessed=1, transcendentals=0),
    )


def per_device(
    inputs,
    segments,
    cotangent,
    triple_weight,
    triple_first,
    triple_second,
    outward_weight,
    outward_first,
    outward_second,
    expand_weight,
    expand_first,
    expand_second,
    reduce_weight,
    reduce_first,
    reduce_second,
    norm_params,
    norm_first,
    norm_second,
    paired_bias,
    paired_first,
    paired_second,
    hidden_bias,
    hidden_first,
    hidden_second,
):
    ndp, nmp = lax.axis_size("dp"), lax.axis_size("mp")
    width = inputs.shape[1]
    hidden = hidden_bias.shape[0] * nmp
    plan = Plan(ndp, nmp, width, hidden)
    nz, rows, half, cols, part = plan.nz, plan.rows, plan.half, plan.cols, plan.part
    count = inputs.shape[0] // nmp
    row_count, row_length = segments.shape
    own_rows = row_count // nmp
    steps = count // CHUNK
    quarter = cols // 2

    dp, mp = lax.axis_index("dp"), lax.axis_index("mp")
    z, x, y, c = dp // 2, dp % 2, mp // 2, mp % 2
    meta = jnp.stack([mp, z, x, y, c, jnp.bitwise_xor(mp, 2)]).astype(jnp.int32)
    core_zero = c == 0
    SDS = jax.ShapeDtypeStruct

    shard = jnp.concatenate(
        [triple_weight.astype(bf16), outward_weight.T.astype(bf16)[None]], axis=0
    ).transpose(1, 0, 2)
    keep = lax.dynamic_slice_in_dim(shard, c * half, half, 0)
    send = lax.dynamic_slice_in_dim(shard, (1 - c) * half, half, 0)
    got = plan.core(send)
    low = jnp.where(core_zero, keep, got)
    high = jnp.where(core_zero, got, keep)
    unit = jnp.concatenate([low, high], axis=2).reshape(half, 4 * cols)
    attn_z = [plan.along_z(unit, k) for k in range(1, nz)]

    e_unit = after(expand_weight.astype(bf16), attn_z[0])
    e_z = [plan.along_z(e_unit, k) for k in range(1, nz)]
    r_unit = after(reduce_weight.T.astype(bf16), e_z[0])
    r_z = [plan.along_z(r_unit, k) for k in range(1, nz)]

    biases = jnp.concatenate([paired_bias.reshape(-1), hidden_bias])
    by_core = plan.core(after(biases, attn_z[0]))
    other_pair = by_core[: 2 * quarter].reshape(2, quarter)
    near = jnp.where(
        core_zero,
        jnp.concatenate([paired_bias, other_pair], axis=1),
        jnp.concatenate([other_pair, paired_bias], axis=1),
    )
    far = plan.along_y(near)
    pair_full = jnp.where(
        y == 0, jnp.concatenate([near, far], axis=1), jnp.concatenate([far, near], axis=1)
    )
    hidden_rows = jnp.stack([hidden_bias, by_core[2 * quarter :]])

    marks = lax.dynamic_slice_in_dim(segments, mp * own_rows, own_rows, 0)
    marks = marks + row_length * lax.broadcasted_iota(jnp.int32, marks.shape, 0)
    mark_col = marks.reshape(count, 1)
    mark_row = marks.reshape(count // LANES, LANES)

    spread = jnp.stack([unit] + attn_z)
    spread = jnp.stack([spread, plan.first(spread)])
    spread, *_, meta, mark_col, mark_row, pair_full, hidden_rows = lax.optimization_barrier(
        (spread, e_z[0], meta, mark_col, mark_row, pair_full, hidden_rows)
    )
    attn_w = [spread, after(plan.second(spread), *e_z)]
    e_spread = after(jnp.stack([e_unit] + e_z), attn_w[1])
    e_x = plan.along_x(e_spread)
    attn_w = attn_w + [plan.core(v) for v in attn_w]
    attn_w[1] = after(attn_w[1], e_spread, r_z[0])

    if not plan.direct:
        attn_w = [absolute_attn(plan, jnp.stack(attn_w[:2]), jnp.stack(attn_w[2:]), z, x, y, c)]
        attn_w = attn_w + [meta] * 3

    whole = lambda shape: (shape, lambda i, m: (0,) * len(shape))
    chunk = lambda n: ((CHUNK, n), lambda i, m: (i, 0))
    pieces = 2 * 2 * 2 * nz if plan.direct else 1
    dma = pltpu.SemaphoreType.DMA

    tokens_low, tokens_f32 = SDS((count, width), bf16), SDS((count, width), f32)
    sem_x = dma((2 * steps,))
    buf_low = pltpu.VMEM((count, width), bf16)
    sl, middle, fl, qkv, probs, ctx, attn_full = local_call(
        meta,
        functools.partial(attn_fwd_kernel, plan),
        "attn_fwd",
        [
            (inputs, False),
            (mark_col, True),
            (mark_row, True),
            (norm_params, True),
            (pair_full, True),
            *[(v, False) for v in attn_w],
        ],
        [
            (tokens_low, False),
            (tokens_f32, True),
            (tokens_low, True),
            (SDS((2, count, 3 * cols), bf16), True),
            (SDS((count // LANES * 2, 2 * cols, LANES), bf16), True),
            (tokens_low, True),
            (SDS((2, width, 4 * cols), bf16), True),
        ],
        [buf_low, buf_low, dma((pieces,)), sem_x],
    )

    sl_far = plan.along_y(sl)
    r_spread = jnp.stack([r_unit, r_z[0]] + [after(v, sl) for v in r_z[1:]])
    r_x = plan.along_x(r_spread)
    e_x = after(e_x, sl)
    ff_w = []
    for near, far in ((e_spread, e_x), (r_spread, r_x)):
        pieces_of = [near, far, plan.core(near), plan.core(far)]
        if not plan.direct:
            pairs = (pieces_of[:2], pieces_of[2:])
            pieces_of = [v for p in pairs for v in (absolute_ff(plan, jnp.stack(p), z, x), meta)]
        ff_w = ff_w + pieces_of

    act_shape = SDS((2, count, part), bf16)
    gh_shape = SDS((2, part), f32)
    sg_send, fed_send, act_far, hg_far, gh_far, cot_far, ff_full = local_call(
        meta,
        functools.partial(ff_kernel, plan, False),
        "ff_far",
        [
            (sl_far, True),
            (cotangent, False),
            (hidden_rows, True),
            *[(v, False) for v in ff_w],
        ],
        [
            (tokens_low, False),
            (tokens_low, False),
            (act_shape, True),
            (act_shape, True),
            (gh_shape, True),
            (tokens_low, True),
            (SDS((2, 2, width, part), bf16), True),
        ],
        [buf_low, buf_low, dma((2, 2, 2 * nz if plan.direct else 1)), sem_x],
    )
    sg_far = plan.along_y(sg_send)
    sg_near, pre_near, act_near, hg_near, gh_near, cot_near = local_call(
        meta,
        functools.partial(ff_kernel, plan, True),
        "ff_near",
        [
            (sl, True),
            (cotangent, False),
            (hidden_rows, True),
            (ff_full, True),
            (middle, True),
        ],
        [
            (tokens_low, True),
            (tokens_low, False),
            (act_shape, True),
            (act_shape, True),
            (gh_shape, True),
            (tokens_low, True),
        ],
        [buf_low, sem_x],
    )

    if plan.direct:
        grad_shapes = [SDS((nz, rows, part), bf16)] * 8
    else:
        grad_shapes = [SDS((width, part), bf16)] * 4
    ff_ins = (sl, sl_far, cot_near, cot_far, act_near, act_far, hg_near, hg_far)
    ff_grads = local_call(
        meta,
        functools.partial(ff_grad_kernel, plan),
        "ff_grad",
        [(v, True) for v in ff_ins],
        [(v, False) for v in grad_shapes],
        [pltpu.VMEM((2, 2, width, part), bf16), dma((2, 4 * nz if plan.direct else 2))],
    )
    if not plan.direct:
        ff_grads = [v for g in ff_grads for v in relative_ff(plan, g, z, x)]

    ff_got = [plan.core(v) for v in ff_grads[4:]]
    sg_far = after(sg_far, ff_grads[0])
    fed_far = plan.along_y(after(fed_send, sg_far))

    bwd_ins = (sg_near, sg_far, middle, cot_near, norm_params, qkv, probs, attn_full)
    dqkv, ml, mg, vec_two, pair_sum = local_call(
        meta,
        functools.partial(attn_bwd_kernel, plan),
        "attn_bwd",
        [(v, True) for v in bwd_ins],
        [
            (SDS((2, count, 3 * cols), bf16), True),
            (tokens_low, True),
            (tokens_f32, True),
            (SDS((8, width), f32), True),
            (SDS((2, width), f32), True),
        ],
        [],
    )

    ff_got[0] = after(ff_got[0], dqkv)
    e_keep, e_send, r_keep, r_send = add_lists(meta, ff_grads[:4], ff_got)
    e_got = plan.along_x(e_send)

    if plan.direct:
        grad_shapes = [SDS((2, 2, half, 4 * cols), bf16)] * (2 * nz)
    else:
        grad_shapes = [SDS((2, width, 4 * cols), bf16)]
    ml = after(ml, e_send, r_send)
    attn_grads = local_call(
        meta,
        functools.partial(attn_grad_kernel, plan),
        "attn_grad",
        [(v, True) for v in (fl, ml, dqkv, ctx)],
        [(v, plan.direct and i < nz) for i, v in enumerate(grad_shapes)],
        [pltpu.VMEM((2, width, 4 * cols), bf16), dma((2, 4 * nz if plan.direct else 1))],
    )
    if not plan.direct:
        both = relative_attn(plan, attn_grads[0], z, x, y, c)
        attn_grads = [v[:, :, k] for v in both for k in range(nz)]
    attn_mine, attn_theirs = list(attn_grads[:nz]), list(attn_grads[nz:])
    attn_theirs[0] = after(attn_theirs[0], fed_far)
    attn_got = [plan.core(v) for v in attn_theirs]

    dqkv_late = after(dqkv, attn_theirs[0])
    ig, vec_one = local_call(
        meta,
        functools.partial(input_grad_kernel, plan),
        "input_grad",
        [
            (inputs, False),
            (mg, True),
            (norm_params, True),
            (dqkv_late, True),
            (attn_full, True),
        ],
        [(tokens_low, False), (SDS((8, width), f32), True)],
        [buf_low, buf_low, sem_x],
    )
    attn_got[0] = after(attn_got[0], ig, e_got)
    attn_keep, attn_send = add_first(meta, attn_mine, attn_got)
    attn_got = plan.second(attn_send)
    pre_far = plan.along_y(after(pre_near, attn_send))
    r_got = plan.along_x(after(r_send, attn_send))
    e_parts = add_parts(meta, e_keep, after(e_got, attn_send))
    e_z = [e_parts[0]] + [plan.along_z(e_parts[k], k) for k in range(1, nz)]
    size = -(-(8 * width + hidden) // (LANES * plan.ndev)) * LANES
    parts_in = (vec_one, vec_two, pair_sum, gh_near, gh_far)
    (vectors,) = local_call(
        meta,
        functools.partial(vectors_kernel, plan),
        "vectors",
        [(v, True) for v in parts_in],
        [(SDS((plan.ndev, 1, size), f32), False)],
        [pltpu.VMEM((plan.ndev, 1, size), f32), dma((1,))],
    )
    got = lax.all_to_all(vectors, AXES, 0, 0, tiled=True)
    local = jnp.sum(got, axis=0)

    attn_got = after(attn_got, local, *e_z, r_got)
    attn_keep, attn_send = add_parts(meta, attn_keep, attn_got)
    r_parts = add_parts(meta, r_keep, after(r_got, attn_send))
    r_z = [r_parts[0]] + [plan.along_z(r_parts[k], k) for k in range(1, nz)]
    attn_got = plan.first(attn_send)

    attn_parts = add_parts(meta, attn_keep, after(attn_got, pre_far, *r_z))

    ff_in = [*e_z, *r_z]
    grad_expand, grad_reduce, ff_square = call(
        ff_total_kernel,
        "ff_total",
        (1,),
        [(v, *whole(v.shape)) for v in ff_in],
        [
            (SDS((rows, part), f32), *whole((rows, part))),
            (SDS((rows, part), f32), *whole((rows, part))),
            (SDS((1, 1), f32), *whole((1, 1))),
        ],
        [],
    )(meta, *ff_in)

    pre_in = after(pre_near, attn_parts[0])
    out, out_pair = call(
        out_kernel,
        "out_sum",
        (steps,),
        [
            (pre_in, *chunk(width)),
            (fed_far, *chunk(width)),
            (pre_far, *chunk(width)),
            (fed_send, *chunk(width)),
            (norm_params, *whole(norm_params.shape)),
        ],
        [(SDS((count, width), bf16), *chunk(width))] * 2,
        [],
    )(meta, pre_in, fed_far, pre_far, fed_send, norm_params)
    ig = after(ig, attn_parts[0])
    ig_pair = plan.along_y(ig)
    attn_z = [attn_parts[0]] + [plan.along_z(attn_parts[k], k) for k in range(1, nz)]
    total_in = attn_z + [ff_square, local]
    def everywhere(block, by_y):
        blocks = [block, by_y, plan.core(block), plan.core(by_y)]
        return call(
            place_kernel,
            "place",
            (1,),
            [(b, *whole((count, width))) for b in blocks],
            [(SDS((count * nmp, width), bf16), None, None)],
            [dma((4,))],
        )(meta, *blocks)[0]

    outputs = everywhere(out, out_pair)
    total_in[-1] = after(total_in[-1], outputs)
    keep, send, payload = call(
        total_kernel,
        "total",
        (1,),
        [(v, *whole(v.shape)) for v in total_in],
        [
            (SDS((half, 2 * cols), f32), *whole((half, 2 * cols))),
            (SDS((half, 2 * cols), f32), *whole((half, 2 * cols))),
            (
                SDS((plan.ndev, 1, size + LANES), f32),
                *whole((plan.ndev, 1, size + LANES)),
            ),
        ],
        [],
    )(meta, *total_in)
    by_core = plan.core(send)
    ig_pair = after(ig_pair, keep)
    input_gradient = everywhere(ig, ig_pair)
    got = after(lax.all_to_all(payload, AXES, 0, 0, tiled=True), input_gradient)

    low, high = jnp.where(core_zero, keep, by_core), jnp.where(core_zero, by_core, keep)
    shard = jnp.concatenate([low, high], axis=0).reshape(rows, 4, quarter)
    grad_triple = shard[:, :3].transpose(1, 0, 2)
    grad_outward = shard[:, 3].T

    matrix, vector = (LR_MATRIX, DECAY), (LR_VECTOR, 0.0)
    groups = [
        [triple_weight, triple_first, triple_second, grad_triple],
        [outward_weight, outward_first, outward_second, grad_outward],
        [expand_weight, expand_first, expand_second, grad_expand],
        [reduce_weight.T, reduce_first.T, reduce_second.T, grad_reduce],
        [norm_params, norm_first, norm_second],
        [paired_bias, paired_first, paired_second],
        [hidden_bias, hidden_first, hidden_second],
    ]
    flat = [got] + [v for group in groups for v in group]
    new_shapes = [SDS(group[0].shape, f32) for group in groups for _ in range(3)]
    new_shapes.append(SDS((1, 1), f32))
    new = call(
        functools.partial(adam_kernel, plan, (matrix,) * 4 + (vector,) * 3),
        "adam",
        (1,),
        [(v, *whole(v.shape)) for v in flat],
        [(s, *whole(s.shape)) for s in new_shapes],
        [],
        vmem=60,
    )(meta, *flat)
    new = list(new)
    gradient_norm = new.pop().reshape(())
    new[9:12] = [v.T for v in new[9:12]]
    return (outputs, input_gradient, gradient_norm, *new)


def turn(plan, value, z, axis):
    value = jnp.flip(value, axis)
    return jnp.roll(value, z + 1, axis)


def unturn(plan, value, z, axis):
    return jnp.roll(value, -z, axis)


def swap(value, flag, axis):
    return jnp.where(flag == 1, jnp.flip(value, axis), value)


def absolute_ff(plan, value, z, x):
    value = swap(turn(plan, value, z, 1), x, 0)
    return value.transpose(1, 0, 2, 3).reshape(plan.width, plan.part)


def relative_ff(plan, value, z, x):
    value = value.reshape(plan.nz, 2, plan.rows, plan.part).transpose(1, 0, 2, 3)
    value = unturn(plan, swap(value, x, 0), z, 1)
    return value[0], value[1]


def absolute_attn(plan, own, other, z, x, y, c):
    zero = jnp.where(c == 0, own, other)
    one = jnp.where(c == 0, other, own).transpose(1, 0, 2, 3, 4)
    value = jnp.stack([zero, one])
    value = turn(plan, swap(swap(value, y, 1), x, 2), z, 3)
    value = value.transpose(1, 3, 2, 0, 4, 5)
    return value.reshape(2, plan.width, 4 * plan.cols)


def relative_attn(plan, value, z, x, y, c):
    value = value.reshape(2, plan.nz, 2, 2, plan.half, 4 * plan.cols)
    value = value.transpose(3, 0, 2, 1, 4, 5)
    value = unturn(plan, swap(swap(value, y, 1), x, 2), z, 3)
    zero, one = value[0], value[1].transpose(1, 0, 2, 3, 4)
    return jnp.where(c == 0, zero, one), jnp.where(c == 0, one, zero)


def solution(mesh):
    tokens = P("dp", None)
    triple = P(None, "dp", "mp")
    tall = P("mp", "dp")
    wide = P("dp", "mp")
    pair = P(None, "mp")
    states = ((triple,) * 3, (tall,) * 3, (wide,) * 3, (tall,) * 3, (P(),) * 3, (pair,) * 3)
    states = sum(states, ()) + (P("mp"),) * 3
    return jax.shard_map(
        per_device,
        mesh=mesh,
        in_specs=(tokens,) * 3 + states,
        out_specs=(tokens, tokens, P()) + states,
        check_vma=False,
    )
```

```python
import functools

import jax
import jax.numpy as jnp
from jax import lax
from jax.experimental import pallas as pl
from jax.experimental.pallas import tpu as pltpu
from jax.sharding import PartitionSpec as P

HD = 64
STEP = 5
EPS_NORM = 1e-06
BETA = 0.5
LR_MATRIX = 0.03
LR_VECTOR = 0.2
DECAY = 0.1
ADAM_EPS = 1e-08
CLIP = 1.0
NEG = -1e30
GELU_C = 0.7978845608028654
GELU_K = 0.044715

f32 = jnp.float32
bf16 = jnp.bfloat16
AXES = ("dp", "mp")
LANES = 128
CHUNK = 256
MIB = 1 << 20


def mm(left, right):
    return lax.dot_general(left, right, (((1,), (0,)), ((), ())), preferred_element_type=f32)


def mm_nt(left, right):
    return lax.dot_general(left, right, (((1,), (1,)), ((), ())), preferred_element_type=f32)


def mm_tn(left, right):
    return lax.dot_general(left, right, (((0,), (0,)), ((), ())), preferred_element_type=f32)


def norm_stats(rows_in):
    centred = rows_in - jnp.mean(rows_in, axis=-1, keepdims=True)
    scaled = lax.rsqrt(jnp.mean(centred * centred, axis=-1, keepdims=True) + EPS_NORM)
    return centred * scaled, scaled


def norm_backward(upstream, normal_rows, scaled, gain_row):
    gained = upstream * gain_row
    mean_one = jnp.mean(gained, axis=-1, keepdims=True)
    mean_two = jnp.mean(gained * normal_rows, axis=-1, keepdims=True)
    return scaled * (gained - mean_one - normal_rows * mean_two)


def lane_low(shape):
    return lax.broadcasted_iota(jnp.int32, shape, 1) % LANES < HD


def split_heads(block):
    low = lane_low(block.shape)
    zero = jnp.zeros_like(block)
    return jnp.concatenate([jnp.where(low, block, zero), jnp.where(low, zero, block)], axis=0)


def join_heads(stacked):
    half = stacked.shape[0] // 2
    low = lane_low((half, stacked.shape[1]))
    return jnp.where(low, stacked[:half], stacked[half:])


class Plan:
    def __init__(self, ndp, nmp, width, hidden):
        assert ndp % 2 == 0 and nmp == 4
        self.ndev = ndp * nmp
        self.nz = ndp // 2
        self.rows = width // ndp
        self.half = self.rows // 2
        self.width = width
        self.cols = width // 2
        self.part = hidden // nmp
        self.direct = self.half % 16 == 0

    def perm(self, move):
        pairs = []
        for z in range(self.nz):
            for x in range(2):
                for y in range(2):
                    for c in range(2):
                        there = move(z, x, y, c)
                        pairs.append((self.index(z, x, y, c), self.index(*there)))
        return pairs

    def index(self, z, x, y, c):
        return (2 * z + x) * 4 + 2 * y + c

    def core(self, value):
        return lax.ppermute(value, AXES, self.perm(lambda z, x, y, c: (z, x, y, 1 - c)))

    def along_x(self, value):
        return lax.ppermute(value, AXES, self.perm(lambda z, x, y, c: (z, 1 - x, y, c)))

    def along_y(self, value):
        return lax.ppermute(value, AXES, self.perm(lambda z, x, y, c: (z, x, 1 - y, c)))

    def along_z(self, value, step):
        return lax.ppermute(
            value, AXES, self.perm(lambda z, x, y, c: ((z + step) % self.nz, x, y, c))
        )

    def first(self, value):
        return lax.ppermute(
            value,
            AXES,
            self.perm(lambda z, x, y, c: (z, x, 1 - y, c) if c else (z, 1 - x, y, c)),
        )

    def second(self, value):
        return lax.ppermute(
            value,
            AXES,
            self.perm(lambda z, x, y, c: (z, 1 - x, y, c) if c else (z, x, 1 - y, c)),
        )


def piece_spot(plan, meta, r, fy, fx, k, sign):
    z, x, y, c = meta[1], meta[2], meta[3], meta[4]
    cc = jnp.bitwise_xor(c, r)
    zz = lax.rem(z + sign * k + plan.nz, plan.nz)
    xx = jnp.bitwise_xor(x, fx)
    yy = jnp.bitwise_xor(y, fy)
    return cc, zz, xx, yy


def attn_weight_copies(plan, meta, srcs, w, sem, lanes):
    if not plan.direct:
        return [pltpu.make_async_copy(srcs[0].at[:, :, lanes], w, sem.at[0])]
    copies = []
    for s2 in range(2):
        for r in range(2):
            for s1 in range(2):
                for k in range(plan.nz):
                    cc = jnp.bitwise_xor(meta[4], r)
                    fx = jnp.where(cc == 0, s1, s2)
                    fy = jnp.where(cc == 0, s2, s1)
                    _, zz, xx, yy = piece_spot(plan, meta, r, fy, fx, k, -1)
                    row = pl.multiple_of((zz * 2 + xx) * plan.rows + cc * plan.half, 16)
                    copies.append(
                        pltpu.make_async_copy(
                            srcs[2 * r + s2].at[s1, k, :, lanes],
                            w.at[yy, pl.ds(row, plan.half), :],
                            sem.at[len(copies)],
                        )
                    )
    return copies


def token_copy(src, block, dst, sem):
    count = dst.shape[0]
    return pltpu.make_async_copy(
        src.at[pl.ds(pl.multiple_of(block * count, 16), count), :], dst, sem
    )


def chunks(count, body):
    def step(i, carry):
        body(i, pl.ds(pl.multiple_of(i * CHUNK, CHUNK), CHUNK))
        return carry

    lax.fori_loop(0, count // CHUNK, step, 0)


def lanes_of(base, b, cols, p):
    return slice(base + b * cols + p * LANES, base + b * cols + (p + 1) * LANES)


def attn_fwd_kernel(plan, meta, x_all, segc_ref, segr_ref, np_ref, pb_ref, *refs):
    srcs, refs = refs[:4], refs[4:]
    sl_ref, mid_ref, fl_ref, qkv_ref, p_ref, ctx_ref, w, sl_buf, x_ref, sem, sem_x = refs
    cols = plan.cols
    count = x_ref.shape[0]
    copies = attn_weight_copies(plan, meta, srcs, w, sem, slice(None))
    load = token_copy(x_all, meta[0], x_ref, sem_x.at[0])
    load.start()
    for copy in copies:
        copy.start()
    load.wait()

    def first(i, at):
        normal, _ = norm_stats(x_ref[at, :].astype(f32))
        fl_ref[at, :] = (normal * np_ref[0:1, :] + np_ref[1:2, :]).astype(bf16)

    chunks(count, first)
    for copy in copies:
        copy.wait()
    tiles = CHUNK // LANES
    pairs = cols // LANES

    def second(i, at):
        for y in range(2):
            for part in range(3):
                lanes = slice(part * cols, (part + 1) * cols)
                got = mm(fl_ref[at, :], w[y, :, lanes])
                if part != 1:
                    got = got + pb_ref[part // 2 : part // 2 + 1, y * cols : (y + 1) * cols]
                qkv_ref[y, at, lanes] = got.astype(bf16)
        for t in range(tiles):
            tile = i * tiles + t
            tok = pl.ds(pl.multiple_of(tile * LANES, LANES), LANES)
            same = segc_ref[tok, :] == segr_ref[pl.ds(tile, 1), :]
            same = jnp.concatenate([same] * (2 * pairs), axis=0)
            for y in range(2):
                s = jnp.concatenate(
                    [
                        mm_nt(
                            split_heads(qkv_ref[y, tok, lanes_of(0, 0, cols, p)]),
                            qkv_ref[y, tok, lanes_of(0, 1, cols, p)],
                        )
                        for p in range(pairs)
                    ],
                    axis=0,
                )
                s = jnp.where(same, s * HD**-0.5, NEG)
                e = jnp.exp(s - jnp.max(s, axis=-1, keepdims=True))
                probs = (e * (1.0 / jnp.sum(e, axis=-1, keepdims=True))).astype(bf16)
                p_ref[tile * 2 + y] = probs
                for p in range(pairs):
                    own = probs[p * 2 * LANES : (p + 1) * 2 * LANES]
                    ctx = join_heads(mm(own, qkv_ref[y, tok, lanes_of(0, 2, cols, p)]))
                    ctx_ref[tok, lanes_of(y * cols, 0, cols, p)] = ctx.astype(bf16)
        attended = mm_nt(ctx_ref[at, 0:cols], w[0, :, 3 * cols :])
        attended = attended + mm_nt(ctx_ref[at, cols:], w[1, :, 3 * cols :])
        middle = x_ref[at, :].astype(f32) + attended + np_ref[4:5, :]
        mid_ref[at, :] = middle
        normal, _ = norm_stats(middle)
        sl = (normal * np_ref[2:3, :] + np_ref[3:4, :]).astype(bf16)
        sl_buf[at, :] = sl
        pltpu.make_async_copy(sl_buf.at[at, :], sl_ref.at[at, :], sem_x.at[i]).start()

    chunks(count, second)
    for i in range(count // CHUNK):
        at = pl.ds(i * CHUNK, CHUNK)
        pltpu.make_async_copy(sl_buf.at[at, :], sl_ref.at[at, :], sem_x.at[i]).wait()


def ff_weight_copies(plan, meta, srcs, w, sem, r, e):
    src = srcs[4 * e + 2 * r : 4 * e + 2 * r + 2]
    if not plan.direct:
        return [pltpu.make_async_copy(src[0], w.at[e, r], sem.at[r, e, 0])]
    copies = []
    for fx in range(2):
        for k in range(plan.nz):
            _, zz, xx, _ = piece_spot(plan, meta, r, 0, fx, k, -1)
            row = pl.multiple_of((zz * 2 + xx) * plan.rows, 16)
            copies.append(
                pltpu.make_async_copy(
                    src[fx].at[k],
                    w.at[e, r, pl.ds(row, plan.rows), :],
                    sem.at[r, e, len(copies)],
                )
            )
    return copies


def ff_kernel(plan, own, meta, sl_ref, cot_all, hb_ref, *refs):
    copies = []
    if own:
        w, mid_ref, sg_ref, fed_ref, act_ref, hg_ref, gh_ref, cot_ref, buf, sem_x = refs
    else:
        *srcs, sg_ref, fed_ref, act_ref, hg_ref, gh_ref, cot_ref, w, sg_buf, buf, sem, sem_x = refs
        for r in range(2):
            for e in range(2):
                copies = copies + ff_weight_copies(plan, meta, srcs, w, sem, r, e)
    for copy in copies:
        copy.start()
    count = cot_ref.shape[0]
    load = token_copy(cot_all, meta[0 if own else 5], cot_ref, sem_x.at[0])
    load.start()
    gh_ref[...] = jnp.zeros_like(gh_ref)
    load.wait()
    for copy in copies:
        copy.wait()

    def body(i, at):
        sl = sl_ref[at, :]
        cot = cot_ref[at, :]
        total = [None, None]
        for r in range(2):
            h = mm(sl, w[0, r]) + hb_ref[r : r + 1, :]
            grown = mm(cot, w[1, r])
            square = h * h
            half = 0.5 * jnp.tanh(h * (GELU_C + (GELU_C * GELU_K) * square)) + 0.5
            act = h * half
            slope = half + (act - act * half) * (2.0 * GELU_C + (6.0 * GELU_C * GELU_K) * square)
            grown = grown * slope
            gh_ref[r : r + 1, :] += jnp.sum(grown, axis=0, keepdims=True)
            act = act.astype(bf16)
            grown = grown.astype(bf16)
            act_ref[r, at, :] = act
            hg_ref[r, at, :] = grown
            for e, left in enumerate((grown, act)):
                got = mm_nt(left, w[e, r])
                total[e] = got if total[e] is None else total[e] + got
        fed = total[1] + mid_ref[at, :] if own else total[1]
        buf[at, :] = fed.astype(bf16)
        pltpu.make_async_copy(buf.at[at, :], fed_ref.at[at, :], sem_x.at[i]).start()
        if own:
            sg_ref[at, :] = total[0].astype(bf16)
        else:
            sg_buf[at, :] = total[0].astype(bf16)
            pltpu.make_async_copy(
                sg_buf.at[at, :], sg_ref.at[at, :], sem_x.at[count // CHUNK + i]
            ).start()

    chunks(count, body)
    for i in range(count // CHUNK):
        at = pl.ds(i * CHUNK, CHUNK)
        pltpu.make_async_copy(buf.at[at, :], fed_ref.at[at, :], sem_x.at[i]).wait()
        if not own:
            pltpu.make_async_copy(
                sg_buf.at[at, :], sg_ref.at[at, :], sem_x.at[count // CHUNK + i]
            ).wait()


def ff_grad_copies(plan, meta, buf, outs, sem, r):
    if not plan.direct:
        return [
            pltpu.make_async_copy(buf.at[r, e], outs[2 * r + e], sem.at[r, e]) for e in range(2)
        ]
    copies = []
    for e in range(2):
        for fx in range(2):
            for k in range(plan.nz):
                _, zz, xx, _ = piece_spot(plan, meta, r, 0, fx, k, 1)
                row = pl.multiple_of((zz * 2 + xx) * plan.rows, 16)
                copies.append(
                    pltpu.make_async_copy(
                        buf.at[r, e, pl.ds(row, plan.rows), :],
                        outs[4 * r + 2 * e + fx].at[k],
                        sem.at[r, len(copies)],
                    )
                )
    return copies


def ff_grad_kernel(plan, meta, sl_a, sl_b, cot_a, cot_b, act_a, act_b, hg_a, hg_b, *rest):
    *outs, buf, sem = rest
    for r in (1, 0):
        for e, (a, b, one, two) in enumerate(
            ((sl_a, sl_b, hg_a, hg_b), (cot_a, cot_b, act_a, act_b))
        ):
            buf[r, e] = (mm_tn(a[...], one[r]) + mm_tn(b[...], two[r])).astype(bf16)
        for copy in ff_grad_copies(plan, meta, buf, outs, sem, r):
            copy.start()
    for r in range(2):
        for copy in ff_grad_copies(plan, meta, buf, outs, sem, r):
            copy.wait()


def attn_bwd_kernel(
    plan,
    meta,
    sga_ref,
    sgb_ref,
    mid_ref,
    cot_ref,
    np_ref,
    qkv_ref,
    p_ref,
    w,
    dqkv_ref,
    ml_ref,
    mg_ref,
    vec_ref,
    pair_ref,
):
    cols = plan.cols
    tiles = CHUNK // LANES
    pairs = cols // LANES
    vec_ref[...] = jnp.zeros_like(vec_ref)
    pair_ref[...] = jnp.zeros_like(pair_ref)

    def body(i, at):
        sg = sga_ref[at, :].astype(f32) + sgb_ref[at, :].astype(f32)
        cot = cot_ref[at, :].astype(f32)
        normal, scaled = norm_stats(mid_ref[at, :])
        mg = cot + norm_backward(sg, normal, scaled, np_ref[2:3, :])
        mg_ref[at, :] = mg
        ml = mg.astype(bf16)
        ml_ref[at, :] = ml
        vec_ref[0:1, :] += jnp.sum(sg * normal, axis=0, keepdims=True)
        vec_ref[1:2, :] += jnp.sum(sg, axis=0, keepdims=True)
        vec_ref[2:3, :] += jnp.sum(mg, axis=0, keepdims=True)
        vec_ref[3:4, :] += jnp.sum(cot, axis=0, keepdims=True)
        for y in range(2):
            dctx = mm(ml, w[y, :, 3 * cols :]).astype(bf16)
            for t in range(tiles):
                tile = i * tiles + t
                tok = pl.ds(pl.multiple_of(tile * LANES, LANES), LANES)
                dcs = [
                    split_heads(dctx[t * LANES : (t + 1) * LANES, lanes_of(0, 0, cols, p)])
                    for p in range(pairs)
                ]
                low = p_ref[tile * 2 + y]
                probs = low.astype(f32)
                dp = jnp.concatenate(
                    [
                        mm_nt(dcs[p], qkv_ref[y, tok, lanes_of(0, 2, cols, p)])
                        for p in range(pairs)
                    ],
                    axis=0,
                )
                inner = jnp.sum(dp * probs, axis=-1, keepdims=True)
                ds = (probs * (dp - inner) * HD**-0.5).astype(bf16)
                for p in range(pairs):
                    at_q, at_k, at_v = (lanes_of(0, b, cols, p) for b in range(3))
                    rows = slice(p * 2 * LANES, (p + 1) * 2 * LANES)
                    qs = split_heads(qkv_ref[y, tok, at_q])
                    dq = join_heads(mm(ds[rows], qkv_ref[y, tok, at_k])).astype(bf16)
                    dqkv_ref[y, tok, at_q] = dq
                    dqkv_ref[y, tok, at_k] = mm_tn(ds[rows], qs).astype(bf16)
                    dqkv_ref[y, tok, at_v] = mm_tn(low[rows], dcs[p]).astype(bf16)
            for b in (0, 2):
                lanes = slice(b * cols, (b + 1) * cols)
                pair_ref[b // 2 : b // 2 + 1, y * cols : (y + 1) * cols] += jnp.sum(
                    dqkv_ref[y, at, lanes].astype(f32), axis=0, keepdims=True
                )

    chunks(sga_ref.shape[0], body)


def attn_grad_pieces(plan, meta, buf, outs, sem, fy):
    if not plan.direct:
        yy = jnp.bitwise_xor(meta[3], fy)
        return [pltpu.make_async_copy(buf.at[fy], outs[0].at[yy], sem.at[fy, 0])]
    copies = []
    for r in range(2):
        for fx in range(2):
            for k in range(plan.nz):
                cc, zz, xx, _ = piece_spot(plan, meta, r, fy, fx, k, 1)
                s1 = jnp.where(cc == 0, fx, fy)
                s2 = jnp.where(cc == 0, fy, fx)
                row = pl.multiple_of((zz * 2 + xx) * plan.rows + cc * plan.half, 16)
                out = outs[r * plan.nz + k]
                if r == 0:
                    out[s2, s1] = buf[fy, pl.ds(row, plan.half), :]
                else:
                    copies.append(
                        pltpu.make_async_copy(
                            buf.at[fy, pl.ds(row, plan.half), :],
                            out.at[s2, s1],
                            sem.at[fy, len(copies)],
                        )
                    )
    return copies


def attn_grad_kernel(plan, meta, fl_ref, ml_ref, dqkv_ref, ctx_ref, *rest):
    *outs, buf, sem = rest
    cols = plan.cols
    copies = []
    for fy in range(2):
        y = jnp.bitwise_xor(meta[3], fy)
        lanes = pl.ds(pl.multiple_of(y * cols, LANES), cols)
        buf[fy, :, : 3 * cols] = mm_tn(fl_ref[...], dqkv_ref[y]).astype(bf16)
        buf[fy, :, 3 * cols :] = mm_tn(ml_ref[...], ctx_ref[:, lanes]).astype(bf16)
        some = attn_grad_pieces(plan, meta, buf, outs, sem, fy)
        for copy in some:
            copy.start()
        copies = copies + some
    for copy in copies:
        copy.wait()


def input_grad_kernel(
    plan, meta, x_all, mg_ref, np_ref, dqkv_ref, w, ig_ref, vec_ref, x_ref, buf, sem
):
    cols = plan.cols
    count = x_ref.shape[0]
    load = token_copy(x_all, meta[0], x_ref, sem.at[0])
    load.start()
    vec_ref[...] = jnp.zeros_like(vec_ref)
    load.wait()

    def body(i, at):
        normal, scaled = norm_stats(x_ref[at, :].astype(f32))
        fg = mm_nt(dqkv_ref[0, at, :], w[0, :, : 3 * cols])
        fg = fg + mm_nt(dqkv_ref[1, at, :], w[1, :, : 3 * cols])
        vec_ref[0:1, :] += jnp.sum(fg * normal, axis=0, keepdims=True)
        vec_ref[1:2, :] += jnp.sum(fg, axis=0, keepdims=True)
        ig = mg_ref[at, :] + norm_backward(fg, normal, scaled, np_ref[0:1, :])
        buf[at, :] = ig.astype(bf16)
        pltpu.make_async_copy(buf.at[at, :], ig_ref.at[at, :], sem.at[i]).start()

    chunks(count, body)
    for i in range(count // CHUNK):
        at = pl.ds(i * CHUNK, CHUNK)
        pltpu.make_async_copy(buf.at[at, :], ig_ref.at[at, :], sem.at[i]).wait()


def add_kernel(meta, left, right, *outs):
    for i, out in enumerate(outs):
        out[...] = (left[i].astype(f32) + right[i].astype(f32)).astype(out.dtype)


def add_parts(meta, left, right):
    n, size = left.shape[0], left.shape[-1]
    shape = left.shape[1:]
    left, right = left.reshape(n, -1, size), right.reshape(n, -1, size)
    length = left.shape[1]
    blocks = 4 if length % 64 == 0 and length >= 384 else 1
    step = length // blocks
    outs = call(
        add_kernel,
        "add_parts",
        (blocks,),
        [(v, (n, step, size), lambda i, m: (0, i, 0)) for v in (left, right)],
        [(jax.ShapeDtypeStruct((length, size), bf16), (step, size), lambda i, m: (i, 0))] * n,
        [],
    )(meta, left, right)
    return [v.reshape(shape) for v in outs]


def sums_kernel(meta, *refs):
    n = len(refs) // 3
    for left, right, out in zip(refs[:n], refs[n : 2 * n], refs[2 * n :]):
        out[...] = (left[...].astype(f32) + right[...].astype(f32)).astype(out.dtype)


def add_lists(meta, left, right):
    n, shape = len(left), left[0].shape
    flat = [v.reshape(-1, shape[-1]) for v in (*left, *right)]
    length, size = flat[0].shape
    blocks = 2 if length % 32 == 0 and length >= 384 else 1
    block = ((length // blocks, size), lambda i, m: (i, 0))
    outs = call(
        sums_kernel,
        "add_lists",
        (blocks,),
        [(v, *block) for v in flat],
        [(jax.ShapeDtypeStruct((length, size), bf16), *block)] * n,
        [],
    )(meta, *flat)
    return [v.reshape(shape) for v in outs]


def first_kernel(n, meta, *refs):
    left, right, (keep, send, got, buf, sem) = refs[:n], refs[n : 2 * n], refs[2 * n :]
    loads = [pltpu.make_async_copy(right[k], got.at[k], sem.at[k]) for k in range(n)]
    for load in loads:
        load.start()
    for k in range(n):
        loads[k].wait()
        for s, out in enumerate((keep, buf)):
            for i in range(out.shape[0]):
                out[i, k] = (left[k][s, i].astype(f32) + got[k, s, i].astype(f32)).astype(bf16)
    store = pltpu.make_async_copy(buf, send, sem.at[n])
    store.start()
    store.wait()


def add_first(meta, left, right):
    n, shape = len(left), left[0].shape[1:]
    out = jax.ShapeDtypeStruct((shape[0], n, *shape[1:]), bf16)
    return local_call(
        meta,
        functools.partial(first_kernel, n),
        "add_first",
        [(v, True) for v in left] + [(v, False) for v in right],
        [(out, True), (out, False)],
        [
            pltpu.VMEM((n, 2, *shape), bf16),
            pltpu.VMEM(out.shape, bf16),
            pltpu.SemaphoreType.DMA((n + 1,)),
        ],
    )


def vectors_kernel(plan, meta, one, two, pair, near, far, out, buf, sem):
    buf[...] = jnp.zeros_like(buf)
    per = buf.shape[2] // LANES
    lines = plan.width // LANES

    def put(start, row):
        for q in range(row.shape[1] // LANES):
            b = start + q
            at = slice(b % per * LANES, (b % per + 1) * LANES)
            buf[b // per, :, at] = row[:, q * LANES : (q + 1) * LANES]

    for i in range(2):
        put(i * lines, one[i : i + 1, :])
        put((6 + i) * lines, pair[i : i + 1, :])
    for i in range(4):
        put((2 + i) * lines, two[i : i + 1, :])
    total = near[...] + far[...]
    for y in range(2):
        for c in range(2):

            @pl.when((meta[3] == y) & (meta[4] == c))
            def _():
                for r in range(2):
                    m = 2 * y + (c + r) % 2
                    put(8 * lines + m * plan.part // LANES, total[r : r + 1, :])

    copy = pltpu.make_async_copy(buf, out, sem.at[0])
    copy.start()
    copy.wait()


def ff_total_kernel(meta, *refs):
    *parts, expand, reduce, square = refs
    half = len(parts) // 2
    sums = None
    for out, some in ((expand, parts[:half]), (reduce, parts[half:])):
        total = some[0][...].astype(f32)
        for part in some[1:]:
            total = total + part[...].astype(f32)
        out[...] = total
        line = jnp.sum(total * total, axis=0, keepdims=True)
        sums = line if sums is None else sums + line
    square[...] = jnp.sum(sums, axis=1, keepdims=True)


def total_kernel(meta, *refs):
    *parts, ff_square, local, keep, send, payload = refs
    total = parts[0][...].astype(f32)
    for part in parts[1:]:
        total = total + part[...].astype(f32)
    quarter = total.shape[1] // 8
    for core in range(2):
        for out, c in ((keep, core), (send, 1 - core)):

            @pl.when(meta[4] == core)
            def _():
                for b in range(4):
                    at = (2 * b + c) * quarter
                    out[:, b * quarter : (b + 1) * quarter] = total[:, at : at + quarter]

    square = jnp.sum(total * total) + jnp.sum(ff_square[...]) + jnp.sum(local[...] * local[...])
    size = local.shape[1]
    count = payload.shape[0]
    payload[:, :, :size] = jnp.broadcast_to(local[...][None], (count, 1, size))
    payload[:, :, size:] = jnp.full((count, 1, LANES), square, f32)


def out_kernel(meta, pre_a, fed_a, pre_b, fed_b, np_ref, out_a, out_b):
    for pre, fed, out in ((pre_a, fed_a, out_a), (pre_b, fed_b, out_b)):
        total = pre[...].astype(f32) + fed[...].astype(f32) + np_ref[5:6, :]
        out[...] = total.astype(bf16)


def place_kernel(meta, own, by_y, by_c, by_yc, out, sem):
    count = own.shape[0]
    copies = []
    for fy, fc, src in ((0, 0, own), (1, 0, by_y), (0, 1, by_c), (1, 1, by_yc)):
        at = jnp.bitwise_xor(meta[3], fy) * 2 + jnp.bitwise_xor(meta[4], fc)
        dst = out.at[pl.ds(pl.multiple_of(at * count, 16), count), :]
        copies.append(pltpu.make_async_copy(src, dst, sem.at[len(copies)]))
    for copy in copies:
        copy.start()
    for copy in copies:
        copy.wait()


def adam_kernel(plan, rates, meta, got, *refs):
    per = got.shape[2] // LANES - 1
    total = jnp.sum(got[:, 0, per * LANES :], axis=0, keepdims=True)[:, 0:1]
    norm = jnp.sqrt(total)
    refs[-1][...] = norm
    factor = jnp.minimum(1.0, CLIP / norm)
    correction = 1.0 - BETA**STEP
    width, quarter, part = plan.width, plan.width // 4, plan.part

    def line(start, length):
        spots = range(start // LANES, (start + length) // LANES)
        return jnp.concatenate(
            [got[b // per, :, b % per * LANES : (b % per + 1) * LANES] for b in spots],
            axis=1,
        )

    def owned(pick):
        value = pick(0)
        for m in range(1, 4):
            value = jnp.where(meta[0] == m, pick(m), value)
        return value

    pairs = [line((6 + i) * width, width) for i in range(2)]
    small = (
        jnp.concatenate([line(i * width, width) for i in range(6)], axis=0),
        jnp.concatenate(
            [owned(lambda m: v[:, m * quarter : (m + 1) * quarter]) for v in pairs], axis=0
        ),
        owned(lambda m: line(8 * width + m * part, part)),
    )
    ins, outs = refs[: 4 * 4 + 3 * 3], refs[4 * 4 + 3 * 3 : -1]
    attn = {}
    if plan.direct:
        mine, other = ins[3][...], ins[7][...]
        low = jnp.where(meta[4] == 0, mine, other)
        high = jnp.where(meta[4] == 0, other, mine)
        for p in range(4):
            at = slice(p * quarter, (p + 1) * quarter)
            attn[p] = jnp.concatenate([low[:, at], high[:, at]], axis=0)
    for i, (rate, decay) in enumerate(rates):
        if i < 4:
            w_ref, m_ref, s_ref, g_ref = ins[4 * i : 4 * i + 4]
            if plan.direct and i < 2:
                g_ref = attn if i == 0 else {Ellipsis: attn[3].T}
        else:
            w_ref, m_ref, s_ref = ins[3 * i + 4 : 3 * i + 7]
            g_ref = {Ellipsis: small[i - 4]}
        m_out, s_out, w_out = outs[3 * i : 3 * i + 3]
        planes = range(w_ref.shape[0]) if len(w_ref.shape) == 3 else (Ellipsis,)
        for p in planes:
            clipped = g_ref[p] * factor
            shape = w_ref[p].shape
            weight, first, second = (
                v[p].reshape(clipped.shape) for v in (w_ref, m_ref, s_ref)
            )
            first = BETA * first + (1.0 - BETA) * clipped
            second = BETA * second + (1.0 - BETA) * clipped * clipped
            direction = first / correction / (jnp.sqrt(second / correction) + ADAM_EPS)
            m_out[p] = first.reshape(shape)
            s_out[p] = second.reshape(shape)
            w_out[p] = (weight - rate * (direction + decay * weight)).reshape(shape)


def after(value, *others):
    return lax.optimization_barrier((value, *others))[0]


def any_spec():
    return pl.BlockSpec(memory_space=pl.ANY)


def local_call(meta, kernel, name, ins, outs, scratch, vmem=16):
    def space(item):
        return pltpu.VMEM if item[1] else pltpu.HBM

    def place(item):
        return item[0] if item[1] else pltpu.with_memory_space_constraint(item[0], pltpu.HBM)

    kernel_call = pl.pallas_call(
        kernel,
        name=name,
        out_shape=[space(o)(o[0].shape, o[0].dtype) for o in outs],
        in_specs=[pl.BlockSpec(memory_space=s) for s in (pltpu.SMEM, *map(space, ins))],
        out_specs=[pl.BlockSpec(memory_space=space(o)) for o in outs],
        scratch_shapes=scratch,
        compiler_params=pltpu.CompilerParams(vmem_limit_bytes=vmem * MIB),
        cost_estimate=pl.CostEstimate(flops=1, bytes_accessed=1, transcendentals=0),
    )
    return kernel_call(meta, *map(place, ins))


def call(kernel, name, grid, ins, outs, scratch, vmem=16):
    def spec(item):
        if item[1] is None:
            return any_spec()
        return pl.BlockSpec(item[1], item[2])

    return pl.pallas_call(
        kernel,
        name=name,
        out_shape=[o[0] for o in outs],
        grid_spec=pltpu.PrefetchScalarGridSpec(
            num_scalar_prefetch=1,
            grid=grid,
            in_specs=[spec(i) for i in ins],
            out_specs=[spec(o) for o in outs],
            scratch_shapes=scratch,
        ),
        compiler_params=pltpu.CompilerParams(vmem_limit_bytes=vmem * MIB),
        cost_estimate=pl.CostEstimate(flops=1, bytes_accessed=1, transcendentals=0),
    )


def per_device(
    inputs,
    segments,
    cotangent,
    triple_weight,
    triple_first,
    triple_second,
    outward_weight,
    outward_first,
    outward_second,
    expand_weight,
    expand_first,
    expand_second,
    reduce_weight,
    reduce_first,
    reduce_second,
    norm_params,
    norm_first,
    norm_second,
    paired_bias,
    paired_first,
    paired_second,
    hidden_bias,
    hidden_first,
    hidden_second,
):
    ndp, nmp = lax.axis_size("dp"), lax.axis_size("mp")
    width = inputs.shape[1]
    hidden = hidden_bias.shape[0] * nmp
    plan = Plan(ndp, nmp, width, hidden)
    nz, rows, half, cols, part = plan.nz, plan.rows, plan.half, plan.cols, plan.part
    count = inputs.shape[0] // nmp
    row_count, row_length = segments.shape
    own_rows = row_count // nmp
    steps = count // CHUNK
    quarter = cols // 2

    dp, mp = lax.axis_index("dp"), lax.axis_index("mp")
    z, x, y, c = dp // 2, dp % 2, mp // 2, mp % 2
    meta = jnp.stack([mp, z, x, y, c, jnp.bitwise_xor(mp, 2)]).astype(jnp.int32)
    core_zero = c == 0
    SDS = jax.ShapeDtypeStruct

    shard = jnp.concatenate(
        [triple_weight.astype(bf16), outward_weight.T.astype(bf16)[None]], axis=0
    ).transpose(1, 0, 2)
    keep = lax.dynamic_slice_in_dim(shard, c * half, half, 0)
    send = lax.dynamic_slice_in_dim(shard, (1 - c) * half, half, 0)
    got = plan.core(send)
    low = jnp.where(core_zero, keep, got)
    high = jnp.where(core_zero, got, keep)
    unit = jnp.concatenate([low, high], axis=2).reshape(half, 4 * cols)
    attn_z = [plan.along_z(unit, k) for k in range(1, nz)]

    e_unit = after(expand_weight.astype(bf16), attn_z[0])
    e_z = [plan.along_z(e_unit, k) for k in range(1, nz)]
    r_unit = after(reduce_weight.T.astype(bf16), e_z[0])
    r_z = [plan.along_z(r_unit, k) for k in range(1, nz)]

    biases = jnp.concatenate([paired_bias.reshape(-1), hidden_bias])
    by_core = plan.core(after(biases, attn_z[0]))
    other_pair = by_core[: 2 * quarter].reshape(2, quarter)
    near = jnp.where(
        core_zero,
        jnp.concatenate([paired_bias, other_pair], axis=1),
        jnp.concatenate([other_pair, paired_bias], axis=1),
    )
    far = plan.along_y(near)
    pair_full = jnp.where(
        y == 0, jnp.concatenate([near, far], axis=1), jnp.concatenate([far, near], axis=1)
    )
    hidden_rows = jnp.stack([hidden_bias, by_core[2 * quarter :]])

    marks = lax.dynamic_slice_in_dim(segments, mp * own_rows, own_rows, 0)
    marks = marks + row_length * lax.broadcasted_iota(jnp.int32, marks.shape, 0)
    mark_col = marks.reshape(count, 1)
    mark_row = marks.reshape(count // LANES, LANES)

    spread = jnp.stack([unit] + attn_z)
    spread = jnp.stack([spread, plan.first(spread)])
    spread, *_, meta, mark_col, mark_row, pair_full, hidden_rows = lax.optimization_barrier(
        (spread, e_z[0], meta, mark_col, mark_row, pair_full, hidden_rows)
    )
    attn_w = [spread, after(plan.second(spread), *e_z)]
    e_spread = after(jnp.stack([e_unit] + e_z), attn_w[1])
    e_x = plan.along_x(e_spread)
    attn_w = attn_w + [plan.core(v) for v in attn_w]
    attn_w[1] = after(attn_w[1], e_spread)

    if not plan.direct:
        attn_w = [absolute_attn(plan, jnp.stack(attn_w[:2]), jnp.stack(attn_w[2:]), z, x, y, c)]
        attn_w = attn_w + [meta] * 3

    whole = lambda shape: (shape, lambda i, m: (0,) * len(shape))
    chunk = lambda n: ((CHUNK, n), lambda i, m: (i, 0))
    pieces = 2 * 2 * 2 * nz if plan.direct else 1
    dma = pltpu.SemaphoreType.DMA

    tokens_low, tokens_f32 = SDS((count, width), bf16), SDS((count, width), f32)
    sem_x = dma((2 * steps,))
    buf_low = pltpu.VMEM((count, width), bf16)
    sl, middle, fl, qkv, probs, ctx, attn_full = local_call(
        meta,
        functools.partial(attn_fwd_kernel, plan),
        "attn_fwd",
        [
            (inputs, False),
            (mark_col, True),
            (mark_row, True),
            (norm_params, True),
            (pair_full, True),
            *[(v, False) for v in attn_w],
        ],
        [
            (tokens_low, False),
            (tokens_f32, True),
            (tokens_low, True),
            (SDS((2, count, 3 * cols), bf16), True),
            (SDS((count // LANES * 2, 2 * cols, LANES), bf16), True),
            (tokens_low, True),
            (SDS((2, width, 4 * cols), bf16), True),
        ],
        [buf_low, buf_low, dma((pieces,)), sem_x],
    )

    sl_far = plan.along_y(sl)
    r_spread = jnp.stack([r_unit] + [after(v, sl) for v in r_z])
    r_x = plan.along_x(r_spread)
    e_x = after(e_x, sl)
    ff_w = []
    for near, far in ((e_spread, e_x), (r_spread, r_x)):
        pieces_of = [near, far, plan.core(near), plan.core(far)]
        if not plan.direct:
            pairs = (pieces_of[:2], pieces_of[2:])
            pieces_of = [v for p in pairs for v in (absolute_ff(plan, jnp.stack(p), z, x), meta)]
        ff_w = ff_w + pieces_of

    act_shape = SDS((2, count, part), bf16)
    gh_shape = SDS((2, part), f32)
    sg_send, fed_send, act_far, hg_far, gh_far, cot_far, ff_full = local_call(
        meta,
        functools.partial(ff_kernel, plan, False),
        "ff_far",
        [
            (sl_far, True),
            (cotangent, False),
            (hidden_rows, True),
            *[(v, False) for v in ff_w],
        ],
        [
            (tokens_low, False),
            (tokens_low, False),
            (act_shape, True),
            (act_shape, True),
            (gh_shape, True),
            (tokens_low, True),
            (SDS((2, 2, width, part), bf16), True),
        ],
        [buf_low, buf_low, dma((2, 2, 2 * nz if plan.direct else 1)), sem_x],
    )
    sg_far = plan.along_y(sg_send)
    sg_near, pre_near, act_near, hg_near, gh_near, cot_near = local_call(
        meta,
        functools.partial(ff_kernel, plan, True),
        "ff_near",
        [
            (sl, True),
            (cotangent, False),
            (hidden_rows, True),
            (ff_full, True),
            (middle, True),
        ],
        [
            (tokens_low, True),
            (tokens_low, False),
            (act_shape, True),
            (act_shape, True),
            (gh_shape, True),
            (tokens_low, True),
        ],
        [buf_low, sem_x],
    )

    if plan.direct:
        grad_shapes = [SDS((nz, rows, part), bf16)] * 8
    else:
        grad_shapes = [SDS((width, part), bf16)] * 4
    ff_ins = (sl, sl_far, cot_near, cot_far, act_near, act_far, hg_near, hg_far)
    ff_grads = local_call(
        meta,
        functools.partial(ff_grad_kernel, plan),
        "ff_grad",
        [(v, True) for v in ff_ins],
        [(v, False) for v in grad_shapes],
        [pltpu.VMEM((2, 2, width, part), bf16), dma((2, 4 * nz if plan.direct else 2))],
    )
    if not plan.direct:
        ff_grads = [v for g in ff_grads for v in relative_ff(plan, g, z, x)]

    ff_got = [plan.core(v) for v in ff_grads[4:]]
    sg_far = after(sg_far, ff_grads[0])
    fed_far = plan.along_y(after(fed_send, sg_far))

    bwd_ins = (sg_near, sg_far, middle, cot_near, norm_params, qkv, probs, attn_full)
    dqkv, ml, mg, vec_two, pair_sum = local_call(
        meta,
        functools.partial(attn_bwd_kernel, plan),
        "attn_bwd",
        [(v, True) for v in bwd_ins],
        [
            (SDS((2, count, 3 * cols), bf16), True),
            (tokens_low, True),
            (tokens_f32, True),
            (SDS((8, width), f32), True),
            (SDS((2, width), f32), True),
        ],
        [],
    )

    ff_got[0] = after(ff_got[0], dqkv)
    e_keep, e_send, r_keep, r_send = add_lists(meta, ff_grads[:4], ff_got)
    e_got = plan.along_x(e_send)

    if plan.direct:
        grad_shapes = [SDS((2, 2, half, 4 * cols), bf16)] * (2 * nz)
    else:
        grad_shapes = [SDS((2, width, 4 * cols), bf16)]
    ml = after(ml, e_send, r_send)
    attn_grads = local_call(
        meta,
        functools.partial(attn_grad_kernel, plan),
        "attn_grad",
        [(v, True) for v in (fl, ml, dqkv, ctx)],
        [(v, plan.direct and i < nz) for i, v in enumerate(grad_shapes)],
        [pltpu.VMEM((2, width, 4 * cols), bf16), dma((2, 4 * nz if plan.direct else 1))],
    )
    if not plan.direct:
        both = relative_attn(plan, attn_grads[0], z, x, y, c)
        attn_grads = [v[:, :, k] for v in both for k in range(nz)]
    attn_mine, attn_theirs = list(attn_grads[:nz]), list(attn_grads[nz:])
    attn_theirs[0] = after(attn_theirs[0], fed_far)
    attn_got = [plan.core(v) for v in attn_theirs]

    dqkv_late = after(dqkv, attn_theirs[0])
    ig, vec_one = local_call(
        meta,
        functools.partial(input_grad_kernel, plan),
        "input_grad",
        [
            (inputs, False),
            (mg, True),
            (norm_params, True),
            (dqkv_late, True),
            (attn_full, True),
        ],
        [(tokens_low, False), (SDS((8, width), f32), True)],
        [buf_low, buf_low, sem_x],
    )
    attn_got[0] = after(attn_got[0], ig, e_got)
    attn_keep, attn_send = add_first(meta, attn_mine, attn_got)
    attn_got = plan.second(attn_send)
    r_got = plan.along_x(after(r_send, attn_send))
    pre_far = plan.along_y(after(pre_near, attn_send))
    e_parts = add_parts(meta, e_keep, after(e_got, attn_send))
    e_z = [e_parts[0]] + [plan.along_z(e_parts[k], k) for k in range(1, nz)]
    size = -(-(8 * width + hidden) // (LANES * plan.ndev)) * LANES
    parts_in = (vec_one, vec_two, pair_sum, gh_near, gh_far)
    (vectors,) = local_call(
        meta,
        functools.partial(vectors_kernel, plan),
        "vectors",
        [(v, True) for v in parts_in],
        [(SDS((plan.ndev, 1, size), f32), False)],
        [pltpu.VMEM((plan.ndev, 1, size), f32), dma((1,))],
    )
    got = lax.all_to_all(vectors, AXES, 0, 0, tiled=True)
    local = jnp.sum(got, axis=0)

    attn_got = after(attn_got, local, r_got, *e_z)
    attn_keep, attn_send = add_parts(meta, attn_keep, attn_got)
    attn_got = plan.first(attn_send)
    r_got = after(r_got, attn_send)
    r_parts = add_parts(meta, r_keep, r_got)
    r_z = [r_parts[0]] + [plan.along_z(r_parts[k], k) for k in range(1, nz)]

    pre_in, pre_far = after(pre_near, attn_send), after(pre_far, attn_send)
    out, out_pair = call(
        out_kernel,
        "out_sum",
        (steps,),
        [
            (pre_in, *chunk(width)),
            (fed_far, *chunk(width)),
            (pre_far, *chunk(width)),
            (fed_send, *chunk(width)),
            (norm_params, *whole(norm_params.shape)),
        ],
        [(SDS((count, width), bf16), *chunk(width))] * 2,
        [],
    )(meta, pre_in, fed_far, pre_far, fed_send, norm_params)

    def everywhere(block, by_y):
        blocks = [block, by_y, plan.core(block), plan.core(by_y)]
        return call(
            place_kernel,
            "place",
            (1,),
            [(b, *whole((count, width))) for b in blocks],
            [(SDS((count * nmp, width), bf16), None, None)],
            [dma((4,))],
        )(meta, *blocks)[0]

    outputs = everywhere(out, out_pair)
    attn_parts = add_parts(meta, attn_keep, after(attn_got, outputs, *r_z))

    ff_in = [*e_z, *r_z]
    grad_expand, grad_reduce, ff_square = call(
        ff_total_kernel,
        "ff_total",
        (1,),
        [(v, *whole(v.shape)) for v in ff_in],
        [
            (SDS((rows, part), f32), *whole((rows, part))),
            (SDS((rows, part), f32), *whole((rows, part))),
            (SDS((1, 1), f32), *whole((1, 1))),
        ],
        [],
    )(meta, *ff_in)

    ig = after(ig, attn_parts[0])
    ig_pair = plan.along_y(ig)
    attn_z = [attn_parts[0]] + [plan.along_z(attn_parts[k], k) for k in range(1, nz)]
    total_in = attn_z + [ff_square, local]
    keep, send, payload = call(
        total_kernel,
        "total",
        (1,),
        [(v, *whole(v.shape)) for v in total_in],
        [
            (SDS((half, 2 * cols), f32), *whole((half, 2 * cols))),
            (SDS((half, 2 * cols), f32), *whole((half, 2 * cols))),
            (
                SDS((plan.ndev, 1, size + LANES), f32),
                *whole((plan.ndev, 1, size + LANES)),
            ),
        ],
        [],
    )(meta, *total_in)
    by_core = plan.core(send)
    ig_pair = after(ig_pair, keep)
    input_gradient = everywhere(ig, ig_pair)
    got = after(lax.all_to_all(payload, AXES, 0, 0, tiled=True), input_gradient)

    if not plan.direct:
        low, high = jnp.where(core_zero, keep, by_core), jnp.where(core_zero, by_core, keep)
        shard = jnp.concatenate([low, high], axis=0).reshape(rows, 4, quarter)
        keep = shard[:, :3].transpose(1, 0, 2)
        by_core = shard[:, 3].T

    matrix, vector = (LR_MATRIX, DECAY), (LR_VECTOR, 0.0)
    groups = [
        [triple_weight, triple_first, triple_second, keep],
        [outward_weight, outward_first, outward_second, by_core],
        [expand_weight, expand_first, expand_second, grad_expand],
        [reduce_weight.T, reduce_first.T, reduce_second.T, grad_reduce],
        [norm_params, norm_first, norm_second],
        [paired_bias, paired_first, paired_second],
        [hidden_bias, hidden_first, hidden_second],
    ]
    flat = [got] + [v for group in groups for v in group]
    new_shapes = [SDS(group[0].shape, f32) for group in groups for _ in range(3)]
    new_shapes.append(SDS((1, 1), f32))
    new = call(
        functools.partial(adam_kernel, plan, (matrix,) * 4 + (vector,) * 3),
        "adam",
        (1,),
        [(v, *whole(v.shape)) for v in flat],
        [(s, *whole(s.shape)) for s in new_shapes],
        [],
        vmem=60,
    )(meta, *flat)
    new = list(new)
    gradient_norm = new.pop().reshape(())
    new[9:12] = [v.T for v in new[9:12]]
    return (outputs, input_gradient, gradient_norm, *new)


def turn(plan, value, z, axis):
    value = jnp.flip(value, axis)
    return jnp.roll(value, z + 1, axis)


def unturn(plan, value, z, axis):
    return jnp.roll(value, -z, axis)


def swap(value, flag, axis):
    return jnp.where(flag == 1, jnp.flip(value, axis), value)


def absolute_ff(plan, value, z, x):
    value = swap(turn(plan, value, z, 1), x, 0)
    return value.transpose(1, 0, 2, 3).reshape(plan.width, plan.part)


def relative_ff(plan, value, z, x):
    value = value.reshape(plan.nz, 2, plan.rows, plan.part).transpose(1, 0, 2, 3)
    value = unturn(plan, swap(value, x, 0), z, 1)
    return value[0], value[1]


def absolute_attn(plan, own, other, z, x, y, c):
    zero = jnp.where(c == 0, own, other)
    one = jnp.where(c == 0, other, own).transpose(1, 0, 2, 3, 4)
    value = jnp.stack([zero, one])
    value = turn(plan, swap(swap(value, y, 1), x, 2), z, 3)
    value = value.transpose(1, 3, 2, 0, 4, 5)
    return value.reshape(2, plan.width, 4 * plan.cols)


def relative_attn(plan, value, z, x, y, c):
    value = value.reshape(2, plan.nz, 2, 2, plan.half, 4 * plan.cols)
    value = value.transpose(3, 0, 2, 1, 4, 5)
    value = unturn(plan, swap(swap(value, y, 1), x, 2), z, 3)
    zero, one = value[0], value[1].transpose(1, 0, 2, 3, 4)
    return jnp.where(c == 0, zero, one), jnp.where(c == 0, one, zero)


def solution(mesh):
    tokens = P("dp", None)
    triple = P(None, "dp", "mp")
    tall = P("mp", "dp")
    wide = P("dp", "mp")
    pair = P(None, "mp")
    states = ((triple,) * 3, (tall,) * 3, (wide,) * 3, (tall,) * 3, (P(),) * 3, (pair,) * 3)
    states = sum(states, ()) + (P("mp"),) * 3
    return jax.shard_map(
        per_device,
        mesh=mesh,
        in_specs=(tokens,) * 3 + states,
        out_specs=(tokens, tokens, P()) + states,
        check_vma=False,
    )
```

```python
import functools

import jax
import jax.numpy as jnp
from jax import lax
from jax.experimental import pallas as pl
from jax.experimental.pallas import tpu as pltpu
from jax.sharding import PartitionSpec as P

HD = 64
STEP = 5
EPS_NORM = 1e-06
BETA = 0.5
LR_MATRIX = 0.03
LR_VECTOR = 0.2
DECAY = 0.1
ADAM_EPS = 1e-08
CLIP = 1.0
NEG = -1e30
GELU_C = 0.7978845608028654
GELU_K = 0.044715

f32 = jnp.float32
bf16 = jnp.bfloat16
AXES = ("dp", "mp")
LANES = 128
CHUNK = 256
MIB = 1 << 20


def mm(left, right):
    return lax.dot_general(left, right, (((1,), (0,)), ((), ())), preferred_element_type=f32)


def mm_nt(left, right):
    return lax.dot_general(left, right, (((1,), (1,)), ((), ())), preferred_element_type=f32)


def mm_tn(left, right):
    return lax.dot_general(left, right, (((0,), (0,)), ((), ())), preferred_element_type=f32)


def norm_stats(rows_in):
    centred = rows_in - jnp.mean(rows_in, axis=-1, keepdims=True)
    scaled = lax.rsqrt(jnp.mean(centred * centred, axis=-1, keepdims=True) + EPS_NORM)
    return centred * scaled, scaled


def norm_backward(upstream, normal_rows, scaled, gain_row):
    gained = upstream * gain_row
    mean_one = jnp.mean(gained, axis=-1, keepdims=True)
    mean_two = jnp.mean(gained * normal_rows, axis=-1, keepdims=True)
    return scaled * (gained - mean_one - normal_rows * mean_two)


def lane_low(shape):
    return lax.broadcasted_iota(jnp.int32, shape, 1) % LANES < HD


def split_heads(block):
    low = lane_low(block.shape)
    zero = jnp.zeros_like(block)
    return jnp.concatenate([jnp.where(low, block, zero), jnp.where(low, zero, block)], axis=0)


def join_heads(stacked):
    half = stacked.shape[0] // 2
    low = lane_low((half, stacked.shape[1]))
    return jnp.where(low, stacked[:half], stacked[half:])


class Plan:
    def __init__(self, ndp, nmp, width, hidden):
        assert ndp % 2 == 0 and nmp == 4
        self.ndev = ndp * nmp
        self.nz = ndp // 2
        self.rows = width // ndp
        self.half = self.rows // 2
        self.width = width
        self.cols = width // 2
        self.part = hidden // nmp
        self.direct = self.half % 16 == 0

    def perm(self, move):
        pairs = []
        for z in range(self.nz):
            for x in range(2):
                for y in range(2):
                    for c in range(2):
                        there = move(z, x, y, c)
                        pairs.append((self.index(z, x, y, c), self.index(*there)))
        return pairs

    def index(self, z, x, y, c):
        return (2 * z + x) * 4 + 2 * y + c

    def core(self, value):
        return lax.ppermute(value, AXES, self.perm(lambda z, x, y, c: (z, x, y, 1 - c)))

    def along_x(self, value):
        return lax.ppermute(value, AXES, self.perm(lambda z, x, y, c: (z, 1 - x, y, c)))

    def along_y(self, value):
        return lax.ppermute(value, AXES, self.perm(lambda z, x, y, c: (z, x, 1 - y, c)))

    def along_z(self, value, step):
        return lax.ppermute(
            value, AXES, self.perm(lambda z, x, y, c: ((z + step) % self.nz, x, y, c))
        )

    def first(self, value):
        return lax.ppermute(
            value,
            AXES,
            self.perm(lambda z, x, y, c: (z, x, 1 - y, c) if c else (z, 1 - x, y, c)),
        )

    def second(self, value):
        return lax.ppermute(
            value,
            AXES,
            self.perm(lambda z, x, y, c: (z, 1 - x, y, c) if c else (z, x, 1 - y, c)),
        )


def piece_spot(plan, meta, r, fy, fx, k, sign):
    z, x, y, c = meta[1], meta[2], meta[3], meta[4]
    cc = jnp.bitwise_xor(c, r)
    zz = lax.rem(z + sign * k + plan.nz, plan.nz)
    xx = jnp.bitwise_xor(x, fx)
    yy = jnp.bitwise_xor(y, fy)
    return cc, zz, xx, yy


def attn_weight_copies(plan, meta, srcs, w, sem, lanes):
    if not plan.direct:
        return [pltpu.make_async_copy(srcs[0].at[:, :, lanes], w, sem.at[0])]
    copies = []
    for s2 in range(2):
        for r in range(2):
            for s1 in range(2):
                for k in range(plan.nz):
                    cc = jnp.bitwise_xor(meta[4], r)
                    fx = jnp.where(cc == 0, s1, s2)
                    fy = jnp.where(cc == 0, s2, s1)
                    _, zz, xx, yy = piece_spot(plan, meta, r, fy, fx, k, -1)
                    row = pl.multiple_of((zz * 2 + xx) * plan.rows + cc * plan.half, 16)
                    copies.append(
                        pltpu.make_async_copy(
                            srcs[2 * r + s2].at[s1, k, :, lanes],
                            w.at[yy, pl.ds(row, plan.half), :],
                            sem.at[len(copies)],
                        )
                    )
    return copies


def token_copy(src, block, dst, sem):
    count = dst.shape[0]
    return pltpu.make_async_copy(
        src.at[pl.ds(pl.multiple_of(block * count, 16), count), :], dst, sem
    )


def chunks(count, body):
    def step(i, carry):
        body(i, pl.ds(pl.multiple_of(i * CHUNK, CHUNK), CHUNK))
        return carry

    lax.fori_loop(0, count // CHUNK, step, 0)


def lanes_of(base, b, cols, p):
    return slice(base + b * cols + p * LANES, base + b * cols + (p + 1) * LANES)


def attn_prep_kernel(meta, x_all, np_ref, x_ref, fl_ref, sem):
    load = token_copy(x_all, meta[0], x_ref, sem.at[0])
    load.start()
    load.wait()

    def body(i, at):
        normal, _ = norm_stats(x_ref[at, :].astype(f32))
        fl_ref[at, :] = (normal * np_ref[0:1, :] + np_ref[1:2, :]).astype(bf16)

    chunks(x_ref.shape[0], body)


def attn_fwd_kernel(plan, meta, x_ref, fl_ref, segc_ref, segr_ref, np_ref, pb_ref, *refs):
    srcs, refs = refs[:4], refs[4:]
    sl_ref, mid_ref, qkv_ref, p_ref, ctx_ref, w, sl_buf, sem, sem_x = refs
    cols = plan.cols
    count = x_ref.shape[0]
    copies = attn_weight_copies(plan, meta, srcs, w, sem, slice(None))
    for copy in copies:
        copy.start()
    for copy in copies:
        copy.wait()
    tiles = CHUNK // LANES
    pairs = cols // LANES

    def second(i, at):
        for y in range(2):
            for part in range(3):
                lanes = slice(part * cols, (part + 1) * cols)
                got = mm(fl_ref[at, :], w[y, :, lanes])
                if part != 1:
                    got = got + pb_ref[part // 2 : part // 2 + 1, y * cols : (y + 1) * cols]
                qkv_ref[y, at, lanes] = got.astype(bf16)
        for t in range(tiles):
            tile = i * tiles + t
            tok = pl.ds(pl.multiple_of(tile * LANES, LANES), LANES)
            same = segc_ref[tok, :] == segr_ref[pl.ds(tile, 1), :]
            same = jnp.concatenate([same] * (2 * pairs), axis=0)
            for y in range(2):
                s = jnp.concatenate(
                    [
                        mm_nt(
                            split_heads(qkv_ref[y, tok, lanes_of(0, 0, cols, p)]),
                            qkv_ref[y, tok, lanes_of(0, 1, cols, p)],
                        )
                        for p in range(pairs)
                    ],
                    axis=0,
                )
                s = jnp.where(same, s * HD**-0.5, NEG)
                e = jnp.exp(s - jnp.max(s, axis=-1, keepdims=True))
                probs = (e * (1.0 / jnp.sum(e, axis=-1, keepdims=True))).astype(bf16)
                p_ref[tile * 2 + y] = probs
                for p in range(pairs):
                    own = probs[p * 2 * LANES : (p + 1) * 2 * LANES]
                    ctx = join_heads(mm(own, qkv_ref[y, tok, lanes_of(0, 2, cols, p)]))
                    ctx_ref[tok, lanes_of(y * cols, 0, cols, p)] = ctx.astype(bf16)
        attended = mm_nt(ctx_ref[at, 0:cols], w[0, :, 3 * cols :])
        attended = attended + mm_nt(ctx_ref[at, cols:], w[1, :, 3 * cols :])
        middle = x_ref[at, :].astype(f32) + attended + np_ref[4:5, :]
        mid_ref[at, :] = middle
        normal, _ = norm_stats(middle)
        sl = (normal * np_ref[2:3, :] + np_ref[3:4, :]).astype(bf16)
        sl_buf[at, :] = sl
        pltpu.make_async_copy(sl_buf.at[at, :], sl_ref.at[at, :], sem_x.at[i]).start()

    chunks(count, second)
    for i in range(count // CHUNK):
        at = pl.ds(i * CHUNK, CHUNK)
        pltpu.make_async_copy(sl_buf.at[at, :], sl_ref.at[at, :], sem_x.at[i]).wait()


def ff_weight_copies(plan, meta, srcs, w, sem, r, e):
    src = srcs[4 * e + 2 * r : 4 * e + 2 * r + 2]
    if not plan.direct:
        return [pltpu.make_async_copy(src[0], w.at[e, r], sem.at[r, e, 0])]
    copies = []
    for fx in range(2):
        for k in range(plan.nz):
            _, zz, xx, _ = piece_spot(plan, meta, r, 0, fx, k, -1)
            row = pl.multiple_of((zz * 2 + xx) * plan.rows, 16)
            copies.append(
                pltpu.make_async_copy(
                    src[fx].at[k],
                    w.at[e, r, pl.ds(row, plan.rows), :],
                    sem.at[r, e, len(copies)],
                )
            )
    return copies


def ff_kernel(plan, own, meta, sl_ref, cot_all, hb_ref, *refs):
    copies = []
    if own:
        w, mid_ref, sg_ref, fed_ref, act_ref, hg_ref, gh_ref, cot_ref, buf, sem_x = refs
    else:
        *srcs, sg_ref, fed_ref, act_ref, hg_ref, gh_ref, cot_ref, w, sg_buf, buf, sem, sem_x = refs
        for r in range(2):
            for e in range(2):
                copies = copies + ff_weight_copies(plan, meta, srcs, w, sem, r, e)
    for copy in copies:
        copy.start()
    count = cot_ref.shape[0]
    load = token_copy(cot_all, meta[0 if own else 5], cot_ref, sem_x.at[0])
    load.start()
    gh_ref[...] = jnp.zeros_like(gh_ref)
    load.wait()
    for copy in copies:
        copy.wait()

    def body(i, at):
        sl = sl_ref[at, :]
        cot = cot_ref[at, :]
        total = [None, None]
        for r in range(2):
            h = mm(sl, w[0, r]) + hb_ref[r : r + 1, :]
            grown = mm(cot, w[1, r])
            square = h * h
            half = 0.5 * jnp.tanh(h * (GELU_C + (GELU_C * GELU_K) * square)) + 0.5
            act = h * half
            slope = half + (act - act * half) * (2.0 * GELU_C + (6.0 * GELU_C * GELU_K) * square)
            grown = grown * slope
            gh_ref[r : r + 1, :] += jnp.sum(grown, axis=0, keepdims=True)
            act = act.astype(bf16)
            grown = grown.astype(bf16)
            act_ref[r, at, :] = act
            hg_ref[r, at, :] = grown
            for e, left in enumerate((grown, act)):
                got = mm_nt(left, w[e, r])
                total[e] = got if total[e] is None else total[e] + got
        fed = total[1] + mid_ref[at, :] if own else total[1]
        buf[at, :] = fed.astype(bf16)
        pltpu.make_async_copy(buf.at[at, :], fed_ref.at[at, :], sem_x.at[i]).start()
        if own:
            sg_ref[at, :] = total[0].astype(bf16)
        else:
            sg_buf[at, :] = total[0].astype(bf16)
            pltpu.make_async_copy(
                sg_buf.at[at, :], sg_ref.at[at, :], sem_x.at[count // CHUNK + i]
            ).start()

    chunks(count, body)
    for i in range(count // CHUNK):
        at = pl.ds(i * CHUNK, CHUNK)
        pltpu.make_async_copy(buf.at[at, :], fed_ref.at[at, :], sem_x.at[i]).wait()
        if not own:
            pltpu.make_async_copy(
                sg_buf.at[at, :], sg_ref.at[at, :], sem_x.at[count // CHUNK + i]
            ).wait()


def ff_grad_copies(plan, meta, buf, outs, sem, r):
    if not plan.direct:
        return [
            pltpu.make_async_copy(buf.at[r, e], outs[2 * r + e], sem.at[r, e]) for e in range(2)
        ]
    copies = []
    for e in range(2):
        for fx in range(2):
            for k in range(plan.nz):
                _, zz, xx, _ = piece_spot(plan, meta, r, 0, fx, k, 1)
                row = pl.multiple_of((zz * 2 + xx) * plan.rows, 16)
                copies.append(
                    pltpu.make_async_copy(
                        buf.at[r, e, pl.ds(row, plan.rows), :],
                        outs[4 * r + 2 * e + fx].at[k],
                        sem.at[r, len(copies)],
                    )
                )
    return copies


def ff_grad_kernel(plan, meta, sl_a, sl_b, cot_a, cot_b, act_a, act_b, hg_a, hg_b, *rest):
    *outs, buf, sem = rest
    for r in (1, 0):
        for e, (a, b, one, two) in enumerate(
            ((sl_a, sl_b, hg_a, hg_b), (cot_a, cot_b, act_a, act_b))
        ):
            buf[r, e] = (mm_tn(a[...], one[r]) + mm_tn(b[...], two[r])).astype(bf16)
        for copy in ff_grad_copies(plan, meta, buf, outs, sem, r):
            copy.start()
    for r in range(2):
        for copy in ff_grad_copies(plan, meta, buf, outs, sem, r):
            copy.wait()


def attn_bwd_kernel(
    plan,
    meta,
    sga_ref,
    sgb_ref,
    mid_ref,
    cot_ref,
    np_ref,
    qkv_ref,
    p_ref,
    w,
    dqkv_ref,
    ml_ref,
    mg_ref,
    vec_ref,
    pair_ref,
):
    cols = plan.cols
    tiles = CHUNK // LANES
    pairs = cols // LANES
    vec_ref[...] = jnp.zeros_like(vec_ref)
    pair_ref[...] = jnp.zeros_like(pair_ref)

    def body(i, at):
        sg = sga_ref[at, :].astype(f32) + sgb_ref[at, :].astype(f32)
        cot = cot_ref[at, :].astype(f32)
        normal, scaled = norm_stats(mid_ref[at, :])
        mg = cot + norm_backward(sg, normal, scaled, np_ref[2:3, :])
        mg_ref[at, :] = mg
        ml = mg.astype(bf16)
        ml_ref[at, :] = ml
        vec_ref[0:1, :] += jnp.sum(sg * normal, axis=0, keepdims=True)
        vec_ref[1:2, :] += jnp.sum(sg, axis=0, keepdims=True)
        vec_ref[2:3, :] += jnp.sum(mg, axis=0, keepdims=True)
        vec_ref[3:4, :] += jnp.sum(cot, axis=0, keepdims=True)
        for y in range(2):
            dctx = mm(ml, w[y, :, 3 * cols :]).astype(bf16)
            for t in range(tiles):
                tile = i * tiles + t
                tok = pl.ds(pl.multiple_of(tile * LANES, LANES), LANES)
                dcs = [
                    split_heads(dctx[t * LANES : (t + 1) * LANES, lanes_of(0, 0, cols, p)])
                    for p in range(pairs)
                ]
                low = p_ref[tile * 2 + y]
                probs = low.astype(f32)
                dp = jnp.concatenate(
                    [
                        mm_nt(dcs[p], qkv_ref[y, tok, lanes_of(0, 2, cols, p)])
                        for p in range(pairs)
                    ],
                    axis=0,
                )
                inner = jnp.sum(dp * probs, axis=-1, keepdims=True)
                ds = (probs * (dp - inner) * HD**-0.5).astype(bf16)
                for p in range(pairs):
                    at_q, at_k, at_v = (lanes_of(0, b, cols, p) for b in range(3))
                    rows = slice(p * 2 * LANES, (p + 1) * 2 * LANES)
                    qs = split_heads(qkv_ref[y, tok, at_q])
                    dq = join_heads(mm(ds[rows], qkv_ref[y, tok, at_k])).astype(bf16)
                    dqkv_ref[y, tok, at_q] = dq
                    dqkv_ref[y, tok, at_k] = mm_tn(ds[rows], qs).astype(bf16)
                    dqkv_ref[y, tok, at_v] = mm_tn(low[rows], dcs[p]).astype(bf16)
            for b in (0, 2):
                lanes = slice(b * cols, (b + 1) * cols)
                pair_ref[b // 2 : b // 2 + 1, y * cols : (y + 1) * cols] += jnp.sum(
                    dqkv_ref[y, at, lanes].astype(f32), axis=0, keepdims=True
                )

    chunks(sga_ref.shape[0], body)


def attn_grad_pieces(plan, meta, buf, outs, sem, fy):
    if not plan.direct:
        yy = jnp.bitwise_xor(meta[3], fy)
        return [pltpu.make_async_copy(buf.at[fy], outs[0].at[yy], sem.at[fy, 0])]
    copies = []
    for r in range(2):
        for fx in range(2):
            for k in range(plan.nz):
                cc, zz, xx, _ = piece_spot(plan, meta, r, fy, fx, k, 1)
                s1 = jnp.where(cc == 0, fx, fy)
                s2 = jnp.where(cc == 0, fy, fx)
                row = pl.multiple_of((zz * 2 + xx) * plan.rows + cc * plan.half, 16)
                out = outs[r * plan.nz + k]
                if r == 0:
                    out[s2, s1] = buf[fy, pl.ds(row, plan.half), :]
                else:
                    copies.append(
                        pltpu.make_async_copy(
                            buf.at[fy, pl.ds(row, plan.half), :],
                            out.at[s2, s1],
                            sem.at[fy, len(copies)],
                        )
                    )
    return copies


def attn_grad_kernel(plan, meta, fl_ref, ml_ref, dqkv_ref, ctx_ref, *rest):
    *outs, buf, sem = rest
    cols = plan.cols
    copies = []
    for fy in range(2):
        y = jnp.bitwise_xor(meta[3], fy)
        lanes = pl.ds(pl.multiple_of(y * cols, LANES), cols)
        buf[fy, :, : 3 * cols] = mm_tn(fl_ref[...], dqkv_ref[y]).astype(bf16)
        buf[fy, :, 3 * cols :] = mm_tn(ml_ref[...], ctx_ref[:, lanes]).astype(bf16)
        some = attn_grad_pieces(plan, meta, buf, outs, sem, fy)
        for copy in some:
            copy.start()
        copies = copies + some
    for copy in copies:
        copy.wait()


def input_grad_kernel(
    plan, meta, x_ref, mg_ref, np_ref, dqkv_ref, w, ig_ref, vec_ref, buf, sem
):
    cols = plan.cols
    count = x_ref.shape[0]
    vec_ref[...] = jnp.zeros_like(vec_ref)

    def body(i, at):
        normal, scaled = norm_stats(x_ref[at, :].astype(f32))
        fg = mm_nt(dqkv_ref[0, at, :], w[0, :, : 3 * cols])
        fg = fg + mm_nt(dqkv_ref[1, at, :], w[1, :, : 3 * cols])
        vec_ref[0:1, :] += jnp.sum(fg * normal, axis=0, keepdims=True)
        vec_ref[1:2, :] += jnp.sum(fg, axis=0, keepdims=True)
        ig = mg_ref[at, :] + norm_backward(fg, normal, scaled, np_ref[0:1, :])
        buf[at, :] = ig.astype(bf16)
        pltpu.make_async_copy(buf.at[at, :], ig_ref.at[at, :], sem.at[i]).start()

    chunks(count, body)
    for i in range(count // CHUNK):
        at = pl.ds(i * CHUNK, CHUNK)
        pltpu.make_async_copy(buf.at[at, :], ig_ref.at[at, :], sem.at[i]).wait()


def add_kernel(meta, left, right, *outs):
    for i, out in enumerate(outs):
        out[...] = (left[i].astype(f32) + right[i].astype(f32)).astype(out.dtype)


def add_parts(meta, left, right):
    n, size = left.shape[0], left.shape[-1]
    shape = left.shape[1:]
    left, right = left.reshape(n, -1, size), right.reshape(n, -1, size)
    length = left.shape[1]
    blocks = 4 if length % 64 == 0 and length >= 384 else 1
    step = length // blocks
    outs = call(
        add_kernel,
        "add_parts",
        (blocks,),
        [(v, (n, step, size), lambda i, m: (0, i, 0)) for v in (left, right)],
        [(jax.ShapeDtypeStruct((length, size), bf16), (step, size), lambda i, m: (i, 0))] * n,
        [],
    )(meta, left, right)
    return [v.reshape(shape) for v in outs]


def sums_kernel(meta, *refs):
    n = len(refs) // 3
    for left, right, out in zip(refs[:n], refs[n : 2 * n], refs[2 * n :]):
        out[...] = (left[...].astype(f32) + right[...].astype(f32)).astype(out.dtype)


def add_lists(meta, left, right):
    n, shape = len(left), left[0].shape
    flat = [v.reshape(-1, shape[-1]) for v in (*left, *right)]
    length, size = flat[0].shape
    blocks = 2 if length % 32 == 0 and length >= 384 else 1
    block = ((length // blocks, size), lambda i, m: (i, 0))
    outs = call(
        sums_kernel,
        "add_lists",
        (blocks,),
        [(v, *block) for v in flat],
        [(jax.ShapeDtypeStruct((length, size), bf16), *block)] * n,
        [],
    )(meta, *flat)
    return [v.reshape(shape) for v in outs]


def first_kernel(n, meta, *refs):
    left, right, (keep, send, got, buf, sem) = refs[:n], refs[n : 2 * n], refs[2 * n :]
    loads = [pltpu.make_async_copy(right[k], got.at[k], sem.at[k]) for k in range(n)]
    for load in loads:
        load.start()
    for k in range(n):
        loads[k].wait()
        for s, out in enumerate((keep, buf)):
            for i in range(out.shape[0]):
                out[i, k] = (left[k][s, i].astype(f32) + got[k, s, i].astype(f32)).astype(bf16)
    store = pltpu.make_async_copy(buf, send, sem.at[n])
    store.start()
    store.wait()


def add_first(meta, left, right):
    n, shape = len(left), left[0].shape[1:]
    out = jax.ShapeDtypeStruct((shape[0], n, *shape[1:]), bf16)
    return local_call(
        meta,
        functools.partial(first_kernel, n),
        "add_first",
        [(v, True) for v in left] + [(v, False) for v in right],
        [(out, True), (out, False)],
        [
            pltpu.VMEM((n, 2, *shape), bf16),
            pltpu.VMEM(out.shape, bf16),
            pltpu.SemaphoreType.DMA((n + 1,)),
        ],
    )


def vectors_kernel(plan, meta, one, two, pair, near, far, out, buf, sem):
    buf[...] = jnp.zeros_like(buf)
    per = buf.shape[2] // LANES
    lines = plan.width // LANES

    def put(start, row):
        for q in range(row.shape[1] // LANES):
            b = start + q
            at = slice(b % per * LANES, (b % per + 1) * LANES)
            buf[b // per, :, at] = row[:, q * LANES : (q + 1) * LANES]

    for i in range(2):
        put(i * lines, one[i : i + 1, :])
        put((6 + i) * lines, pair[i : i + 1, :])
    for i in range(4):
        put((2 + i) * lines, two[i : i + 1, :])
    total = near[...] + far[...]
    for y in range(2):
        for c in range(2):

            @pl.when((meta[3] == y) & (meta[4] == c))
            def _():
                for r in range(2):
                    m = 2 * y + (c + r) % 2
                    put(8 * lines + m * plan.part // LANES, total[r : r + 1, :])

    copy = pltpu.make_async_copy(buf, out, sem.at[0])
    copy.start()
    copy.wait()


def ff_total_kernel(meta, *refs):
    *parts, expand, reduce, square = refs
    half = len(parts) // 2
    sums = None
    for out, some in ((expand, parts[:half]), (reduce, parts[half:])):
        total = some[0][...].astype(f32)
        for part in some[1:]:
            total = total + part[...].astype(f32)
        out[...] = total
        line = jnp.sum(total * total, axis=0, keepdims=True)
        sums = line if sums is None else sums + line
    square[...] = jnp.sum(sums, axis=1, keepdims=True)


def total_kernel(meta, *refs):
    *parts, ff_square, local, keep, send, payload = refs
    total = parts[0][...].astype(f32)
    for part in parts[1:]:
        total = total + part[...].astype(f32)
    quarter = total.shape[1] // 8
    for core in range(2):
        for out, c in ((keep, core), (send, 1 - core)):

            @pl.when(meta[4] == core)
            def _():
                for b in range(4):
                    at = (2 * b + c) * quarter
                    out[:, b * quarter : (b + 1) * quarter] = total[:, at : at + quarter]

    square = jnp.sum(total * total) + jnp.sum(ff_square[...]) + jnp.sum(local[...] * local[...])
    size = local.shape[1]
    count = payload.shape[0]
    payload[:, :, :size] = jnp.broadcast_to(local[...][None], (count, 1, size))
    payload[:, :, size:] = jnp.full((count, 1, LANES), square, f32)


def out_kernel(meta, pre_a, fed_a, pre_b, fed_b, np_ref, out_a, out_b):
    for pre, fed, out in ((pre_a, fed_a, out_a), (pre_b, fed_b, out_b)):
        total = pre[...].astype(f32) + fed[...].astype(f32) + np_ref[5:6, :]
        out[...] = total.astype(bf16)


def place_kernel(meta, own, by_y, by_c, by_yc, out, sem):
    count = own.shape[0]
    copies = []
    for fy, fc, src in ((0, 0, own), (1, 0, by_y), (0, 1, by_c), (1, 1, by_yc)):
        at = jnp.bitwise_xor(meta[3], fy) * 2 + jnp.bitwise_xor(meta[4], fc)
        dst = out.at[pl.ds(pl.multiple_of(at * count, 16), count), :]
        copies.append(pltpu.make_async_copy(src, dst, sem.at[len(copies)]))
    for copy in copies:
        copy.start()
    for copy in copies:
        copy.wait()


def adam_kernel(plan, rates, meta, got, *refs):
    per = got.shape[2] // LANES - 1
    total = jnp.sum(got[:, 0, per * LANES :], axis=0, keepdims=True)[:, 0:1]
    norm = jnp.sqrt(total)
    refs[-1][...] = norm
    factor = jnp.minimum(1.0, CLIP / norm)
    correction = 1.0 - BETA**STEP
    width, quarter, part = plan.width, plan.width // 4, plan.part

    def line(start, length):
        spots = range(start // LANES, (start + length) // LANES)
        return jnp.concatenate(
            [got[b // per, :, b % per * LANES : (b % per + 1) * LANES] for b in spots],
            axis=1,
        )

    def owned(pick):
        value = pick(0)
        for m in range(1, 4):
            value = jnp.where(meta[0] == m, pick(m), value)
        return value

    pairs = [line((6 + i) * width, width) for i in range(2)]
    small = (
        jnp.concatenate([line(i * width, width) for i in range(6)], axis=0),
        jnp.concatenate(
            [owned(lambda m: v[:, m * quarter : (m + 1) * quarter]) for v in pairs], axis=0
        ),
        owned(lambda m: line(8 * width + m * part, part)),
    )
    ins, outs = refs[: 4 * 4 + 3 * 3], refs[4 * 4 + 3 * 3 : -1]
    attn = {}
    if plan.direct:
        mine, other = ins[3][...], ins[7][...]
        low = jnp.where(meta[4] == 0, mine, other)
        high = jnp.where(meta[4] == 0, other, mine)
        for p in range(4):
            at = slice(p * quarter, (p + 1) * quarter)
            attn[p] = jnp.concatenate([low[:, at], high[:, at]], axis=0)
    for i, (rate, decay) in enumerate(rates):
        if i < 4:
            w_ref, m_ref, s_ref, g_ref = ins[4 * i : 4 * i + 4]
            if plan.direct and i < 2:
                g_ref = attn if i == 0 else {Ellipsis: attn[3].T}
        else:
            w_ref, m_ref, s_ref = ins[3 * i + 4 : 3 * i + 7]
            g_ref = {Ellipsis: small[i - 4]}
        m_out, s_out, w_out = outs[3 * i : 3 * i + 3]
        planes = range(w_ref.shape[0]) if len(w_ref.shape) == 3 else (Ellipsis,)
        for p in planes:
            clipped = g_ref[p] * factor
            shape = w_ref[p].shape
            weight, first, second = (
                v[p].reshape(clipped.shape) for v in (w_ref, m_ref, s_ref)
            )
            first = BETA * first + (1.0 - BETA) * clipped
            second = BETA * second + (1.0 - BETA) * clipped * clipped
            direction = first / correction / (jnp.sqrt(second / correction) + ADAM_EPS)
            m_out[p] = first.reshape(shape)
            s_out[p] = second.reshape(shape)
            w_out[p] = (weight - rate * (direction + decay * weight)).reshape(shape)


def after(value, *others):
    return lax.optimization_barrier((value, *others))[0]


def any_spec():
    return pl.BlockSpec(memory_space=pl.ANY)


def local_call(meta, kernel, name, ins, outs, scratch, vmem=16):
    def space(item):
        return pltpu.VMEM if item[1] else pltpu.HBM

    def place(item):
        return item[0] if item[1] else pltpu.with_memory_space_constraint(item[0], pltpu.HBM)

    kernel_call = pl.pallas_call(
        kernel,
        name=name,
        out_shape=[space(o)(o[0].shape, o[0].dtype) for o in outs],
        in_specs=[pl.BlockSpec(memory_space=s) for s in (pltpu.SMEM, *map(space, ins))],
        out_specs=[pl.BlockSpec(memory_space=space(o)) for o in outs],
        scratch_shapes=scratch,
        compiler_params=pltpu.CompilerParams(vmem_limit_bytes=vmem * MIB),
        cost_estimate=pl.CostEstimate(flops=1, bytes_accessed=1, transcendentals=0),
    )
    return kernel_call(meta, *map(place, ins))


def call(kernel, name, grid, ins, outs, scratch, vmem=16):
    def spec(item):
        if item[1] is None:
            return any_spec()
        return pl.BlockSpec(item[1], item[2])

    return pl.pallas_call(
        kernel,
        name=name,
        out_shape=[o[0] for o in outs],
        grid_spec=pltpu.PrefetchScalarGridSpec(
            num_scalar_prefetch=1,
            grid=grid,
            in_specs=[spec(i) for i in ins],
            out_specs=[spec(o) for o in outs],
            scratch_shapes=scratch,
        ),
        compiler_params=pltpu.CompilerParams(vmem_limit_bytes=vmem * MIB),
        cost_estimate=pl.CostEstimate(flops=1, bytes_accessed=1, transcendentals=0),
    )


def per_device(
    inputs,
    segments,
    cotangent,
    triple_weight,
    triple_first,
    triple_second,
    outward_weight,
    outward_first,
    outward_second,
    expand_weight,
    expand_first,
    expand_second,
    reduce_weight,
    reduce_first,
    reduce_second,
    norm_params,
    norm_first,
    norm_second,
    paired_bias,
    paired_first,
    paired_second,
    hidden_bias,
    hidden_first,
    hidden_second,
):
    ndp, nmp = lax.axis_size("dp"), lax.axis_size("mp")
    width = inputs.shape[1]
    hidden = hidden_bias.shape[0] * nmp
    plan = Plan(ndp, nmp, width, hidden)
    nz, rows, half, cols, part = plan.nz, plan.rows, plan.half, plan.cols, plan.part
    count = inputs.shape[0] // nmp
    row_count, row_length = segments.shape
    own_rows = row_count // nmp
    steps = count // CHUNK
    quarter = cols // 2

    dp, mp = lax.axis_index("dp"), lax.axis_index("mp")
    z, x, y, c = dp // 2, dp % 2, mp // 2, mp % 2
    meta = jnp.stack([mp, z, x, y, c, jnp.bitwise_xor(mp, 2)]).astype(jnp.int32)
    core_zero = c == 0
    SDS = jax.ShapeDtypeStruct

    shard = jnp.concatenate(
        [triple_weight.astype(bf16), outward_weight.T.astype(bf16)[None]], axis=0
    ).transpose(1, 0, 2)
    keep = lax.dynamic_slice_in_dim(shard, c * half, half, 0)
    send = lax.dynamic_slice_in_dim(shard, (1 - c) * half, half, 0)
    got = plan.core(send)
    low = jnp.where(core_zero, keep, got)
    high = jnp.where(core_zero, got, keep)
    unit = jnp.concatenate([low, high], axis=2).reshape(half, 4 * cols)
    attn_z = [plan.along_z(unit, k) for k in range(nz - 1, 0, -1)][::-1]

    e_unit = after(expand_weight.astype(bf16), attn_z[0])
    e_z = [plan.along_z(e_unit, k) for k in range(1, nz)]
    r_unit = after(reduce_weight.T.astype(bf16), e_z[0])
    r_z = [plan.along_z(r_unit, k) for k in range(1, nz)]

    biases = jnp.concatenate([paired_bias.reshape(-1), hidden_bias])
    by_core = plan.core(after(biases, attn_z[0]))
    other_pair = by_core[: 2 * quarter].reshape(2, quarter)
    near = jnp.where(
        core_zero,
        jnp.concatenate([paired_bias, other_pair], axis=1),
        jnp.concatenate([other_pair, paired_bias], axis=1),
    )
    far = plan.along_y(near)
    pair_full = jnp.where(
        y == 0, jnp.concatenate([near, far], axis=1), jnp.concatenate([far, near], axis=1)
    )
    hidden_rows = jnp.stack([hidden_bias, by_core[2 * quarter :]])

    marks = lax.dynamic_slice_in_dim(segments, mp * own_rows, own_rows, 0)
    marks = marks + row_length * lax.broadcasted_iota(jnp.int32, marks.shape, 0)
    mark_col = marks.reshape(count, 1)
    mark_row = marks.reshape(count // LANES, LANES)

    spread = jnp.stack([unit] + attn_z)
    spread = jnp.stack([spread, plan.first(spread)])
    spread, *_, meta, mark_col, mark_row, pair_full, hidden_rows = lax.optimization_barrier(
        (spread, e_z[0], meta, mark_col, mark_row, pair_full, hidden_rows)
    )
    dma = pltpu.SemaphoreType.DMA
    tokens_low, tokens_f32 = SDS((count, width), bf16), SDS((count, width), f32)
    sem_x = dma((2 * steps,))
    buf_low = pltpu.VMEM((count, width), bf16)
    own_x, fl = local_call(
        meta,
        attn_prep_kernel,
        "attn_prep",
        [(inputs, False), (norm_params, True)],
        [(tokens_low, True), (tokens_low, True)],
        [sem_x],
    )
    attn_w = [spread, after(plan.second(spread), fl, *e_z)]
    e_spread = after(jnp.stack([e_unit] + e_z), attn_w[1])
    e_x = plan.along_x(e_spread)
    attn_w = attn_w + [plan.core(v) for v in attn_w]
    attn_w[1] = after(attn_w[1], e_spread)

    if not plan.direct:
        attn_w = [absolute_attn(plan, jnp.stack(attn_w[:2]), jnp.stack(attn_w[2:]), z, x, y, c)]
        attn_w = attn_w + [meta] * 3

    whole = lambda shape: (shape, lambda i, m: (0,) * len(shape))
    chunk = lambda n: ((CHUNK, n), lambda i, m: (i, 0))
    pieces = 2 * 2 * 2 * nz if plan.direct else 1

    sl, middle, qkv, probs, ctx, attn_full = local_call(
        meta,
        functools.partial(attn_fwd_kernel, plan),
        "attn_fwd",
        [
            (own_x, True),
            (fl, True),
            (mark_col, True),
            (mark_row, True),
            (norm_params, True),
            (pair_full, True),
            *[(v, False) for v in attn_w],
        ],
        [
            (tokens_low, False),
            (tokens_f32, True),
            (SDS((2, count, 3 * cols), bf16), True),
            (SDS((count // LANES * 2, 2 * cols, LANES), bf16), True),
            (tokens_low, True),
            (SDS((2, width, 4 * cols), bf16), True),
        ],
        [buf_low, dma((pieces,)), sem_x],
    )

    sl_far = plan.along_y(sl)
    r_spread = jnp.stack([r_unit] + [after(v, sl) for v in r_z])
    r_x = plan.along_x(r_spread)
    e_x = after(e_x, sl)
    ff_w = []
    for near, far in ((e_spread, e_x), (r_spread, r_x)):
        pieces_of = [near, far, plan.core(near), plan.core(far)]
        if not plan.direct:
            pairs = (pieces_of[:2], pieces_of[2:])
            pieces_of = [v for p in pairs for v in (absolute_ff(plan, jnp.stack(p), z, x), meta)]
        ff_w = ff_w + pieces_of

    act_shape = SDS((2, count, part), bf16)
    gh_shape = SDS((2, part), f32)
    sg_send, fed_send, act_far, hg_far, gh_far, cot_far, ff_full = local_call(
        meta,
        functools.partial(ff_kernel, plan, False),
        "ff_far",
        [
            (sl_far, True),
            (cotangent, False),
            (hidden_rows, True),
            *[(v, False) for v in ff_w],
        ],
        [
            (tokens_low, False),
            (tokens_low, False),
            (act_shape, True),
            (act_shape, True),
            (gh_shape, True),
            (tokens_low, True),
            (SDS((2, 2, width, part), bf16), True),
        ],
        [buf_low, buf_low, dma((2, 2, 2 * nz if plan.direct else 1)), sem_x],
    )
    sg_far = plan.along_y(sg_send)
    sg_near, pre_near, act_near, hg_near, gh_near, cot_near = local_call(
        meta,
        functools.partial(ff_kernel, plan, True),
        "ff_near",
        [
            (sl, True),
            (cotangent, False),
            (hidden_rows, True),
            (ff_full, True),
            (middle, True),
        ],
        [
            (tokens_low, True),
            (tokens_low, False),
            (act_shape, True),
            (act_shape, True),
            (gh_shape, True),
            (tokens_low, True),
        ],
        [buf_low, sem_x],
    )

    if plan.direct:
        grad_shapes = [SDS((nz, rows, part), bf16)] * 8
    else:
        grad_shapes = [SDS((width, part), bf16)] * 4
    ff_ins = (sl, sl_far, cot_near, cot_far, act_near, act_far, hg_near, hg_far)
    ff_grads = local_call(
        meta,
        functools.partial(ff_grad_kernel, plan),
        "ff_grad",
        [(v, True) for v in ff_ins],
        [(v, False) for v in grad_shapes],
        [pltpu.VMEM((2, 2, width, part), bf16), dma((2, 4 * nz if plan.direct else 2))],
    )
    if not plan.direct:
        ff_grads = [v for g in ff_grads for v in relative_ff(plan, g, z, x)]

    ff_got = [plan.core(v) for v in ff_grads[4:]]
    sg_far = after(sg_far, ff_grads[0])
    fed_far = plan.along_y(after(fed_send, sg_far))

    bwd_ins = (sg_near, sg_far, middle, cot_near, norm_params, qkv, probs, attn_full)
    dqkv, ml, mg, vec_two, pair_sum = local_call(
        meta,
        functools.partial(attn_bwd_kernel, plan),
        "attn_bwd",
        [(v, True) for v in bwd_ins],
        [
            (SDS((2, count, 3 * cols), bf16), True),
            (tokens_low, True),
            (tokens_f32, True),
            (SDS((8, width), f32), True),
            (SDS((2, width), f32), True),
        ],
        [],
    )

    ff_got[0] = after(ff_got[0], dqkv)
    e_keep, e_send, r_keep, r_send = add_lists(meta, ff_grads[:4], ff_got)
    e_got = plan.along_x(e_send)

    if plan.direct:
        grad_shapes = [SDS((2, 2, half, 4 * cols), bf16)] * (2 * nz)
    else:
        grad_shapes = [SDS((2, width, 4 * cols), bf16)]
    ml = after(ml, e_send, r_send)
    attn_grads = local_call(
        meta,
        functools.partial(attn_grad_kernel, plan),
        "attn_grad",
        [(v, True) for v in (fl, ml, dqkv, ctx)],
        [(v, plan.direct and i < nz) for i, v in enumerate(grad_shapes)],
        [pltpu.VMEM((2, width, 4 * cols), bf16), dma((2, 4 * nz if plan.direct else 1))],
    )
    if not plan.direct:
        both = relative_attn(plan, attn_grads[0], z, x, y, c)
        attn_grads = [v[:, :, k] for v in both for k in range(nz)]
    attn_mine, attn_theirs = list(attn_grads[:nz]), list(attn_grads[nz:])
    attn_theirs[0] = after(attn_theirs[0], fed_far)
    attn_got = [plan.core(v) for v in attn_theirs]

    dqkv_late = after(dqkv, attn_theirs[0])
    ig, vec_one = local_call(
        meta,
        functools.partial(input_grad_kernel, plan),
        "input_grad",
        [
            (own_x, True),
            (mg, True),
            (norm_params, True),
            (dqkv_late, True),
            (attn_full, True),
        ],
        [(tokens_low, False), (SDS((8, width), f32), True)],
        [buf_low, sem_x],
    )
    attn_got[0] = after(attn_got[0], ig, e_got)
    attn_keep, attn_send = add_first(meta, attn_mine, attn_got)
    attn_got = plan.second(attn_send)
    r_got = plan.along_x(after(r_send, attn_send))
    e_parts = add_parts(meta, e_keep, after(e_got, attn_send))
    e_z = [e_parts[0]] + [plan.along_z(e_parts[k], k) for k in range(1, nz)]
    size = -(-(8 * width + hidden) // (LANES * plan.ndev)) * LANES
    parts_in = (vec_one, vec_two, pair_sum, gh_near, gh_far)
    (vectors,) = local_call(
        meta,
        functools.partial(vectors_kernel, plan),
        "vectors",
        [(v, True) for v in parts_in],
        [(SDS((plan.ndev, 1, size), f32), False)],
        [pltpu.VMEM((plan.ndev, 1, size), f32), dma((1,))],
    )
    got = lax.all_to_all(vectors, AXES, 0, 0, tiled=True)
    local = jnp.sum(got, axis=0)

    attn_got = after(attn_got, local, r_got, *e_z)
    attn_keep, attn_send = add_parts(meta, attn_keep, attn_got)
    attn_got = plan.first(attn_send)
    pre_far = plan.along_y(after(pre_near, attn_send))
    r_got = after(r_got, attn_send)
    r_parts = add_parts(meta, r_keep, r_got)
    r_z = [r_parts[0]] + [plan.along_z(r_parts[k], k) for k in range(1, nz)]

    attn_parts = add_parts(meta, attn_keep, after(attn_got, *r_z))

    ff_in = [*e_z, *r_z]
    grad_expand, grad_reduce, ff_square = call(
        ff_total_kernel,
        "ff_total",
        (1,),
        [(v, *whole(v.shape)) for v in ff_in],
        [
            (SDS((rows, part), f32), *whole((rows, part))),
            (SDS((rows, part), f32), *whole((rows, part))),
            (SDS((1, 1), f32), *whole((1, 1))),
        ],
        [],
    )(meta, *ff_in)

    ig = after(ig, attn_parts[0])
    ig_pair = plan.along_y(ig)
    attn_z = [attn_parts[0]] + [plan.along_z(attn_parts[k], k) for k in range(1, nz)]
    pre_in, pre_far = pre_near, after(pre_far, attn_z[1])
    out, out_pair = call(
        out_kernel,
        "out_sum",
        (steps,),
        [
            (pre_in, *chunk(width)),
            (fed_far, *chunk(width)),
            (pre_far, *chunk(width)),
            (fed_send, *chunk(width)),
            (norm_params, *whole(norm_params.shape)),
        ],
        [(SDS((count, width), bf16), *chunk(width))] * 2,
        [],
    )(meta, pre_in, fed_far, pre_far, fed_send, norm_params)
    total_in = attn_z + [ff_square, after(local, out)]
    def everywhere(block, by_y):
        blocks = [block, by_y, plan.core(block), plan.core(by_y)]
        return call(
            place_kernel,
            "place",
            (1,),
            [(b, *whole((count, width))) for b in blocks],
            [(SDS((count * nmp, width), bf16), None, None)],
            [dma((4,))],
        )(meta, *blocks)[0]

    keep, send, payload = call(
        total_kernel,
        "total",
        (1,),
        [(v, *whole(v.shape)) for v in total_in],
        [
            (SDS((half, 2 * cols), f32), *whole((half, 2 * cols))),
            (SDS((half, 2 * cols), f32), *whole((half, 2 * cols))),
            (
                SDS((plan.ndev, 1, size + LANES), f32),
                *whole((plan.ndev, 1, size + LANES)),
            ),
        ],
        [],
    )(meta, *total_in)
    by_core = plan.core(send)
    ig_pair = after(ig_pair, keep)
    outputs = everywhere(out, out_pair)
    input_gradient = everywhere(ig, ig_pair)
    got = after(lax.all_to_all(payload, AXES, 0, 0, tiled=True), input_gradient, outputs)

    if not plan.direct:
        low, high = jnp.where(core_zero, keep, by_core), jnp.where(core_zero, by_core, keep)
        shard = jnp.concatenate([low, high], axis=0).reshape(rows, 4, quarter)
        keep = shard[:, :3].transpose(1, 0, 2)
        by_core = shard[:, 3].T

    matrix, vector = (LR_MATRIX, DECAY), (LR_VECTOR, 0.0)
    groups = [
        [triple_weight, triple_first, triple_second, keep],
        [outward_weight, outward_first, outward_second, by_core],
        [expand_weight, expand_first, expand_second, grad_expand],
        [reduce_weight.T, reduce_first.T, reduce_second.T, grad_reduce],
        [norm_params, norm_first, norm_second],
        [paired_bias, paired_first, paired_second],
        [hidden_bias, hidden_first, hidden_second],
    ]
    flat = [got] + [v for group in groups for v in group]
    new_shapes = [SDS(group[0].shape, f32) for group in groups for _ in range(3)]
    new_shapes.append(SDS((1, 1), f32))
    new = call(
        functools.partial(adam_kernel, plan, (matrix,) * 4 + (vector,) * 3),
        "adam",
        (1,),
        [(v, *whole(v.shape)) for v in flat],
        [(s, *whole(s.shape)) for s in new_shapes],
        [],
        vmem=60,
    )(meta, *flat)
    new = list(new)
    gradient_norm = new.pop().reshape(())
    new[9:12] = [v.T for v in new[9:12]]
    return (outputs, input_gradient, gradient_norm, *new)


def turn(plan, value, z, axis):
    value = jnp.flip(value, axis)
    return jnp.roll(value, z + 1, axis)


def unturn(plan, value, z, axis):
    return jnp.roll(value, -z, axis)


def swap(value, flag, axis):
    return jnp.where(flag == 1, jnp.flip(value, axis), value)


def absolute_ff(plan, value, z, x):
    value = swap(turn(plan, value, z, 1), x, 0)
    return value.transpose(1, 0, 2, 3).reshape(plan.width, plan.part)


def relative_ff(plan, value, z, x):
    value = value.reshape(plan.nz, 2, plan.rows, plan.part).transpose(1, 0, 2, 3)
    value = unturn(plan, swap(value, x, 0), z, 1)
    return value[0], value[1]


def absolute_attn(plan, own, other, z, x, y, c):
    zero = jnp.where(c == 0, own, other)
    one = jnp.where(c == 0, other, own).transpose(1, 0, 2, 3, 4)
    value = jnp.stack([zero, one])
    value = turn(plan, swap(swap(value, y, 1), x, 2), z, 3)
    value = value.transpose(1, 3, 2, 0, 4, 5)
    return value.reshape(2, plan.width, 4 * plan.cols)


def relative_attn(plan, value, z, x, y, c):
    value = value.reshape(2, plan.nz, 2, 2, plan.half, 4 * plan.cols)
    value = value.transpose(3, 0, 2, 1, 4, 5)
    value = unturn(plan, swap(swap(value, y, 1), x, 2), z, 3)
    zero, one = value[0], value[1].transpose(1, 0, 2, 3, 4)
    return jnp.where(c == 0, zero, one), jnp.where(c == 0, one, zero)


def solution(mesh):
    tokens = P("dp", None)
    triple = P(None, "dp", "mp")
    tall = P("mp", "dp")
    wide = P("dp", "mp")
    pair = P(None, "mp")
    states = ((triple,) * 3, (tall,) * 3, (wide,) * 3, (tall,) * 3, (P(),) * 3, (pair,) * 3)
    states = sum(states, ()) + (P("mp"),) * 3
    return jax.shard_map(
        per_device,
        mesh=mesh,
        in_specs=(tokens,) * 3 + states,
        out_specs=(tokens, tokens, P()) + states,
        check_vma=False,
    )
```

```python
import functools

import jax
import jax.numpy as jnp
from jax import lax
from jax.experimental import pallas as pl
from jax.experimental.pallas import tpu as pltpu
from jax.sharding import PartitionSpec as P

HD = 64
STEP = 5
EPS_NORM = 1e-06
BETA = 0.5
LR_MATRIX = 0.03
LR_VECTOR = 0.2
DECAY = 0.1
ADAM_EPS = 1e-08
CLIP = 1.0
NEG = -1e30
GELU_C = 0.7978845608028654
GELU_K = 0.044715

f32 = jnp.float32
bf16 = jnp.bfloat16
AXES = ("dp", "mp")
LANES = 128
CHUNK = 256
MIB = 1 << 20


def mm(left, right):
    return lax.dot_general(left, right, (((1,), (0,)), ((), ())), preferred_element_type=f32)


def mm_nt(left, right):
    return lax.dot_general(left, right, (((1,), (1,)), ((), ())), preferred_element_type=f32)


def mm_tn(left, right):
    return lax.dot_general(left, right, (((0,), (0,)), ((), ())), preferred_element_type=f32)


def norm_stats(rows_in):
    centred = rows_in - jnp.mean(rows_in, axis=-1, keepdims=True)
    scaled = lax.rsqrt(jnp.mean(centred * centred, axis=-1, keepdims=True) + EPS_NORM)
    return centred * scaled, scaled


def norm_backward(upstream, normal_rows, scaled, gain_row):
    gained = upstream * gain_row
    mean_one = jnp.mean(gained, axis=-1, keepdims=True)
    mean_two = jnp.mean(gained * normal_rows, axis=-1, keepdims=True)
    return scaled * (gained - mean_one - normal_rows * mean_two)


def lane_low(shape):
    return lax.broadcasted_iota(jnp.int32, shape, 1) % LANES < HD


def split_heads(block):
    low = lane_low(block.shape)
    zero = jnp.zeros_like(block)
    return jnp.concatenate([jnp.where(low, block, zero), jnp.where(low, zero, block)], axis=0)


def join_heads(stacked):
    half = stacked.shape[0] // 2
    low = lane_low((half, stacked.shape[1]))
    return jnp.where(low, stacked[:half], stacked[half:])


class Plan:
    def __init__(self, ndp, nmp, width, hidden):
        assert ndp % 2 == 0 and nmp == 4
        self.ndev = ndp * nmp
        self.nz = ndp // 2
        self.rows = width // ndp
        self.half = self.rows // 2
        self.width = width
        self.cols = width // 2
        self.part = hidden // nmp
        self.direct = self.half % 16 == 0

    def perm(self, move):
        pairs = []
        for z in range(self.nz):
            for x in range(2):
                for y in range(2):
                    for c in range(2):
                        there = move(z, x, y, c)
                        pairs.append((self.index(z, x, y, c), self.index(*there)))
        return pairs

    def index(self, z, x, y, c):
        return (2 * z + x) * 4 + 2 * y + c

    def core(self, value):
        return lax.ppermute(value, AXES, self.perm(lambda z, x, y, c: (z, x, y, 1 - c)))

    def along_x(self, value):
        return lax.ppermute(value, AXES, self.perm(lambda z, x, y, c: (z, 1 - x, y, c)))

    def along_y(self, value):
        return lax.ppermute(value, AXES, self.perm(lambda z, x, y, c: (z, x, 1 - y, c)))

    def along_z(self, value, step):
        return lax.ppermute(
            value, AXES, self.perm(lambda z, x, y, c: ((z + step) % self.nz, x, y, c))
        )

    def first(self, value):
        return lax.ppermute(
            value,
            AXES,
            self.perm(lambda z, x, y, c: (z, x, 1 - y, c) if c else (z, 1 - x, y, c)),
        )

    def second(self, value):
        return lax.ppermute(
            value,
            AXES,
            self.perm(lambda z, x, y, c: (z, 1 - x, y, c) if c else (z, x, 1 - y, c)),
        )


def piece_spot(plan, meta, r, fy, fx, k, sign):
    z, x, y, c = meta[1], meta[2], meta[3], meta[4]
    cc = jnp.bitwise_xor(c, r)
    zz = lax.rem(z + sign * k + plan.nz, plan.nz)
    xx = jnp.bitwise_xor(x, fx)
    yy = jnp.bitwise_xor(y, fy)
    return cc, zz, xx, yy


def attn_weight_copies(plan, meta, srcs, w, sem, lanes):
    if not plan.direct:
        return [pltpu.make_async_copy(srcs[0].at[:, :, lanes], w, sem.at[0])]
    copies = []
    for s2 in range(2):
        for r in range(2):
            for s1 in range(2):
                for k in range(plan.nz):
                    cc = jnp.bitwise_xor(meta[4], r)
                    fx = jnp.where(cc == 0, s1, s2)
                    fy = jnp.where(cc == 0, s2, s1)
                    _, zz, xx, yy = piece_spot(plan, meta, r, fy, fx, k, -1)
                    row = pl.multiple_of((zz * 2 + xx) * plan.rows + cc * plan.half, 16)
                    copies.append(
                        pltpu.make_async_copy(
                            srcs[2 * r + s2].at[s1, k, :, lanes],
                            w.at[yy, pl.ds(row, plan.half), :],
                            sem.at[len(copies)],
                        )
                    )
    return copies


def token_copy(src, block, dst, sem):
    count = dst.shape[0]
    return pltpu.make_async_copy(
        src.at[pl.ds(pl.multiple_of(block * count, 16), count), :], dst, sem
    )


def chunks(count, body):
    def step(i, carry):
        body(i, pl.ds(pl.multiple_of(i * CHUNK, CHUNK), CHUNK))
        return carry

    lax.fori_loop(0, count // CHUNK, step, 0)


def lanes_of(base, b, cols, p):
    return slice(base + b * cols + p * LANES, base + b * cols + (p + 1) * LANES)


def attn_prep_kernel(meta, x_all, np_ref, x_ref, fl_ref, sem):
    load = token_copy(x_all, meta[0], x_ref, sem.at[0])
    load.start()
    load.wait()

    def body(i, at):
        normal, _ = norm_stats(x_ref[at, :].astype(f32))
        fl_ref[at, :] = (normal * np_ref[0:1, :] + np_ref[1:2, :]).astype(bf16)

    chunks(x_ref.shape[0], body)


def attn_fwd_kernel(plan, meta, x_ref, fl_ref, segc_ref, segr_ref, np_ref, pb_ref, *refs):
    srcs, refs = refs[:4], refs[4:]
    sl_ref, mid_ref, qkv_ref, p_ref, ctx_ref, w, sl_buf, sem, sem_x = refs
    cols = plan.cols
    count = x_ref.shape[0]
    copies = attn_weight_copies(plan, meta, srcs, w, sem, slice(None))
    for copy in copies:
        copy.start()
    for copy in copies:
        copy.wait()
    tiles = CHUNK // LANES
    pairs = cols // LANES

    def second(i, at):
        for y in range(2):
            for part in range(3):
                lanes = slice(part * cols, (part + 1) * cols)
                got = mm(fl_ref[at, :], w[y, :, lanes])
                if part != 1:
                    got = got + pb_ref[part // 2 : part // 2 + 1, y * cols : (y + 1) * cols]
                qkv_ref[y, at, lanes] = got.astype(bf16)
        for t in range(tiles):
            tile = i * tiles + t
            tok = pl.ds(pl.multiple_of(tile * LANES, LANES), LANES)
            same = segc_ref[tok, :] == segr_ref[pl.ds(tile, 1), :]
            same = jnp.concatenate([same] * (2 * pairs), axis=0)
            for y in range(2):
                s = jnp.concatenate(
                    [
                        mm_nt(
                            split_heads(qkv_ref[y, tok, lanes_of(0, 0, cols, p)]),
                            qkv_ref[y, tok, lanes_of(0, 1, cols, p)],
                        )
                        for p in range(pairs)
                    ],
                    axis=0,
                )
                s = jnp.where(same, s * HD**-0.5, NEG)
                e = jnp.exp(s - jnp.max(s, axis=-1, keepdims=True))
                probs = (e * (1.0 / jnp.sum(e, axis=-1, keepdims=True))).astype(bf16)
                p_ref[tile * 2 + y] = probs
                for p in range(pairs):
                    own = probs[p * 2 * LANES : (p + 1) * 2 * LANES]
                    ctx = join_heads(mm(own, qkv_ref[y, tok, lanes_of(0, 2, cols, p)]))
                    ctx_ref[tok, lanes_of(y * cols, 0, cols, p)] = ctx.astype(bf16)
        attended = mm_nt(ctx_ref[at, 0:cols], w[0, :, 3 * cols :])
        attended = attended + mm_nt(ctx_ref[at, cols:], w[1, :, 3 * cols :])
        middle = x_ref[at, :].astype(f32) + attended + np_ref[4:5, :]
        mid_ref[at, :] = middle
        normal, _ = norm_stats(middle)
        sl = (normal * np_ref[2:3, :] + np_ref[3:4, :]).astype(bf16)
        sl_buf[at, :] = sl
        pltpu.make_async_copy(sl_buf.at[at, :], sl_ref.at[at, :], sem_x.at[i]).start()

    chunks(count, second)
    for i in range(count // CHUNK):
        at = pl.ds(i * CHUNK, CHUNK)
        pltpu.make_async_copy(sl_buf.at[at, :], sl_ref.at[at, :], sem_x.at[i]).wait()


def ff_weight_copies(plan, meta, srcs, w, sem, r, e):
    src = srcs[4 * e + 2 * r : 4 * e + 2 * r + 2]
    if not plan.direct:
        return [pltpu.make_async_copy(src[0], w.at[e, r], sem.at[r, e, 0])]
    copies = []
    for fx in range(2):
        for k in range(plan.nz):
            _, zz, xx, _ = piece_spot(plan, meta, r, 0, fx, k, -1)
            row = pl.multiple_of((zz * 2 + xx) * plan.rows, 16)
            copies.append(
                pltpu.make_async_copy(
                    src[fx].at[k],
                    w.at[e, r, pl.ds(row, plan.rows), :],
                    sem.at[r, e, len(copies)],
                )
            )
    return copies


def ff_kernel(plan, own, meta, sl_ref, cot_all, hb_ref, *refs):
    copies = []
    if own:
        w, mid_ref, sg_ref, fed_ref, act_ref, hg_ref, gh_ref, cot_ref, buf, sem_x = refs
    else:
        *srcs, sg_ref, fed_ref, act_ref, hg_ref, gh_ref, cot_ref, w, sg_buf, buf, sem, sem_x = refs
        for r in range(2):
            for e in range(2):
                copies = copies + ff_weight_copies(plan, meta, srcs, w, sem, r, e)
    for copy in copies:
        copy.start()
    count = cot_ref.shape[0]
    load = token_copy(cot_all, meta[0 if own else 5], cot_ref, sem_x.at[0])
    load.start()
    gh_ref[...] = jnp.zeros_like(gh_ref)
    load.wait()
    for copy in copies:
        copy.wait()

    def body(i, at):
        sl = sl_ref[at, :]
        cot = cot_ref[at, :]
        total = [None, None]
        for r in range(2):
            h = mm(sl, w[0, r]) + hb_ref[r : r + 1, :]
            grown = mm(cot, w[1, r])
            square = h * h
            half = 0.5 * jnp.tanh(h * (GELU_C + (GELU_C * GELU_K) * square)) + 0.5
            act = h * half
            slope = half + (act - act * half) * (2.0 * GELU_C + (6.0 * GELU_C * GELU_K) * square)
            grown = grown * slope
            gh_ref[r : r + 1, :] += jnp.sum(grown, axis=0, keepdims=True)
            act = act.astype(bf16)
            grown = grown.astype(bf16)
            act_ref[r, at, :] = act
            hg_ref[r, at, :] = grown
            for e, left in enumerate((grown, act)):
                got = mm_nt(left, w[e, r])
                total[e] = got if total[e] is None else total[e] + got
        fed = total[1] + mid_ref[at, :] if own else total[1]
        buf[at, :] = fed.astype(bf16)
        pltpu.make_async_copy(buf.at[at, :], fed_ref.at[at, :], sem_x.at[i]).start()
        if own:
            sg_ref[at, :] = total[0].astype(bf16)
        else:
            sg_buf[at, :] = total[0].astype(bf16)
            pltpu.make_async_copy(
                sg_buf.at[at, :], sg_ref.at[at, :], sem_x.at[count // CHUNK + i]
            ).start()

    chunks(count, body)
    for i in range(count // CHUNK):
        at = pl.ds(i * CHUNK, CHUNK)
        pltpu.make_async_copy(buf.at[at, :], fed_ref.at[at, :], sem_x.at[i]).wait()
        if not own:
            pltpu.make_async_copy(
                sg_buf.at[at, :], sg_ref.at[at, :], sem_x.at[count // CHUNK + i]
            ).wait()


def ff_grad_copies(plan, meta, buf, outs, sem, r):
    if not plan.direct:
        return [
            pltpu.make_async_copy(buf.at[r, e], outs[2 * r + e], sem.at[r, e]) for e in range(2)
        ]
    copies = []
    for e in range(2):
        for fx in range(2):
            for k in range(plan.nz):
                _, zz, xx, _ = piece_spot(plan, meta, r, 0, fx, k, 1)
                row = pl.multiple_of((zz * 2 + xx) * plan.rows, 16)
                copies.append(
                    pltpu.make_async_copy(
                        buf.at[r, e, pl.ds(row, plan.rows), :],
                        outs[4 * r + 2 * e + fx].at[k],
                        sem.at[r, len(copies)],
                    )
                )
    return copies


def ff_grad_kernel(plan, meta, sl_a, sl_b, cot_a, cot_b, act_a, act_b, hg_a, hg_b, *rest):
    *outs, buf, sem = rest
    for r in (1, 0):
        for e, (a, b, one, two) in enumerate(
            ((sl_a, sl_b, hg_a, hg_b), (cot_a, cot_b, act_a, act_b))
        ):
            buf[r, e] = (mm_tn(a[...], one[r]) + mm_tn(b[...], two[r])).astype(bf16)
        for copy in ff_grad_copies(plan, meta, buf, outs, sem, r):
            copy.start()
    for r in range(2):
        for copy in ff_grad_copies(plan, meta, buf, outs, sem, r):
            copy.wait()


def attn_bwd_kernel(
    plan,
    meta,
    sga_ref,
    sgb_ref,
    mid_ref,
    cot_ref,
    np_ref,
    qkv_ref,
    p_ref,
    w,
    dqkv_ref,
    ml_ref,
    mg_ref,
    vec_ref,
    pair_ref,
):
    cols = plan.cols
    tiles = CHUNK // LANES
    pairs = cols // LANES
    vec_ref[...] = jnp.zeros_like(vec_ref)
    pair_ref[...] = jnp.zeros_like(pair_ref)

    def body(i, at):
        sg = sga_ref[at, :].astype(f32) + sgb_ref[at, :].astype(f32)
        cot = cot_ref[at, :].astype(f32)
        normal, scaled = norm_stats(mid_ref[at, :])
        mg = cot + norm_backward(sg, normal, scaled, np_ref[2:3, :])
        mg_ref[at, :] = mg
        ml = mg.astype(bf16)
        ml_ref[at, :] = ml
        vec_ref[0:1, :] += jnp.sum(sg * normal, axis=0, keepdims=True)
        vec_ref[1:2, :] += jnp.sum(sg, axis=0, keepdims=True)
        vec_ref[2:3, :] += jnp.sum(mg, axis=0, keepdims=True)
        vec_ref[3:4, :] += jnp.sum(cot, axis=0, keepdims=True)
        for y in range(2):
            dctx = mm(ml, w[y, :, 3 * cols :]).astype(bf16)
            for t in range(tiles):
                tile = i * tiles + t
                tok = pl.ds(pl.multiple_of(tile * LANES, LANES), LANES)
                dcs = [
                    split_heads(dctx[t * LANES : (t + 1) * LANES, lanes_of(0, 0, cols, p)])
                    for p in range(pairs)
                ]
                low = p_ref[tile * 2 + y]
                probs = low.astype(f32)
                dp = jnp.concatenate(
                    [
                        mm_nt(dcs[p], qkv_ref[y, tok, lanes_of(0, 2, cols, p)])
                        for p in range(pairs)
                    ],
                    axis=0,
                )
                inner = jnp.sum(dp * probs, axis=-1, keepdims=True)
                ds = (probs * (dp - inner) * HD**-0.5).astype(bf16)
                for p in range(pairs):
                    at_q, at_k, at_v = (lanes_of(0, b, cols, p) for b in range(3))
                    rows = slice(p * 2 * LANES, (p + 1) * 2 * LANES)
                    qs = split_heads(qkv_ref[y, tok, at_q])
                    dq = join_heads(mm(ds[rows], qkv_ref[y, tok, at_k])).astype(bf16)
                    dqkv_ref[y, tok, at_q] = dq
                    dqkv_ref[y, tok, at_k] = mm_tn(ds[rows], qs).astype(bf16)
                    dqkv_ref[y, tok, at_v] = mm_tn(low[rows], dcs[p]).astype(bf16)
            for b in (0, 2):
                lanes = slice(b * cols, (b + 1) * cols)
                pair_ref[b // 2 : b // 2 + 1, y * cols : (y + 1) * cols] += jnp.sum(
                    dqkv_ref[y, at, lanes].astype(f32), axis=0, keepdims=True
                )

    chunks(sga_ref.shape[0], body)


def attn_grad_pieces(plan, meta, buf, outs, sem, fy):
    if not plan.direct:
        yy = jnp.bitwise_xor(meta[3], fy)
        return [pltpu.make_async_copy(buf.at[fy], outs[0].at[yy], sem.at[fy, 0])]
    copies = []
    for r in range(2):
        for fx in range(2):
            for k in range(plan.nz):
                cc, zz, xx, _ = piece_spot(plan, meta, r, fy, fx, k, 1)
                s1 = jnp.where(cc == 0, fx, fy)
                s2 = jnp.where(cc == 0, fy, fx)
                row = pl.multiple_of((zz * 2 + xx) * plan.rows + cc * plan.half, 16)
                out = outs[r * plan.nz + k]
                if r == 0:
                    out[s2, s1] = buf[fy, pl.ds(row, plan.half), :]
                else:
                    copies.append(
                        pltpu.make_async_copy(
                            buf.at[fy, pl.ds(row, plan.half), :],
                            out.at[s2, s1],
                            sem.at[fy, len(copies)],
                        )
                    )
    return copies


def attn_grad_kernel(plan, meta, fl_ref, ml_ref, dqkv_ref, ctx_ref, *rest):
    *outs, buf, sem = rest
    cols = plan.cols
    copies = []
    for fy in range(2):
        y = jnp.bitwise_xor(meta[3], fy)
        lanes = pl.ds(pl.multiple_of(y * cols, LANES), cols)
        buf[fy, :, : 3 * cols] = mm_tn(fl_ref[...], dqkv_ref[y]).astype(bf16)
        buf[fy, :, 3 * cols :] = mm_tn(ml_ref[...], ctx_ref[:, lanes]).astype(bf16)
        some = attn_grad_pieces(plan, meta, buf, outs, sem, fy)
        for copy in some:
            copy.start()
        copies = copies + some
    for copy in copies:
        copy.wait()


def input_grad_kernel(
    plan, meta, x_ref, mg_ref, np_ref, dqkv_ref, w, ig_ref, vec_ref, buf, sem
):
    cols = plan.cols
    count = x_ref.shape[0]
    vec_ref[...] = jnp.zeros_like(vec_ref)

    def body(i, at):
        normal, scaled = norm_stats(x_ref[at, :].astype(f32))
        fg = mm_nt(dqkv_ref[0, at, :], w[0, :, : 3 * cols])
        fg = fg + mm_nt(dqkv_ref[1, at, :], w[1, :, : 3 * cols])
        vec_ref[0:1, :] += jnp.sum(fg * normal, axis=0, keepdims=True)
        vec_ref[1:2, :] += jnp.sum(fg, axis=0, keepdims=True)
        ig = mg_ref[at, :] + norm_backward(fg, normal, scaled, np_ref[0:1, :])
        buf[at, :] = ig.astype(bf16)
        pltpu.make_async_copy(buf.at[at, :], ig_ref.at[at, :], sem.at[i]).start()

    chunks(count, body)
    for i in range(count // CHUNK):
        at = pl.ds(i * CHUNK, CHUNK)
        pltpu.make_async_copy(buf.at[at, :], ig_ref.at[at, :], sem.at[i]).wait()


def add_kernel(meta, left, right, *outs):
    for i, out in enumerate(outs):
        out[...] = (left[i].astype(f32) + right[i].astype(f32)).astype(out.dtype)


def add_parts(meta, left, right):
    n, size = left.shape[0], left.shape[-1]
    shape = left.shape[1:]
    left, right = left.reshape(n, -1, size), right.reshape(n, -1, size)
    length = left.shape[1]
    blocks = 4 if length % 64 == 0 and length >= 384 else 1
    step = length // blocks
    outs = call(
        add_kernel,
        "add_parts",
        (blocks,),
        [(v, (n, step, size), lambda i, m: (0, i, 0)) for v in (left, right)],
        [(jax.ShapeDtypeStruct((length, size), bf16), (step, size), lambda i, m: (i, 0))] * n,
        [],
    )(meta, left, right)
    return [v.reshape(shape) for v in outs]


def sums_kernel(meta, *refs):
    n = len(refs) // 3
    for left, right, out in zip(refs[:n], refs[n : 2 * n], refs[2 * n :]):
        out[...] = (left[...].astype(f32) + right[...].astype(f32)).astype(out.dtype)


def add_lists(meta, left, right):
    n, shape = len(left), left[0].shape
    flat = [v.reshape(-1, shape[-1]) for v in (*left, *right)]
    length, size = flat[0].shape
    blocks = 2 if length % 32 == 0 and length >= 384 else 1
    block = ((length // blocks, size), lambda i, m: (i, 0))
    outs = call(
        sums_kernel,
        "add_lists",
        (blocks,),
        [(v, *block) for v in flat],
        [(jax.ShapeDtypeStruct((length, size), bf16), *block)] * n,
        [],
    )(meta, *flat)
    return [v.reshape(shape) for v in outs]


def first_kernel(n, meta, *refs):
    left, right, (keep, send, got, buf, sem) = refs[:n], refs[n : 2 * n], refs[2 * n :]
    loads = [pltpu.make_async_copy(right[k], got.at[k], sem.at[k]) for k in range(n)]
    for load in loads:
        load.start()
    for k in range(n):
        loads[k].wait()
        for s, out in enumerate((keep, buf)):
            for i in range(out.shape[0]):
                out[i, k] = (left[k][s, i].astype(f32) + got[k, s, i].astype(f32)).astype(bf16)
    store = pltpu.make_async_copy(buf, send, sem.at[n])
    store.start()
    store.wait()


def add_first(meta, left, right):
    n, shape = len(left), left[0].shape[1:]
    out = jax.ShapeDtypeStruct((shape[0], n, *shape[1:]), bf16)
    return local_call(
        meta,
        functools.partial(first_kernel, n),
        "add_first",
        [(v, True) for v in left] + [(v, False) for v in right],
        [(out, True), (out, False)],
        [
            pltpu.VMEM((n, 2, *shape), bf16),
            pltpu.VMEM(out.shape, bf16),
            pltpu.SemaphoreType.DMA((n + 1,)),
        ],
    )


def vectors_kernel(plan, meta, one, two, pair, near, far, out, buf, sem):
    buf[...] = jnp.zeros_like(buf)
    per = buf.shape[2] // LANES
    lines = plan.width // LANES

    def put(start, row):
        for q in range(row.shape[1] // LANES):
            b = start + q
            at = slice(b % per * LANES, (b % per + 1) * LANES)
            buf[b // per, :, at] = row[:, q * LANES : (q + 1) * LANES]

    for i in range(2):
        put(i * lines, one[i : i + 1, :])
        put((6 + i) * lines, pair[i : i + 1, :])
    for i in range(4):
        put((2 + i) * lines, two[i : i + 1, :])
    total = near[...] + far[...]
    for y in range(2):
        for c in range(2):

            @pl.when((meta[3] == y) & (meta[4] == c))
            def _():
                for r in range(2):
                    m = 2 * y + (c + r) % 2
                    put(8 * lines + m * plan.part // LANES, total[r : r + 1, :])

    copy = pltpu.make_async_copy(buf, out, sem.at[0])
    copy.start()
    copy.wait()


def ff_total_kernel(meta, *refs):
    *parts, expand, reduce, square = refs
    half = len(parts) // 2
    sums = None
    for out, some in ((expand, parts[:half]), (reduce, parts[half:])):
        total = some[0][...].astype(f32)
        for part in some[1:]:
            total = total + part[...].astype(f32)
        out[...] = total
        line = jnp.sum(total * total, axis=0, keepdims=True)
        sums = line if sums is None else sums + line
    square[...] = jnp.sum(sums, axis=1, keepdims=True)


def total_kernel(meta, *refs):
    *parts, ff_square, local, keep, send, payload = refs
    total = parts[0][...].astype(f32)
    for part in parts[1:]:
        total = total + part[...].astype(f32)
    quarter = total.shape[1] // 8
    for core in range(2):
        for out, c in ((keep, core), (send, 1 - core)):

            @pl.when(meta[4] == core)
            def _():
                for b in range(4):
                    at = (2 * b + c) * quarter
                    out[:, b * quarter : (b + 1) * quarter] = total[:, at : at + quarter]

    square = jnp.sum(total * total) + jnp.sum(ff_square[...]) + jnp.sum(local[...] * local[...])
    size = local.shape[1]
    count = payload.shape[0]
    payload[:, :, :size] = jnp.broadcast_to(local[...][None], (count, 1, size))
    payload[:, :, size:] = jnp.full((count, 1, LANES), square, f32)


def out_kernel(meta, pre_a, fed_a, pre_b, fed_b, np_ref, out_a, out_b):
    for pre, fed, out in ((pre_a, fed_a, out_a), (pre_b, fed_b, out_b)):
        total = pre[...].astype(f32) + fed[...].astype(f32) + np_ref[5:6, :]
        out[...] = total.astype(bf16)


def place_kernel(meta, own, by_y, by_c, by_yc, out, sem):
    count = own.shape[0]
    copies = []
    for fy, fc, src in ((0, 0, own), (1, 0, by_y), (0, 1, by_c), (1, 1, by_yc)):
        at = jnp.bitwise_xor(meta[3], fy) * 2 + jnp.bitwise_xor(meta[4], fc)
        dst = out.at[pl.ds(pl.multiple_of(at * count, 16), count), :]
        copies.append(pltpu.make_async_copy(src, dst, sem.at[len(copies)]))
    for copy in copies:
        copy.start()
    for copy in copies:
        copy.wait()


def adam_kernel(plan, rates, meta, got, *refs):
    per = got.shape[2] // LANES - 1
    total = jnp.sum(got[:, 0, per * LANES :], axis=0, keepdims=True)[:, 0:1]
    norm = jnp.sqrt(total)
    results = 3 * len(rates) + 1
    inputs = 4 * 4 + 3 * 3
    sources, finals = refs[:inputs], refs[inputs : inputs + results]
    ins, bufs = refs[inputs + results : -2 - results], refs[-2 - results : -2]
    sem_in, sem_out = refs[-2:]
    loads = [
        pltpu.make_async_copy(source, buf, sem_in.at[i])
        for i, (source, buf) in enumerate(zip(sources, ins))
    ]
    stores = [
        pltpu.make_async_copy(buf, final, sem_out.at[i])
        for i, (buf, final) in enumerate(zip(bufs, finals))
    ]
    for load in loads:
        load.start()
    bufs[-1][...] = norm
    stores[-1].start()
    factor = jnp.minimum(1.0, CLIP / norm)
    correction = 1.0 - BETA**STEP
    width, quarter, part = plan.width, plan.width // 4, plan.part

    def line(start, length):
        spots = range(start // LANES, (start + length) // LANES)
        return jnp.concatenate(
            [got[b // per, :, b % per * LANES : (b % per + 1) * LANES] for b in spots],
            axis=1,
        )

    def owned(pick):
        value = pick(0)
        for m in range(1, 4):
            value = jnp.where(meta[0] == m, pick(m), value)
        return value

    pairs = [line((6 + i) * width, width) for i in range(2)]
    small = (
        jnp.concatenate([line(i * width, width) for i in range(6)], axis=0),
        jnp.concatenate(
            [owned(lambda m: v[:, m * quarter : (m + 1) * quarter]) for v in pairs], axis=0
        ),
        owned(lambda m: line(8 * width + m * part, part)),
    )
    outs = bufs[:-1]
    attn = {}
    for i in (3, 7):
        loads[i].wait()
    if plan.direct:
        mine, other = ins[3][...], ins[7][...]
        low = jnp.where(meta[4] == 0, mine, other)
        high = jnp.where(meta[4] == 0, other, mine)
        for p in range(4):
            at = slice(p * quarter, (p + 1) * quarter)
            attn[p] = jnp.concatenate([low[:, at], high[:, at]], axis=0)
    for i, (rate, decay) in enumerate(rates):
        if i < 4:
            first_in = 4 * i
            w_ref, m_ref, s_ref, g_ref = ins[4 * i : 4 * i + 4]
            if plan.direct and i < 2:
                g_ref = attn if i == 0 else {Ellipsis: attn[3].T}
        else:
            first_in = 3 * i + 4
            w_ref, m_ref, s_ref = ins[3 * i + 4 : 3 * i + 7]
            g_ref = {Ellipsis: small[i - 4]}
        for j in range(first_in, first_in + (4 if i < 4 else 3)):
            if j not in (3, 7):
                loads[j].wait()
        m_out, s_out, w_out = outs[3 * i : 3 * i + 3]
        planes = range(w_ref.shape[0]) if len(w_ref.shape) == 3 else (Ellipsis,)
        for p in planes:
            clipped = g_ref[p] * factor
            shape = w_ref[p].shape
            weight, first, second = (
                v[p].reshape(clipped.shape) for v in (w_ref, m_ref, s_ref)
            )
            first = BETA * first + (1.0 - BETA) * clipped
            second = BETA * second + (1.0 - BETA) * clipped * clipped
            direction = first / correction / (jnp.sqrt(second / correction) + ADAM_EPS)
            m_out[p] = first.reshape(shape)
            s_out[p] = second.reshape(shape)
            w_out[p] = (weight - rate * (direction + decay * weight)).reshape(shape)
        for store in stores[3 * i : 3 * i + 3]:
            store.start()
    for store in stores:
        store.wait()


def after(value, *others):
    return lax.optimization_barrier((value, *others))[0]


def any_spec():
    return pl.BlockSpec(memory_space=pl.ANY)


def local_call(meta, kernel, name, ins, outs, scratch, vmem=16):
    def space(item):
        return pltpu.VMEM if item[1] else pltpu.HBM

    def place(item):
        return item[0] if item[1] else pltpu.with_memory_space_constraint(item[0], pltpu.HBM)

    kernel_call = pl.pallas_call(
        kernel,
        name=name,
        out_shape=[space(o)(o[0].shape, o[0].dtype) for o in outs],
        in_specs=[pl.BlockSpec(memory_space=s) for s in (pltpu.SMEM, *map(space, ins))],
        out_specs=[pl.BlockSpec(memory_space=space(o)) for o in outs],
        scratch_shapes=scratch,
        compiler_params=pltpu.CompilerParams(vmem_limit_bytes=vmem * MIB),
        cost_estimate=pl.CostEstimate(flops=1, bytes_accessed=1, transcendentals=0),
    )
    return kernel_call(meta, *map(place, ins))


def call(kernel, name, grid, ins, outs, scratch, vmem=16):
    def spec(item):
        if item[1] is None:
            return any_spec()
        return pl.BlockSpec(item[1], item[2])

    return pl.pallas_call(
        kernel,
        name=name,
        out_shape=[o[0] for o in outs],
        grid_spec=pltpu.PrefetchScalarGridSpec(
            num_scalar_prefetch=1,
            grid=grid,
            in_specs=[spec(i) for i in ins],
            out_specs=[spec(o) for o in outs],
            scratch_shapes=scratch,
        ),
        compiler_params=pltpu.CompilerParams(vmem_limit_bytes=vmem * MIB),
        cost_estimate=pl.CostEstimate(flops=1, bytes_accessed=1, transcendentals=0),
    )


def per_device(
    inputs,
    segments,
    cotangent,
    triple_weight,
    triple_first,
    triple_second,
    outward_weight,
    outward_first,
    outward_second,
    expand_weight,
    expand_first,
    expand_second,
    reduce_weight,
    reduce_first,
    reduce_second,
    norm_params,
    norm_first,
    norm_second,
    paired_bias,
    paired_first,
    paired_second,
    hidden_bias,
    hidden_first,
    hidden_second,
):
    ndp, nmp = lax.axis_size("dp"), lax.axis_size("mp")
    width = inputs.shape[1]
    hidden = hidden_bias.shape[0] * nmp
    plan = Plan(ndp, nmp, width, hidden)
    nz, rows, half, cols, part = plan.nz, plan.rows, plan.half, plan.cols, plan.part
    count = inputs.shape[0] // nmp
    row_count, row_length = segments.shape
    own_rows = row_count // nmp
    steps = count // CHUNK
    quarter = cols // 2

    dp, mp = lax.axis_index("dp"), lax.axis_index("mp")
    z, x, y, c = dp // 2, dp % 2, mp // 2, mp % 2
    meta = jnp.stack([mp, z, x, y, c, jnp.bitwise_xor(mp, 2)]).astype(jnp.int32)
    core_zero = c == 0
    SDS = jax.ShapeDtypeStruct

    shard = jnp.concatenate(
        [triple_weight.astype(bf16), outward_weight.T.astype(bf16)[None]], axis=0
    ).transpose(1, 0, 2)
    keep = lax.dynamic_slice_in_dim(shard, c * half, half, 0)
    send = lax.dynamic_slice_in_dim(shard, (1 - c) * half, half, 0)
    got = plan.core(send)
    low = jnp.where(core_zero, keep, got)
    high = jnp.where(core_zero, got, keep)
    unit = jnp.concatenate([low, high], axis=2).reshape(half, 4 * cols)
    attn_z = [plan.along_z(unit, k) for k in range(nz - 1, 0, -1)][::-1]

    e_unit = after(expand_weight.astype(bf16), attn_z[0])
    e_z = [plan.along_z(e_unit, k) for k in range(1, nz)]
    r_unit = after(reduce_weight.T.astype(bf16), e_z[0])
    r_z = [plan.along_z(r_unit, k) for k in range(1, nz)]

    biases = jnp.concatenate([paired_bias.reshape(-1), hidden_bias])
    by_core = plan.core(after(biases, attn_z[0]))
    other_pair = by_core[: 2 * quarter].reshape(2, quarter)
    near = jnp.where(
        core_zero,
        jnp.concatenate([paired_bias, other_pair], axis=1),
        jnp.concatenate([other_pair, paired_bias], axis=1),
    )
    far = plan.along_y(near)
    pair_full = jnp.where(
        y == 0, jnp.concatenate([near, far], axis=1), jnp.concatenate([far, near], axis=1)
    )
    hidden_rows = jnp.stack([hidden_bias, by_core[2 * quarter :]])

    marks = lax.dynamic_slice_in_dim(segments, mp * own_rows, own_rows, 0)
    marks = marks + row_length * lax.broadcasted_iota(jnp.int32, marks.shape, 0)
    mark_col = marks.reshape(count, 1)
    mark_row = marks.reshape(count // LANES, LANES)

    spread = jnp.stack([unit] + attn_z)
    spread = jnp.stack([spread, plan.first(spread)])
    spread, *_, meta, mark_col, mark_row, pair_full, hidden_rows = lax.optimization_barrier(
        (spread, e_z[0], meta, mark_col, mark_row, pair_full, hidden_rows)
    )
    dma = pltpu.SemaphoreType.DMA
    tokens_low, tokens_f32 = SDS((count, width), bf16), SDS((count, width), f32)
    sem_x = dma((2 * steps,))
    buf_low = pltpu.VMEM((count, width), bf16)
    own_x, fl = local_call(
        meta,
        attn_prep_kernel,
        "attn_prep",
        [(inputs, False), (norm_params, True)],
        [(tokens_low, True), (tokens_low, True)],
        [sem_x],
    )
    attn_w = [spread, after(plan.second(spread), fl, *e_z)]
    e_spread = after(jnp.stack([e_unit] + e_z), attn_w[1])
    e_x = plan.along_x(e_spread)
    attn_w = attn_w + [plan.core(v) for v in attn_w]
    attn_w[1] = after(attn_w[1], e_spread)

    if not plan.direct:
        attn_w = [absolute_attn(plan, jnp.stack(attn_w[:2]), jnp.stack(attn_w[2:]), z, x, y, c)]
        attn_w = attn_w + [meta] * 3

    whole = lambda shape: (shape, lambda i, m: (0,) * len(shape))
    chunk = lambda n: ((CHUNK, n), lambda i, m: (i, 0))
    pieces = 2 * 2 * 2 * nz if plan.direct else 1

    sl, middle, qkv, probs, ctx, attn_full = local_call(
        meta,
        functools.partial(attn_fwd_kernel, plan),
        "attn_fwd",
        [
            (own_x, True),
            (fl, True),
            (mark_col, True),
            (mark_row, True),
            (norm_params, True),
            (pair_full, True),
            *[(v, False) for v in attn_w],
        ],
        [
            (tokens_low, False),
            (tokens_f32, True),
            (SDS((2, count, 3 * cols), bf16), True),
            (SDS((count // LANES * 2, 2 * cols, LANES), bf16), True),
            (tokens_low, True),
            (SDS((2, width, 4 * cols), bf16), True),
        ],
        [buf_low, dma((pieces,)), sem_x],
    )

    sl_far = plan.along_y(sl)
    r_spread = jnp.stack([r_unit] + [after(v, sl) for v in r_z])
    r_x = plan.along_x(r_spread)
    e_x = after(e_x, sl)
    ff_w = []
    for near, far in ((e_spread, e_x), (r_spread, r_x)):
        pieces_of = [near, far, plan.core(near), plan.core(far)]
        if not plan.direct:
            pairs = (pieces_of[:2], pieces_of[2:])
            pieces_of = [v for p in pairs for v in (absolute_ff(plan, jnp.stack(p), z, x), meta)]
        ff_w = ff_w + pieces_of

    act_shape = SDS((2, count, part), bf16)
    gh_shape = SDS((2, part), f32)
    sg_send, fed_send, act_far, hg_far, gh_far, cot_far, ff_full = local_call(
        meta,
        functools.partial(ff_kernel, plan, False),
        "ff_far",
        [
            (sl_far, True),
            (cotangent, False),
            (hidden_rows, True),
            *[(v, False) for v in ff_w],
        ],
        [
            (tokens_low, False),
            (tokens_low, False),
            (act_shape, True),
            (act_shape, True),
            (gh_shape, True),
            (tokens_low, True),
            (SDS((2, 2, width, part), bf16), True),
        ],
        [buf_low, buf_low, dma((2, 2, 2 * nz if plan.direct else 1)), sem_x],
    )
    sg_far = plan.along_y(sg_send)
    sg_near, pre_near, act_near, hg_near, gh_near, cot_near = local_call(
        meta,
        functools.partial(ff_kernel, plan, True),
        "ff_near",
        [
            (sl, True),
            (cotangent, False),
            (hidden_rows, True),
            (ff_full, True),
            (middle, True),
        ],
        [
            (tokens_low, True),
            (tokens_low, False),
            (act_shape, True),
            (act_shape, True),
            (gh_shape, True),
            (tokens_low, True),
        ],
        [buf_low, sem_x],
    )

    if plan.direct:
        grad_shapes = [SDS((nz, rows, part), bf16)] * 8
    else:
        grad_shapes = [SDS((width, part), bf16)] * 4
    ff_ins = (sl, sl_far, cot_near, cot_far, act_near, act_far, hg_near, hg_far)
    ff_grads = local_call(
        meta,
        functools.partial(ff_grad_kernel, plan),
        "ff_grad",
        [(v, True) for v in ff_ins],
        [(v, False) for v in grad_shapes],
        [pltpu.VMEM((2, 2, width, part), bf16), dma((2, 4 * nz if plan.direct else 2))],
    )
    if not plan.direct:
        ff_grads = [v for g in ff_grads for v in relative_ff(plan, g, z, x)]

    ff_got = [plan.core(v) for v in ff_grads[4:]]
    sg_far = after(sg_far, ff_grads[0])
    fed_far = plan.along_y(after(fed_send, sg_far))

    bwd_ins = (sg_near, sg_far, middle, cot_near, norm_params, qkv, probs, attn_full)
    dqkv, ml, mg, vec_two, pair_sum = local_call(
        meta,
        functools.partial(attn_bwd_kernel, plan),
        "attn_bwd",
        [(v, True) for v in bwd_ins],
        [
            (SDS((2, count, 3 * cols), bf16), True),
            (tokens_low, True),
            (tokens_f32, True),
            (SDS((8, width), f32), True),
            (SDS((2, width), f32), True),
        ],
        [],
    )

    ff_got[0] = after(ff_got[0], dqkv)
    e_keep, e_send, r_keep, r_send = add_lists(meta, ff_grads[:4], ff_got)
    e_got = plan.along_x(e_send)

    if plan.direct:
        grad_shapes = [SDS((2, 2, half, 4 * cols), bf16)] * (2 * nz)
    else:
        grad_shapes = [SDS((2, width, 4 * cols), bf16)]
    ml = after(ml, e_send, r_send)
    attn_grads = local_call(
        meta,
        functools.partial(attn_grad_kernel, plan),
        "attn_grad",
        [(v, True) for v in (fl, ml, dqkv, ctx)],
        [(v, plan.direct and i < nz) for i, v in enumerate(grad_shapes)],
        [pltpu.VMEM((2, width, 4 * cols), bf16), dma((2, 4 * nz if plan.direct else 1))],
    )
    if not plan.direct:
        both = relative_attn(plan, attn_grads[0], z, x, y, c)
        attn_grads = [v[:, :, k] for v in both for k in range(nz)]
    attn_mine, attn_theirs = list(attn_grads[:nz]), list(attn_grads[nz:])
    attn_theirs[0] = after(attn_theirs[0], fed_far)
    attn_got = [plan.core(v) for v in attn_theirs]

    dqkv_late = after(dqkv, attn_theirs[0])
    ig, vec_one = local_call(
        meta,
        functools.partial(input_grad_kernel, plan),
        "input_grad",
        [
            (own_x, True),
            (mg, True),
            (norm_params, True),
            (dqkv_late, True),
            (attn_full, True),
        ],
        [(tokens_low, False), (SDS((8, width), f32), True)],
        [buf_low, sem_x],
    )
    attn_got[0] = after(attn_got[0], ig, e_got)
    attn_keep, attn_send = add_first(meta, attn_mine, attn_got)
    attn_got = plan.second(attn_send)
    r_got = plan.along_x(after(r_send, attn_send))
    e_parts = add_parts(meta, e_keep, after(e_got, attn_send))
    e_z = [e_parts[0]] + [plan.along_z(e_parts[k], k) for k in range(1, nz)]
    size = -(-(8 * width + hidden) // (LANES * plan.ndev)) * LANES
    parts_in = (vec_one, vec_two, pair_sum, gh_near, gh_far)
    (vectors,) = local_call(
        meta,
        functools.partial(vectors_kernel, plan),
        "vectors",
        [(v, True) for v in parts_in],
        [(SDS((plan.ndev, 1, size), f32), False)],
        [pltpu.VMEM((plan.ndev, 1, size), f32), dma((1,))],
    )
    got = lax.all_to_all(vectors, AXES, 0, 0, tiled=True)
    local = jnp.sum(got, axis=0)

    attn_got = after(attn_got, local, r_got, *e_z)
    attn_keep, attn_send = add_parts(meta, attn_keep, attn_got)
    attn_got = plan.first(attn_send)
    pre_far = plan.along_y(after(pre_near, attn_send))
    r_got = after(r_got, attn_send)
    r_parts = add_parts(meta, r_keep, r_got)
    r_z = [r_parts[0]] + [plan.along_z(r_parts[k], k) for k in range(1, nz)]

    attn_parts = add_parts(meta, attn_keep, after(attn_got, *r_z))

    ff_in = [*e_z, *r_z]
    grad_expand, grad_reduce, ff_square = call(
        ff_total_kernel,
        "ff_total",
        (1,),
        [(v, *whole(v.shape)) for v in ff_in],
        [
            (SDS((rows, part), f32), *whole((rows, part))),
            (SDS((rows, part), f32), *whole((rows, part))),
            (SDS((1, 1), f32), *whole((1, 1))),
        ],
        [],
    )(meta, *ff_in)

    ig = after(ig, attn_parts[0])
    ig_pair = plan.along_y(ig)
    attn_z = [attn_parts[0]] + [plan.along_z(attn_parts[k], k) for k in range(1, nz)]
    pre_in, pre_far = pre_near, after(pre_far, attn_z[1])
    out, out_pair = call(
        out_kernel,
        "out_sum",
        (steps,),
        [
            (pre_in, *chunk(width)),
            (fed_far, *chunk(width)),
            (pre_far, *chunk(width)),
            (fed_send, *chunk(width)),
            (norm_params, *whole(norm_params.shape)),
        ],
        [(SDS((count, width), bf16), *chunk(width))] * 2,
        [],
    )(meta, pre_in, fed_far, pre_far, fed_send, norm_params)
    total_in = attn_z + [ff_square, after(local, out)]
    def everywhere(block, by_y):
        blocks = [block, by_y, plan.core(block), plan.core(by_y)]
        return call(
            place_kernel,
            "place",
            (1,),
            [(b, *whole((count, width))) for b in blocks],
            [(SDS((count * nmp, width), bf16), None, None)],
            [dma((4,))],
        )(meta, *blocks)[0]

    keep, send, payload = call(
        total_kernel,
        "total",
        (1,),
        [(v, *whole(v.shape)) for v in total_in],
        [
            (SDS((half, 2 * cols), f32), *whole((half, 2 * cols))),
            (SDS((half, 2 * cols), f32), *whole((half, 2 * cols))),
            (
                SDS((plan.ndev, 1, size + LANES), f32),
                *whole((plan.ndev, 1, size + LANES)),
            ),
        ],
        [],
    )(meta, *total_in)
    by_core = plan.core(send)
    ig_pair = after(ig_pair, keep)
    outputs = everywhere(out, out_pair)
    input_gradient = everywhere(ig, ig_pair)
    got = after(lax.all_to_all(payload, AXES, 0, 0, tiled=True), input_gradient, outputs)

    if not plan.direct:
        low, high = jnp.where(core_zero, keep, by_core), jnp.where(core_zero, by_core, keep)
        shard = jnp.concatenate([low, high], axis=0).reshape(rows, 4, quarter)
        keep = shard[:, :3].transpose(1, 0, 2)
        by_core = shard[:, 3].T

    matrix, vector = (LR_MATRIX, DECAY), (LR_VECTOR, 0.0)
    groups = [
        [triple_weight, triple_first, triple_second, keep],
        [outward_weight, outward_first, outward_second, by_core],
        [expand_weight, expand_first, expand_second, grad_expand],
        [reduce_weight.T, reduce_first.T, reduce_second.T, grad_reduce],
        [norm_params, norm_first, norm_second],
        [paired_bias, paired_first, paired_second],
        [hidden_bias, hidden_first, hidden_second],
    ]
    flat = [got] + [v for group in groups for v in group]
    new_shapes = [SDS(group[0].shape, f32) for group in groups for _ in range(3)]
    new_shapes.append(SDS((1, 1), f32))
    new = local_call(
        meta,
        functools.partial(adam_kernel, plan, (matrix,) * 4 + (vector,) * 3),
        "adam",
        [(flat[0], True)] + [(v, False) for v in flat[1:]],
        [(v, False) for v in new_shapes],
        [pltpu.VMEM(v.shape, f32) for v in (*flat[1:], *new_shapes)]
        + [dma((len(flat) - 1,)), dma((len(new_shapes),))],
        vmem=32,
    )
    new = list(new)
    gradient_norm = new.pop().reshape(())
    new[9:12] = [v.T for v in new[9:12]]
    return (outputs, input_gradient, gradient_norm, *new)


def turn(plan, value, z, axis):
    value = jnp.flip(value, axis)
    return jnp.roll(value, z + 1, axis)


def unturn(plan, value, z, axis):
    return jnp.roll(value, -z, axis)


def swap(value, flag, axis):
    return jnp.where(flag == 1, jnp.flip(value, axis), value)


def absolute_ff(plan, value, z, x):
    value = swap(turn(plan, value, z, 1), x, 0)
    return value.transpose(1, 0, 2, 3).reshape(plan.width, plan.part)


def relative_ff(plan, value, z, x):
    value = value.reshape(plan.nz, 2, plan.rows, plan.part).transpose(1, 0, 2, 3)
    value = unturn(plan, swap(value, x, 0), z, 1)
    return value[0], value[1]


def absolute_attn(plan, own, other, z, x, y, c):
    zero = jnp.where(c == 0, own, other)
    one = jnp.where(c == 0, other, own).transpose(1, 0, 2, 3, 4)
    value = jnp.stack([zero, one])
    value = turn(plan, swap(swap(value, y, 1), x, 2), z, 3)
    value = value.transpose(1, 3, 2, 0, 4, 5)
    return value.reshape(2, plan.width, 4 * plan.cols)


def relative_attn(plan, value, z, x, y, c):
    value = value.reshape(2, plan.nz, 2, 2, plan.half, 4 * plan.cols)
    value = value.transpose(3, 0, 2, 1, 4, 5)
    value = unturn(plan, swap(swap(value, y, 1), x, 2), z, 3)
    zero, one = value[0], value[1].transpose(1, 0, 2, 3, 4)
    return jnp.where(c == 0, zero, one), jnp.where(c == 0, one, zero)


def solution(mesh):
    tokens = P("dp", None)
    triple = P(None, "dp", "mp")
    tall = P("mp", "dp")
    wide = P("dp", "mp")
    pair = P(None, "mp")
    states = ((triple,) * 3, (tall,) * 3, (wide,) * 3, (tall,) * 3, (P(),) * 3, (pair,) * 3)
    states = sum(states, ()) + (P("mp"),) * 3
    return jax.shard_map(
        per_device,
        mesh=mesh,
        in_specs=(tokens,) * 3 + states,
        out_specs=(tokens, tokens, P()) + states,
        check_vma=False,
    )
```

```python
import functools

import jax
import jax.numpy as jnp
from jax import lax
from jax.experimental import pallas as pl
from jax.experimental.pallas import tpu as pltpu
from jax.sharding import PartitionSpec as P

HD = 64
STEP = 5
EPS_NORM = 1e-06
BETA = 0.5
LR_MATRIX = 0.03
LR_VECTOR = 0.2
DECAY = 0.1
ADAM_EPS = 1e-08
CLIP = 1.0
NEG = -1e30
GELU_C = 0.7978845608028654
GELU_K = 0.044715

f32 = jnp.float32
bf16 = jnp.bfloat16
AXES = ("dp", "mp")
LANES = 128
CHUNK = 256
MIB = 1 << 20


def mm(left, right):
    return lax.dot_general(left, right, (((1,), (0,)), ((), ())), preferred_element_type=f32)


def mm_nt(left, right):
    return lax.dot_general(left, right, (((1,), (1,)), ((), ())), preferred_element_type=f32)


def mm_tn(left, right):
    return lax.dot_general(left, right, (((0,), (0,)), ((), ())), preferred_element_type=f32)


def norm_stats(rows_in):
    centred = rows_in - jnp.mean(rows_in, axis=-1, keepdims=True)
    scaled = lax.rsqrt(jnp.mean(centred * centred, axis=-1, keepdims=True) + EPS_NORM)
    return centred * scaled, scaled


def norm_backward(upstream, normal_rows, scaled, gain_row):
    gained = upstream * gain_row
    mean_one = jnp.mean(gained, axis=-1, keepdims=True)
    mean_two = jnp.mean(gained * normal_rows, axis=-1, keepdims=True)
    return scaled * (gained - mean_one - normal_rows * mean_two)


def lane_low(shape):
    return lax.broadcasted_iota(jnp.int32, shape, 1) % LANES < HD


def split_heads(block):
    low = lane_low(block.shape)
    zero = jnp.zeros_like(block)
    return jnp.concatenate([jnp.where(low, block, zero), jnp.where(low, zero, block)], axis=0)


def join_heads(stacked):
    half = stacked.shape[0] // 2
    low = lane_low((half, stacked.shape[1]))
    return jnp.where(low, stacked[:half], stacked[half:])


class Plan:
    def __init__(self, ndp, nmp, width, hidden):
        assert ndp % 2 == 0 and nmp == 4
        self.ndev = ndp * nmp
        self.nz = ndp // 2
        self.rows = width // ndp
        self.half = self.rows // 2
        self.width = width
        self.cols = width // 2
        self.part = hidden // nmp
        self.direct = self.half % 16 == 0

    def perm(self, move):
        pairs = []
        for z in range(self.nz):
            for x in range(2):
                for y in range(2):
                    for c in range(2):
                        there = move(z, x, y, c)
                        pairs.append((self.index(z, x, y, c), self.index(*there)))
        return pairs

    def index(self, z, x, y, c):
        return (2 * z + x) * 4 + 2 * y + c

    def core(self, value):
        return lax.ppermute(value, AXES, self.perm(lambda z, x, y, c: (z, x, y, 1 - c)))

    def along_x(self, value):
        return lax.ppermute(value, AXES, self.perm(lambda z, x, y, c: (z, 1 - x, y, c)))

    def along_y(self, value):
        return lax.ppermute(value, AXES, self.perm(lambda z, x, y, c: (z, x, 1 - y, c)))

    def along_z(self, value, step):
        return lax.ppermute(
            value, AXES, self.perm(lambda z, x, y, c: ((z + step) % self.nz, x, y, c))
        )

    def first(self, value):
        return lax.ppermute(
            value,
            AXES,
            self.perm(lambda z, x, y, c: (z, x, 1 - y, c) if c else (z, 1 - x, y, c)),
        )

    def second(self, value):
        return lax.ppermute(
            value,
            AXES,
            self.perm(lambda z, x, y, c: (z, 1 - x, y, c) if c else (z, x, 1 - y, c)),
        )


def piece_spot(plan, meta, r, fy, fx, k, sign):
    z, x, y, c = meta[1], meta[2], meta[3], meta[4]
    cc = jnp.bitwise_xor(c, r)
    zz = lax.rem(z + sign * k + plan.nz, plan.nz)
    xx = jnp.bitwise_xor(x, fx)
    yy = jnp.bitwise_xor(y, fy)
    return cc, zz, xx, yy


def attn_weight_copies(plan, meta, srcs, w, sem, lanes):
    if not plan.direct:
        return [pltpu.make_async_copy(srcs[0].at[:, :, lanes], w, sem.at[0])]
    copies = []
    for s2 in range(2):
        for r in range(2):
            for s1 in range(2):
                for k in range(plan.nz):
                    cc = jnp.bitwise_xor(meta[4], r)
                    fx = jnp.where(cc == 0, s1, s2)
                    fy = jnp.where(cc == 0, s2, s1)
                    _, zz, xx, yy = piece_spot(plan, meta, r, fy, fx, k, -1)
                    row = pl.multiple_of((zz * 2 + xx) * plan.rows + cc * plan.half, 16)
                    copies.append(
                        pltpu.make_async_copy(
                            srcs[2 * r + s2].at[s1, k, :, lanes],
                            w.at[yy, pl.ds(row, plan.half), :],
                            sem.at[len(copies)],
                        )
                    )
    return copies


def token_copy(src, block, dst, sem):
    count = dst.shape[0]
    return pltpu.make_async_copy(
        src.at[pl.ds(pl.multiple_of(block * count, 16), count), :], dst, sem
    )


def chunks(count, body):
    def step(i, carry):
        body(i, pl.ds(pl.multiple_of(i * CHUNK, CHUNK), CHUNK))
        return carry

    lax.fori_loop(0, count // CHUNK, step, 0, unroll=True)


def lanes_of(base, b, cols, p):
    return slice(base + b * cols + p * LANES, base + b * cols + (p + 1) * LANES)


def attn_prep_kernel(meta, x_all, np_ref, x_ref, fl_ref, sem):
    load = token_copy(x_all, meta[0], x_ref, sem.at[0])
    load.start()
    load.wait()

    def body(i, at):
        normal, _ = norm_stats(x_ref[at, :].astype(f32))
        fl_ref[at, :] = (normal * np_ref[0:1, :] + np_ref[1:2, :]).astype(bf16)

    chunks(x_ref.shape[0], body)


def attn_fwd_kernel(plan, meta, x_ref, fl_ref, segc_ref, segr_ref, np_ref, pb_ref, *refs):
    srcs, refs = refs[:4], refs[4:]
    sl_ref, mid_ref, qkv_ref, p_ref, ctx_ref, w, sl_buf, sem, sem_x = refs
    cols = plan.cols
    count = x_ref.shape[0]
    copies = attn_weight_copies(plan, meta, srcs, w, sem, slice(None))
    for copy in copies:
        copy.start()
    for copy in copies:
        copy.wait()
    tiles = CHUNK // LANES
    pairs = cols // LANES

    def second(i, at):
        for y in range(2):
            for part in range(3):
                lanes = slice(part * cols, (part + 1) * cols)
                got = mm(fl_ref[at, :], w[y, :, lanes])
                if part != 1:
                    got = got + pb_ref[part // 2 : part // 2 + 1, y * cols : (y + 1) * cols]
                qkv_ref[y, at, lanes] = got.astype(bf16)
        for t in range(tiles):
            tile = i * tiles + t
            tok = pl.ds(pl.multiple_of(tile * LANES, LANES), LANES)
            same = segc_ref[tok, :] == segr_ref[pl.ds(tile, 1), :]
            same = jnp.concatenate([same] * (2 * pairs), axis=0)
            for y in range(2):
                s = jnp.concatenate(
                    [
                        mm_nt(
                            split_heads(qkv_ref[y, tok, lanes_of(0, 0, cols, p)]),
                            qkv_ref[y, tok, lanes_of(0, 1, cols, p)],
                        )
                        for p in range(pairs)
                    ],
                    axis=0,
                )
                s = jnp.where(same, s * HD**-0.5, NEG)
                e = jnp.exp(s - jnp.max(s, axis=-1, keepdims=True))
                probs = (e * (1.0 / jnp.sum(e, axis=-1, keepdims=True))).astype(bf16)
                p_ref[tile * 2 + y] = probs
                for p in range(pairs):
                    own = probs[p * 2 * LANES : (p + 1) * 2 * LANES]
                    ctx = join_heads(mm(own, qkv_ref[y, tok, lanes_of(0, 2, cols, p)]))
                    ctx_ref[tok, lanes_of(y * cols, 0, cols, p)] = ctx.astype(bf16)
        attended = mm_nt(ctx_ref[at, 0:cols], w[0, :, 3 * cols :])
        attended = attended + mm_nt(ctx_ref[at, cols:], w[1, :, 3 * cols :])
        middle = x_ref[at, :].astype(f32) + attended + np_ref[4:5, :]
        mid_ref[at, :] = middle
        normal, _ = norm_stats(middle)
        sl = (normal * np_ref[2:3, :] + np_ref[3:4, :]).astype(bf16)
        sl_buf[at, :] = sl
        pltpu.make_async_copy(sl_buf.at[at, :], sl_ref.at[at, :], sem_x.at[i]).start()

    chunks(count, second)
    for i in range(count // CHUNK):
        at = pl.ds(i * CHUNK, CHUNK)
        pltpu.make_async_copy(sl_buf.at[at, :], sl_ref.at[at, :], sem_x.at[i]).wait()


def ff_weight_copies(plan, meta, srcs, w, sem, r, e):
    src = srcs[4 * e + 2 * r : 4 * e + 2 * r + 2]
    if not plan.direct:
        return [pltpu.make_async_copy(src[0], w.at[e, r], sem.at[r, e, 0])]
    copies = []
    for fx in range(2):
        for k in range(plan.nz):
            _, zz, xx, _ = piece_spot(plan, meta, r, 0, fx, k, -1)
            row = pl.multiple_of((zz * 2 + xx) * plan.rows, 16)
            copies.append(
                pltpu.make_async_copy(
                    src[fx].at[k],
                    w.at[e, r, pl.ds(row, plan.rows), :],
                    sem.at[r, e, len(copies)],
                )
            )
    return copies


def ff_kernel(plan, own, meta, sl_ref, cot_all, hb_ref, *refs):
    copies = []
    if own:
        w, mid_ref, sg_ref, fed_ref, act_ref, hg_ref, gh_ref, cot_ref, buf, sem_x = refs
    else:
        *srcs, sg_ref, fed_ref, act_ref, hg_ref, gh_ref, cot_ref, w, sg_buf, buf, sem, sem_x = refs
        for r in range(2):
            for e in range(2):
                copies = copies + ff_weight_copies(plan, meta, srcs, w, sem, r, e)
    for copy in copies:
        copy.start()
    count = cot_ref.shape[0]
    load = token_copy(cot_all, meta[0 if own else 5], cot_ref, sem_x.at[0])
    load.start()
    gh_ref[...] = jnp.zeros_like(gh_ref)
    load.wait()
    for copy in copies:
        copy.wait()

    def body(i, at):
        sl = sl_ref[at, :]
        cot = cot_ref[at, :]
        total = [None, None]
        for r in range(2):
            h = mm(sl, w[0, r]) + hb_ref[r : r + 1, :]
            grown = mm(cot, w[1, r])
            square = h * h
            half = 0.5 * jnp.tanh(h * (GELU_C + (GELU_C * GELU_K) * square)) + 0.5
            act = h * half
            slope = half + (act - act * half) * (2.0 * GELU_C + (6.0 * GELU_C * GELU_K) * square)
            grown = grown * slope
            gh_ref[r : r + 1, :] += jnp.sum(grown, axis=0, keepdims=True)
            act = act.astype(bf16)
            grown = grown.astype(bf16)
            act_ref[r, at, :] = act
            hg_ref[r, at, :] = grown
            for e, left in enumerate((grown, act)):
                got = mm_nt(left, w[e, r])
                total[e] = got if total[e] is None else total[e] + got
        fed = total[1] + mid_ref[at, :] if own else total[1]
        buf[at, :] = fed.astype(bf16)
        pltpu.make_async_copy(buf.at[at, :], fed_ref.at[at, :], sem_x.at[i]).start()
        if own:
            sg_ref[at, :] = total[0].astype(bf16)
        else:
            sg_buf[at, :] = total[0].astype(bf16)
            pltpu.make_async_copy(
                sg_buf.at[at, :], sg_ref.at[at, :], sem_x.at[count // CHUNK + i]
            ).start()

    chunks(count, body)
    for i in range(count // CHUNK):
        at = pl.ds(i * CHUNK, CHUNK)
        pltpu.make_async_copy(buf.at[at, :], fed_ref.at[at, :], sem_x.at[i]).wait()
        if not own:
            pltpu.make_async_copy(
                sg_buf.at[at, :], sg_ref.at[at, :], sem_x.at[count // CHUNK + i]
            ).wait()


def ff_grad_copies(plan, meta, buf, outs, sem, r):
    if not plan.direct:
        return [
            pltpu.make_async_copy(buf.at[r, e], outs[2 * r + e], sem.at[r, e]) for e in range(2)
        ]
    copies = []
    for e in range(2):
        for fx in range(2):
            for k in range(plan.nz):
                _, zz, xx, _ = piece_spot(plan, meta, r, 0, fx, k, 1)
                row = pl.multiple_of((zz * 2 + xx) * plan.rows, 16)
                copies.append(
                    pltpu.make_async_copy(
                        buf.at[r, e, pl.ds(row, plan.rows), :],
                        outs[4 * r + 2 * e + fx].at[k],
                        sem.at[r, len(copies)],
                    )
                )
    return copies


def ff_grad_kernel(plan, meta, sl_a, sl_b, cot_a, cot_b, act_a, act_b, hg_a, hg_b, *rest):
    *outs, buf, sem = rest
    for r in (1, 0):
        for e, (a, b, one, two) in enumerate(
            ((sl_a, sl_b, hg_a, hg_b), (cot_a, cot_b, act_a, act_b))
        ):
            buf[r, e] = (mm_tn(a[...], one[r]) + mm_tn(b[...], two[r])).astype(bf16)
        for copy in ff_grad_copies(plan, meta, buf, outs, sem, r):
            copy.start()
    for r in range(2):
        for copy in ff_grad_copies(plan, meta, buf, outs, sem, r):
            copy.wait()


def attn_bwd_kernel(
    plan,
    meta,
    sga_ref,
    sgb_ref,
    mid_ref,
    cot_ref,
    np_ref,
    qkv_ref,
    p_ref,
    w,
    dqkv_ref,
    ml_ref,
    mg_ref,
    vec_ref,
    pair_ref,
):
    cols = plan.cols
    tiles = CHUNK // LANES
    pairs = cols // LANES
    vec_ref[...] = jnp.zeros_like(vec_ref)
    pair_ref[...] = jnp.zeros_like(pair_ref)

    def body(i, at):
        sg = sga_ref[at, :].astype(f32) + sgb_ref[at, :].astype(f32)
        cot = cot_ref[at, :].astype(f32)
        normal, scaled = norm_stats(mid_ref[at, :])
        mg = cot + norm_backward(sg, normal, scaled, np_ref[2:3, :])
        mg_ref[at, :] = mg
        ml = mg.astype(bf16)
        ml_ref[at, :] = ml
        vec_ref[0:1, :] += jnp.sum(sg * normal, axis=0, keepdims=True)
        vec_ref[1:2, :] += jnp.sum(sg, axis=0, keepdims=True)
        vec_ref[2:3, :] += jnp.sum(mg, axis=0, keepdims=True)
        vec_ref[3:4, :] += jnp.sum(cot, axis=0, keepdims=True)
        for y in range(2):
            dctx = mm(ml, w[y, :, 3 * cols :]).astype(bf16)
            for t in range(tiles):
                tile = i * tiles + t
                tok = pl.ds(pl.multiple_of(tile * LANES, LANES), LANES)
                dcs = [
                    split_heads(dctx[t * LANES : (t + 1) * LANES, lanes_of(0, 0, cols, p)])
                    for p in range(pairs)
                ]
                low = p_ref[tile * 2 + y]
                probs = low.astype(f32)
                dp = jnp.concatenate(
                    [
                        mm_nt(dcs[p], qkv_ref[y, tok, lanes_of(0, 2, cols, p)])
                        for p in range(pairs)
                    ],
                    axis=0,
                )
                inner = jnp.sum(dp * probs, axis=-1, keepdims=True)
                ds = (probs * (dp - inner) * HD**-0.5).astype(bf16)
                for p in range(pairs):
                    at_q, at_k, at_v = (lanes_of(0, b, cols, p) for b in range(3))
                    rows = slice(p * 2 * LANES, (p + 1) * 2 * LANES)
                    qs = split_heads(qkv_ref[y, tok, at_q])
                    dq = join_heads(mm(ds[rows], qkv_ref[y, tok, at_k])).astype(bf16)
                    dqkv_ref[y, tok, at_q] = dq
                    dqkv_ref[y, tok, at_k] = mm_tn(ds[rows], qs).astype(bf16)
                    dqkv_ref[y, tok, at_v] = mm_tn(low[rows], dcs[p]).astype(bf16)
            for b in (0, 2):
                lanes = slice(b * cols, (b + 1) * cols)
                pair_ref[b // 2 : b // 2 + 1, y * cols : (y + 1) * cols] += jnp.sum(
                    dqkv_ref[y, at, lanes].astype(f32), axis=0, keepdims=True
                )

    chunks(sga_ref.shape[0], body)


def attn_grad_pieces(plan, meta, buf, outs, sem, fy):
    if not plan.direct:
        yy = jnp.bitwise_xor(meta[3], fy)
        return [pltpu.make_async_copy(buf.at[fy], outs[0].at[yy], sem.at[fy, 0])]
    copies = []
    for r in range(2):
        for fx in range(2):
            for k in range(plan.nz):
                cc, zz, xx, _ = piece_spot(plan, meta, r, fy, fx, k, 1)
                s1 = jnp.where(cc == 0, fx, fy)
                s2 = jnp.where(cc == 0, fy, fx)
                row = pl.multiple_of((zz * 2 + xx) * plan.rows + cc * plan.half, 16)
                out = outs[r * plan.nz + k]
                if r == 0:
                    out[s2, s1] = buf[fy, pl.ds(row, plan.half), :]
                else:
                    copies.append(
                        pltpu.make_async_copy(
                            buf.at[fy, pl.ds(row, plan.half), :],
                            out.at[s2, s1],
                            sem.at[fy, len(copies)],
                        )
                    )
    return copies


def attn_grad_kernel(plan, meta, fl_ref, ml_ref, dqkv_ref, ctx_ref, *rest):
    *outs, buf, sem = rest
    cols = plan.cols
    copies = []
    for fy in range(2):
        y = jnp.bitwise_xor(meta[3], fy)
        lanes = pl.ds(pl.multiple_of(y * cols, LANES), cols)
        buf[fy, :, : 3 * cols] = mm_tn(fl_ref[...], dqkv_ref[y]).astype(bf16)
        buf[fy, :, 3 * cols :] = mm_tn(ml_ref[...], ctx_ref[:, lanes]).astype(bf16)
        some = attn_grad_pieces(plan, meta, buf, outs, sem, fy)
        for copy in some:
            copy.start()
        copies = copies + some
    for copy in copies:
        copy.wait()


def input_grad_kernel(
    plan, meta, x_ref, mg_ref, np_ref, dqkv_ref, w, ig_ref, vec_ref, buf, sem
):
    cols = plan.cols
    count = x_ref.shape[0]
    vec_ref[...] = jnp.zeros_like(vec_ref)

    def body(i, at):
        normal, scaled = norm_stats(x_ref[at, :].astype(f32))
        fg = mm_nt(dqkv_ref[0, at, :], w[0, :, : 3 * cols])
        fg = fg + mm_nt(dqkv_ref[1, at, :], w[1, :, : 3 * cols])
        vec_ref[0:1, :] += jnp.sum(fg * normal, axis=0, keepdims=True)
        vec_ref[1:2, :] += jnp.sum(fg, axis=0, keepdims=True)
        ig = mg_ref[at, :] + norm_backward(fg, normal, scaled, np_ref[0:1, :])
        buf[at, :] = ig.astype(bf16)
        pltpu.make_async_copy(buf.at[at, :], ig_ref.at[at, :], sem.at[i]).start()

    chunks(count, body)
    for i in range(count // CHUNK):
        at = pl.ds(i * CHUNK, CHUNK)
        pltpu.make_async_copy(buf.at[at, :], ig_ref.at[at, :], sem.at[i]).wait()


def add_kernel(meta, left, right, *outs):
    for i, out in enumerate(outs):
        out[...] = (left[i].astype(f32) + right[i].astype(f32)).astype(out.dtype)


def add_parts(meta, left, right):
    n, size = left.shape[0], left.shape[-1]
    shape = left.shape[1:]
    left, right = left.reshape(n, -1, size), right.reshape(n, -1, size)
    length = left.shape[1]
    blocks = 4 if length % 64 == 0 and length >= 384 else 1
    step = length // blocks
    outs = call(
        add_kernel,
        "add_parts",
        (blocks,),
        [(v, (n, step, size), lambda i, m: (0, i, 0)) for v in (left, right)],
        [(jax.ShapeDtypeStruct((length, size), bf16), (step, size), lambda i, m: (i, 0))] * n,
        [],
    )(meta, left, right)
    return [v.reshape(shape) for v in outs]


def sums_kernel(meta, *refs):
    n = len(refs) // 3
    for left, right, out in zip(refs[:n], refs[n : 2 * n], refs[2 * n :]):
        out[...] = (left[...].astype(f32) + right[...].astype(f32)).astype(out.dtype)


def add_lists(meta, left, right):
    n, shape = len(left), left[0].shape
    flat = [v.reshape(-1, shape[-1]) for v in (*left, *right)]
    length, size = flat[0].shape
    blocks = 2 if length % 32 == 0 and length >= 384 else 1
    block = ((length // blocks, size), lambda i, m: (i, 0))
    outs = call(
        sums_kernel,
        "add_lists",
        (blocks,),
        [(v, *block) for v in flat],
        [(jax.ShapeDtypeStruct((length, size), bf16), *block)] * n,
        [],
    )(meta, *flat)
    return [v.reshape(shape) for v in outs]


def first_kernel(n, meta, *refs):
    left, right, (keep, send, got, buf, sem) = refs[:n], refs[n : 2 * n], refs[2 * n :]
    loads = [pltpu.make_async_copy(right[k], got.at[k], sem.at[k]) for k in range(n)]
    for load in loads:
        load.start()
    for k in range(n):
        loads[k].wait()
        for s, out in enumerate((keep, buf)):
            for i in range(out.shape[0]):
                out[i, k] = (left[k][s, i].astype(f32) + got[k, s, i].astype(f32)).astype(bf16)
    store = pltpu.make_async_copy(buf, send, sem.at[n])
    store.start()
    store.wait()


def add_first(meta, left, right):
    n, shape = len(left), left[0].shape[1:]
    out = jax.ShapeDtypeStruct((shape[0], n, *shape[1:]), bf16)
    return local_call(
        meta,
        functools.partial(first_kernel, n),
        "add_first",
        [(v, True) for v in left] + [(v, False) for v in right],
        [(out, True), (out, False)],
        [
            pltpu.VMEM((n, 2, *shape), bf16),
            pltpu.VMEM(out.shape, bf16),
            pltpu.SemaphoreType.DMA((n + 1,)),
        ],
    )


def vectors_kernel(plan, meta, one, two, pair, near, far, out, buf, sem):
    buf[...] = jnp.zeros_like(buf)
    per = buf.shape[2] // LANES
    lines = plan.width // LANES

    def put(start, row):
        for q in range(row.shape[1] // LANES):
            b = start + q
            at = slice(b % per * LANES, (b % per + 1) * LANES)
            buf[b // per, :, at] = row[:, q * LANES : (q + 1) * LANES]

    for i in range(2):
        put(i * lines, one[i : i + 1, :])
        put((6 + i) * lines, pair[i : i + 1, :])
    for i in range(4):
        put((2 + i) * lines, two[i : i + 1, :])
    total = near[...] + far[...]
    for y in range(2):
        for c in range(2):

            @pl.when((meta[3] == y) & (meta[4] == c))
            def _():
                for r in range(2):
                    m = 2 * y + (c + r) % 2
                    put(8 * lines + m * plan.part // LANES, total[r : r + 1, :])

    copy = pltpu.make_async_copy(buf, out, sem.at[0])
    copy.start()
    copy.wait()


def ff_total_kernel(meta, *refs):
    *parts, expand, reduce, square = refs
    half = len(parts) // 2
    sums = None
    for out, some in ((expand, parts[:half]), (reduce, parts[half:])):
        total = some[0][...].astype(f32)
        for part in some[1:]:
            total = total + part[...].astype(f32)
        out[...] = total
        line = jnp.sum(total * total, axis=0, keepdims=True)
        sums = line if sums is None else sums + line
    square[...] = jnp.sum(sums, axis=1, keepdims=True)


def total_kernel(meta, *refs):
    *parts, ff_square, local, keep, send, payload = refs
    total = parts[0][...].astype(f32)
    for part in parts[1:]:
        total = total + part[...].astype(f32)
    quarter = total.shape[1] // 8
    for core in range(2):
        for out, c in ((keep, core), (send, 1 - core)):

            @pl.when(meta[4] == core)
            def _():
                for b in range(4):
                    at = (2 * b + c) * quarter
                    out[:, b * quarter : (b + 1) * quarter] = total[:, at : at + quarter]

    square = jnp.sum(total * total) + jnp.sum(ff_square[...]) + jnp.sum(local[...] * local[...])
    size = local.shape[1]
    count = payload.shape[0]
    payload[:, :, :size] = jnp.broadcast_to(local[...][None], (count, 1, size))
    payload[:, :, size:] = jnp.full((count, 1, LANES), square, f32)


def out_kernel(meta, pre_a, fed_a, pre_b, fed_b, np_ref, out_a, out_b):
    for pre, fed, out in ((pre_a, fed_a, out_a), (pre_b, fed_b, out_b)):
        total = pre[...].astype(f32) + fed[...].astype(f32) + np_ref[5:6, :]
        out[...] = total.astype(bf16)


def place_kernel(meta, own, by_y, by_c, by_yc, out, sem):
    count = own.shape[0]
    copies = []
    for fy, fc, src in ((0, 0, own), (1, 0, by_y), (0, 1, by_c), (1, 1, by_yc)):
        at = jnp.bitwise_xor(meta[3], fy) * 2 + jnp.bitwise_xor(meta[4], fc)
        dst = out.at[pl.ds(pl.multiple_of(at * count, 16), count), :]
        copies.append(pltpu.make_async_copy(src, dst, sem.at[len(copies)]))
    for copy in copies:
        copy.start()
    for copy in copies:
        copy.wait()


def adam_kernel(plan, rates, meta, got, *refs):
    per = got.shape[2] // LANES - 1
    total = jnp.sum(got[:, 0, per * LANES :], axis=0, keepdims=True)[:, 0:1]
    norm = jnp.sqrt(total)
    results = 3 * len(rates) + 1
    inputs = 4 * 4 + 3 * 3
    sources, finals = refs[:inputs], refs[inputs : inputs + results]
    ins, bufs = refs[inputs + results : -2 - results], refs[-2 - results : -2]
    sem_in, sem_out = refs[-2:]
    loads = [
        pltpu.make_async_copy(source, buf, sem_in.at[i])
        for i, (source, buf) in enumerate(zip(sources, ins))
    ]
    stores = [
        pltpu.make_async_copy(buf, final, sem_out.at[i])
        for i, (buf, final) in enumerate(zip(bufs, finals))
    ]
    for load in loads:
        load.start()
    bufs[-1][...] = norm
    stores[-1].start()
    factor = jnp.minimum(1.0, CLIP / norm)
    correction = 1.0 - BETA**STEP
    width, quarter, part = plan.width, plan.width // 4, plan.part

    def line(start, length):
        spots = range(start // LANES, (start + length) // LANES)
        return jnp.concatenate(
            [got[b // per, :, b % per * LANES : (b % per + 1) * LANES] for b in spots],
            axis=1,
        )

    def owned(pick):
        value = pick(0)
        for m in range(1, 4):
            value = jnp.where(meta[0] == m, pick(m), value)
        return value

    pairs = [line((6 + i) * width, width) for i in range(2)]
    small = (
        jnp.concatenate([line(i * width, width) for i in range(6)], axis=0),
        jnp.concatenate(
            [owned(lambda m: v[:, m * quarter : (m + 1) * quarter]) for v in pairs], axis=0
        ),
        owned(lambda m: line(8 * width + m * part, part)),
    )
    outs = bufs[:-1]
    attn = {}
    for i in (3, 7):
        loads[i].wait()
    if plan.direct:
        mine, other = ins[3][...], ins[7][...]
        low = jnp.where(meta[4] == 0, mine, other)
        high = jnp.where(meta[4] == 0, other, mine)
        for p in range(4):
            at = slice(p * quarter, (p + 1) * quarter)
            attn[p] = jnp.concatenate([low[:, at], high[:, at]], axis=0)
    for i, (rate, decay) in enumerate(rates):
        if i < 4:
            first_in = 4 * i
            w_ref, m_ref, s_ref, g_ref = ins[4 * i : 4 * i + 4]
            if plan.direct and i < 2:
                g_ref = attn if i == 0 else {Ellipsis: attn[3].T}
        else:
            first_in = 3 * i + 4
            w_ref, m_ref, s_ref = ins[3 * i + 4 : 3 * i + 7]
            g_ref = {Ellipsis: small[i - 4]}
        for j in range(first_in, first_in + (4 if i < 4 else 3)):
            if j not in (3, 7):
                loads[j].wait()
        m_out, s_out, w_out = outs[3 * i : 3 * i + 3]
        planes = range(w_ref.shape[0]) if len(w_ref.shape) == 3 else (Ellipsis,)
        for p in planes:
            clipped = g_ref[p] * factor
            shape = w_ref[p].shape
            weight, first, second = (
                v[p].reshape(clipped.shape) for v in (w_ref, m_ref, s_ref)
            )
            first = BETA * first + (1.0 - BETA) * clipped
            second = BETA * second + (1.0 - BETA) * clipped * clipped
            direction = first / correction / (jnp.sqrt(second / correction) + ADAM_EPS)
            m_out[p] = first.reshape(shape)
            s_out[p] = second.reshape(shape)
            w_out[p] = (weight - rate * (direction + decay * weight)).reshape(shape)
        for store in stores[3 * i : 3 * i + 3]:
            store.start()
    for store in stores:
        store.wait()


def after(value, *others):
    return lax.optimization_barrier((value, *others))[0]


def any_spec():
    return pl.BlockSpec(memory_space=pl.ANY)


def local_call(meta, kernel, name, ins, outs, scratch, vmem=16):
    def space(item):
        return pltpu.VMEM if item[1] else pltpu.HBM

    def place(item):
        return item[0] if item[1] else pltpu.with_memory_space_constraint(item[0], pltpu.HBM)

    kernel_call = pl.pallas_call(
        kernel,
        name=name,
        out_shape=[space(o)(o[0].shape, o[0].dtype) for o in outs],
        in_specs=[pl.BlockSpec(memory_space=s) for s in (pltpu.SMEM, *map(space, ins))],
        out_specs=[pl.BlockSpec(memory_space=space(o)) for o in outs],
        scratch_shapes=scratch,
        compiler_params=pltpu.CompilerParams(vmem_limit_bytes=vmem * MIB),
        cost_estimate=pl.CostEstimate(flops=1, bytes_accessed=1, transcendentals=0),
    )
    return kernel_call(meta, *map(place, ins))


def call(kernel, name, grid, ins, outs, scratch, vmem=16):
    def spec(item):
        if item[1] is None:
            return any_spec()
        return pl.BlockSpec(item[1], item[2])

    return pl.pallas_call(
        kernel,
        name=name,
        out_shape=[o[0] for o in outs],
        grid_spec=pltpu.PrefetchScalarGridSpec(
            num_scalar_prefetch=1,
            grid=grid,
            in_specs=[spec(i) for i in ins],
            out_specs=[spec(o) for o in outs],
            scratch_shapes=scratch,
        ),
        compiler_params=pltpu.CompilerParams(vmem_limit_bytes=vmem * MIB),
        cost_estimate=pl.CostEstimate(flops=1, bytes_accessed=1, transcendentals=0),
    )


def per_device(
    inputs,
    segments,
    cotangent,
    triple_weight,
    triple_first,
    triple_second,
    outward_weight,
    outward_first,
    outward_second,
    expand_weight,
    expand_first,
    expand_second,
    reduce_weight,
    reduce_first,
    reduce_second,
    norm_params,
    norm_first,
    norm_second,
    paired_bias,
    paired_first,
    paired_second,
    hidden_bias,
    hidden_first,
    hidden_second,
):
    ndp, nmp = lax.axis_size("dp"), lax.axis_size("mp")
    width = inputs.shape[1]
    hidden = hidden_bias.shape[0] * nmp
    plan = Plan(ndp, nmp, width, hidden)
    nz, rows, half, cols, part = plan.nz, plan.rows, plan.half, plan.cols, plan.part
    count = inputs.shape[0] // nmp
    row_count, row_length = segments.shape
    own_rows = row_count // nmp
    steps = count // CHUNK
    quarter = cols // 2

    dp, mp = lax.axis_index("dp"), lax.axis_index("mp")
    z, x, y, c = dp // 2, dp % 2, mp // 2, mp % 2
    meta = jnp.stack([mp, z, x, y, c, jnp.bitwise_xor(mp, 2)]).astype(jnp.int32)
    core_zero = c == 0
    SDS = jax.ShapeDtypeStruct

    shard = jnp.concatenate(
        [triple_weight.astype(bf16), outward_weight.T.astype(bf16)[None]], axis=0
    ).transpose(1, 0, 2)
    keep = lax.dynamic_slice_in_dim(shard, c * half, half, 0)
    send = lax.dynamic_slice_in_dim(shard, (1 - c) * half, half, 0)
    got = plan.core(send)
    low = jnp.where(core_zero, keep, got)
    high = jnp.where(core_zero, got, keep)
    unit = jnp.concatenate([low, high], axis=2).reshape(half, 4 * cols)
    attn_z = [plan.along_z(unit, k) for k in range(nz - 1, 0, -1)][::-1]

    e_unit = after(expand_weight.astype(bf16), attn_z[0])
    e_z = [plan.along_z(e_unit, k) for k in range(1, nz)]
    r_unit = after(reduce_weight.T.astype(bf16), e_z[0])
    r_z = [plan.along_z(r_unit, k) for k in range(1, nz)]

    biases = jnp.concatenate([paired_bias.reshape(-1), hidden_bias])
    by_core = plan.core(after(biases, attn_z[0]))
    other_pair = by_core[: 2 * quarter].reshape(2, quarter)
    near = jnp.where(
        core_zero,
        jnp.concatenate([paired_bias, other_pair], axis=1),
        jnp.concatenate([other_pair, paired_bias], axis=1),
    )
    far = plan.along_y(near)
    pair_full = jnp.where(
        y == 0, jnp.concatenate([near, far], axis=1), jnp.concatenate([far, near], axis=1)
    )
    hidden_rows = jnp.stack([hidden_bias, by_core[2 * quarter :]])

    marks = lax.dynamic_slice_in_dim(segments, mp * own_rows, own_rows, 0)
    marks = marks + row_length * lax.broadcasted_iota(jnp.int32, marks.shape, 0)
    mark_col = marks.reshape(count, 1)
    mark_row = marks.reshape(count // LANES, LANES)

    spread = jnp.stack([unit] + attn_z)
    spread = jnp.stack([spread, plan.first(spread)])
    spread, *_, meta, mark_col, mark_row, pair_full, hidden_rows = lax.optimization_barrier(
        (spread, e_z[0], meta, mark_col, mark_row, pair_full, hidden_rows)
    )
    dma = pltpu.SemaphoreType.DMA
    tokens_low, tokens_f32 = SDS((count, width), bf16), SDS((count, width), f32)
    sem_x = dma((2 * steps,))
    buf_low = pltpu.VMEM((count, width), bf16)
    own_x, fl = local_call(
        meta,
        attn_prep_kernel,
        "attn_prep",
        [(inputs, False), (norm_params, True)],
        [(tokens_low, True), (tokens_low, True)],
        [sem_x],
    )
    attn_w = [spread, after(plan.second(spread), fl, *e_z)]
    e_spread = after(jnp.stack([e_unit] + e_z), attn_w[1])
    e_x = plan.along_x(e_spread)
    attn_w = attn_w + [plan.core(v) for v in attn_w]
    attn_w[1] = after(attn_w[1], e_spread)

    if not plan.direct:
        attn_w = [absolute_attn(plan, jnp.stack(attn_w[:2]), jnp.stack(attn_w[2:]), z, x, y, c)]
        attn_w = attn_w + [meta] * 3

    whole = lambda shape: (shape, lambda i, m: (0,) * len(shape))
    chunk = lambda n: ((CHUNK, n), lambda i, m: (i, 0))
    pieces = 2 * 2 * 2 * nz if plan.direct else 1

    sl, middle, qkv, probs, ctx, attn_full = local_call(
        meta,
        functools.partial(attn_fwd_kernel, plan),
        "attn_fwd",
        [
            (own_x, True),
            (fl, True),
            (mark_col, True),
            (mark_row, True),
            (norm_params, True),
            (pair_full, True),
            *[(v, False) for v in attn_w],
        ],
        [
            (tokens_low, False),
            (tokens_f32, True),
            (SDS((2, count, 3 * cols), bf16), True),
            (SDS((count // LANES * 2, 2 * cols, LANES), bf16), True),
            (tokens_low, True),
            (SDS((2, width, 4 * cols), bf16), True),
        ],
        [buf_low, dma((pieces,)), sem_x],
    )

    sl_far = plan.along_y(sl)
    r_spread = jnp.stack([r_unit] + [after(v, sl) for v in r_z])
    r_x = plan.along_x(r_spread)
    e_x = after(e_x, sl)
    ff_w = []
    for near, far in ((e_spread, e_x), (r_spread, r_x)):
        pieces_of = [near, far, plan.core(near), plan.core(far)]
        if not plan.direct:
            pairs = (pieces_of[:2], pieces_of[2:])
            pieces_of = [v for p in pairs for v in (absolute_ff(plan, jnp.stack(p), z, x), meta)]
        ff_w = ff_w + pieces_of

    act_shape = SDS((2, count, part), bf16)
    gh_shape = SDS((2, part), f32)
    sg_send, fed_send, act_far, hg_far, gh_far, cot_far, ff_full = local_call(
        meta,
        functools.partial(ff_kernel, plan, False),
        "ff_far",
        [
            (sl_far, True),
            (cotangent, False),
            (hidden_rows, True),
            *[(v, False) for v in ff_w],
        ],
        [
            (tokens_low, False),
            (tokens_low, False),
            (act_shape, True),
            (act_shape, True),
            (gh_shape, True),
            (tokens_low, True),
            (SDS((2, 2, width, part), bf16), True),
        ],
        [buf_low, buf_low, dma((2, 2, 2 * nz if plan.direct else 1)), sem_x],
    )
    sg_far = plan.along_y(sg_send)
    sg_near, pre_near, act_near, hg_near, gh_near, cot_near = local_call(
        meta,
        functools.partial(ff_kernel, plan, True),
        "ff_near",
        [
            (sl, True),
            (cotangent, False),
            (hidden_rows, True),
            (ff_full, True),
            (middle, True),
        ],
        [
            (tokens_low, True),
            (tokens_low, False),
            (act_shape, True),
            (act_shape, True),
            (gh_shape, True),
            (tokens_low, True),
        ],
        [buf_low, sem_x],
    )

    if plan.direct:
        grad_shapes = [SDS((nz, rows, part), bf16)] * 8
    else:
        grad_shapes = [SDS((width, part), bf16)] * 4
    ff_ins = (sl, sl_far, cot_near, cot_far, act_near, act_far, hg_near, hg_far)
    ff_grads = local_call(
        meta,
        functools.partial(ff_grad_kernel, plan),
        "ff_grad",
        [(v, True) for v in ff_ins],
        [(v, False) for v in grad_shapes],
        [pltpu.VMEM((2, 2, width, part), bf16), dma((2, 4 * nz if plan.direct else 2))],
    )
    if not plan.direct:
        ff_grads = [v for g in ff_grads for v in relative_ff(plan, g, z, x)]

    ff_got = [plan.core(v) for v in ff_grads[4:]]
    sg_far = after(sg_far, ff_grads[0])
    fed_far = plan.along_y(after(fed_send, sg_far))

    bwd_ins = (sg_near, sg_far, middle, cot_near, norm_params, qkv, probs, attn_full)
    dqkv, ml, mg, vec_two, pair_sum = local_call(
        meta,
        functools.partial(attn_bwd_kernel, plan),
        "attn_bwd",
        [(v, True) for v in bwd_ins],
        [
            (SDS((2, count, 3 * cols), bf16), True),
            (tokens_low, True),
            (tokens_f32, True),
            (SDS((8, width), f32), True),
            (SDS((2, width), f32), True),
        ],
        [],
    )

    ff_got[0] = after(ff_got[0], dqkv)
    e_keep, e_send, r_keep, r_send = add_lists(meta, ff_grads[:4], ff_got)
    e_got = plan.along_x(e_send)

    if plan.direct:
        grad_shapes = [SDS((2, 2, half, 4 * cols), bf16)] * (2 * nz)
    else:
        grad_shapes = [SDS((2, width, 4 * cols), bf16)]
    ml = after(ml, e_send, r_send)
    attn_grads = local_call(
        meta,
        functools.partial(attn_grad_kernel, plan),
        "attn_grad",
        [(v, True) for v in (fl, ml, dqkv, ctx)],
        [(v, plan.direct and i < nz) for i, v in enumerate(grad_shapes)],
        [pltpu.VMEM((2, width, 4 * cols), bf16), dma((2, 4 * nz if plan.direct else 1))],
    )
    if not plan.direct:
        both = relative_attn(plan, attn_grads[0], z, x, y, c)
        attn_grads = [v[:, :, k] for v in both for k in range(nz)]
    attn_mine, attn_theirs = list(attn_grads[:nz]), list(attn_grads[nz:])
    attn_theirs[0] = after(attn_theirs[0], fed_far)
    attn_got = [plan.core(v) for v in attn_theirs]

    dqkv_late = after(dqkv, attn_theirs[0])
    ig, vec_one = local_call(
        meta,
        functools.partial(input_grad_kernel, plan),
        "input_grad",
        [
            (own_x, True),
            (mg, True),
            (norm_params, True),
            (dqkv_late, True),
            (attn_full, True),
        ],
        [(tokens_low, False), (SDS((8, width), f32), True)],
        [buf_low, sem_x],
    )
    attn_got[0] = after(attn_got[0], ig, e_got)
    attn_keep, attn_send = add_first(meta, attn_mine, attn_got)
    attn_got = plan.second(attn_send)
    r_got = plan.along_x(after(r_send, attn_send))
    e_parts = add_parts(meta, e_keep, after(e_got, attn_send))
    e_z = [e_parts[0]] + [plan.along_z(e_parts[k], k) for k in range(1, nz)]
    size = -(-(8 * width + hidden) // (LANES * plan.ndev)) * LANES
    parts_in = (vec_one, vec_two, pair_sum, gh_near, gh_far)
    (vectors,) = local_call(
        meta,
        functools.partial(vectors_kernel, plan),
        "vectors",
        [(v, True) for v in parts_in],
        [(SDS((plan.ndev, 1, size), f32), False)],
        [pltpu.VMEM((plan.ndev, 1, size), f32), dma((1,))],
    )
    got = lax.all_to_all(vectors, AXES, 0, 0, tiled=True)
    local = jnp.sum(got, axis=0)

    attn_got = after(attn_got, local, r_got, *e_z)
    attn_keep, attn_send = add_parts(meta, attn_keep, attn_got)
    attn_got = plan.first(attn_send)
    pre_far = plan.along_y(after(pre_near, attn_send))
    r_got = after(r_got, attn_send)
    r_parts = add_parts(meta, r_keep, r_got)
    r_z = [r_parts[0]] + [plan.along_z(r_parts[k], k) for k in range(1, nz)]

    attn_parts = add_parts(meta, attn_keep, after(attn_got, *r_z))

    ff_in = [*e_z, *r_z]
    grad_expand, grad_reduce, ff_square = call(
        ff_total_kernel,
        "ff_total",
        (1,),
        [(v, *whole(v.shape)) for v in ff_in],
        [
            (SDS((rows, part), f32), *whole((rows, part))),
            (SDS((rows, part), f32), *whole((rows, part))),
            (SDS((1, 1), f32), *whole((1, 1))),
        ],
        [],
    )(meta, *ff_in)

    ig = after(ig, attn_parts[0])
    ig_pair = plan.along_y(ig)
    attn_z = [attn_parts[0]] + [plan.along_z(attn_parts[k], k) for k in range(1, nz)]
    pre_in, pre_far = pre_near, after(pre_far, attn_z[1])
    out, out_pair = call(
        out_kernel,
        "out_sum",
        (steps,),
        [
            (pre_in, *chunk(width)),
            (fed_far, *chunk(width)),
            (pre_far, *chunk(width)),
            (fed_send, *chunk(width)),
            (norm_params, *whole(norm_params.shape)),
        ],
        [(SDS((count, width), bf16), *chunk(width))] * 2,
        [],
    )(meta, pre_in, fed_far, pre_far, fed_send, norm_params)
    total_in = attn_z + [ff_square, after(local, out)]
    def everywhere(block, by_y):
        blocks = [block, by_y, plan.core(block), plan.core(by_y)]
        return call(
            place_kernel,
            "place",
            (1,),
            [(b, *whole((count, width))) for b in blocks],
            [(SDS((count * nmp, width), bf16), None, None)],
            [dma((4,))],
        )(meta, *blocks)[0]

    keep, send, payload = call(
        total_kernel,
        "total",
        (1,),
        [(v, *whole(v.shape)) for v in total_in],
        [
            (SDS((half, 2 * cols), f32), *whole((half, 2 * cols))),
            (SDS((half, 2 * cols), f32), *whole((half, 2 * cols))),
            (
                SDS((plan.ndev, 1, size + LANES), f32),
                *whole((plan.ndev, 1, size + LANES)),
            ),
        ],
        [],
    )(meta, *total_in)
    by_core = plan.core(send)
    ig_pair = after(ig_pair, keep)
    outputs = everywhere(out, out_pair)
    input_gradient = everywhere(ig, ig_pair)
    got = after(lax.all_to_all(payload, AXES, 0, 0, tiled=True), input_gradient, outputs)

    if not plan.direct:
        low, high = jnp.where(core_zero, keep, by_core), jnp.where(core_zero, by_core, keep)
        shard = jnp.concatenate([low, high], axis=0).reshape(rows, 4, quarter)
        keep = shard[:, :3].transpose(1, 0, 2)
        by_core = shard[:, 3].T

    matrix, vector = (LR_MATRIX, DECAY), (LR_VECTOR, 0.0)
    groups = [
        [triple_weight, triple_first, triple_second, keep],
        [outward_weight, outward_first, outward_second, by_core],
        [expand_weight, expand_first, expand_second, grad_expand],
        [reduce_weight.T, reduce_first.T, reduce_second.T, grad_reduce],
        [norm_params, norm_first, norm_second],
        [paired_bias, paired_first, paired_second],
        [hidden_bias, hidden_first, hidden_second],
    ]
    flat = [got] + [v for group in groups for v in group]
    new_shapes = [SDS(group[0].shape, f32) for group in groups for _ in range(3)]
    new_shapes.append(SDS((1, 1), f32))
    new = local_call(
        meta,
        functools.partial(adam_kernel, plan, (matrix,) * 4 + (vector,) * 3),
        "adam",
        [(flat[0], True)] + [(v, False) for v in flat[1:]],
        [(v, False) for v in new_shapes],
        [pltpu.VMEM(v.shape, f32) for v in (*flat[1:], *new_shapes)]
        + [dma((len(flat) - 1,)), dma((len(new_shapes),))],
        vmem=32,
    )
    new = list(new)
    gradient_norm = new.pop().reshape(())
    new[9:12] = [v.T for v in new[9:12]]
    return (outputs, input_gradient, gradient_norm, *new)


def turn(plan, value, z, axis):
    value = jnp.flip(value, axis)
    return jnp.roll(value, z + 1, axis)


def unturn(plan, value, z, axis):
    return jnp.roll(value, -z, axis)


def swap(value, flag, axis):
    return jnp.where(flag == 1, jnp.flip(value, axis), value)


def absolute_ff(plan, value, z, x):
    value = swap(turn(plan, value, z, 1), x, 0)
    return value.transpose(1, 0, 2, 3).reshape(plan.width, plan.part)


def relative_ff(plan, value, z, x):
    value = value.reshape(plan.nz, 2, plan.rows, plan.part).transpose(1, 0, 2, 3)
    value = unturn(plan, swap(value, x, 0), z, 1)
    return value[0], value[1]


def absolute_attn(plan, own, other, z, x, y, c):
    zero = jnp.where(c == 0, own, other)
    one = jnp.where(c == 0, other, own).transpose(1, 0, 2, 3, 4)
    value = jnp.stack([zero, one])
    value = turn(plan, swap(swap(value, y, 1), x, 2), z, 3)
    value = value.transpose(1, 3, 2, 0, 4, 5)
    return value.reshape(2, plan.width, 4 * plan.cols)


def relative_attn(plan, value, z, x, y, c):
    value = value.reshape(2, plan.nz, 2, 2, plan.half, 4 * plan.cols)
    value = value.transpose(3, 0, 2, 1, 4, 5)
    value = unturn(plan, swap(swap(value, y, 1), x, 2), z, 3)
    zero, one = value[0], value[1].transpose(1, 0, 2, 3, 4)
    return jnp.where(c == 0, zero, one), jnp.where(c == 0, one, zero)


def solution(mesh):
    tokens = P("dp", None)
    triple = P(None, "dp", "mp")
    tall = P("mp", "dp")
    wide = P("dp", "mp")
    pair = P(None, "mp")
    states = ((triple,) * 3, (tall,) * 3, (wide,) * 3, (tall,) * 3, (P(),) * 3, (pair,) * 3)
    states = sum(states, ()) + (P("mp"),) * 3
    return jax.shard_map(
        per_device,
        mesh=mesh,
        in_specs=(tokens,) * 3 + states,
        out_specs=(tokens, tokens, P()) + states,
        check_vma=False,
    )
```
